512 devices in a mesh: grp: 32 (over x, z), exp: 16 (over y, core).
Axes of the slice: x: 4, y: 8, z: 8, core: 2. Of those that a mesh axis runs over, the one named last changes fastest.
Arguments:
- step_inputs: bfloat16 [32, 4, 4, 2048], P('grp'), may hold values from -10 to 10
- parents: int32 [32, 4, 4], P('grp'), may hold values from 0 to 7
- routes: int32 [32, 4, 4, 6], P('grp'), may hold values from 0 to 63, all different within a row; in each aligned block of 16 rows (0 to 15, 16 to 31, ..., all dimensions but the last counted through in order) at most 3 rows name the same one
- w_qkv: bfloat16 [2048, 3, 2048], P(None, None, 'exp'), may hold values from -0.125 to 0.125
- w_out: bfloat16 [2048, 2048], P('exp'), may hold values from -0.125 to 0.125
- prompt_keys: bfloat16 [32, 1024, 2048], P('grp', None, 'exp'), may hold values from -128 to 128, as said below
- prompt_values: bfloat16 [32, 1024, 2048], P('grp', None, 'exp'), may hold values from -6 to 6
- prompt_parts: int32 [32], P('grp'), may hold values from 1 to 1024, as said below
- tail_keys: bfloat16 [32, 4, 60, 2048], P('grp', None, None, 'exp'), may hold values from -18 to 18
- tail_values: bfloat16 [32, 4, 60, 2048], P('grp', None, None, 'exp'), may hold values from -6 to 6
- w_router: bfloat16 [2048, 64], P('exp'), may hold values from -0.022097087 to 0.022097087
- norm_gain: float32 [2048], P('exp'), may hold values from 0.1 to 1.9
- w_gate_up: bfloat16 [64, 2048, 2816], P('grp', 'exp'), may hold values from -0.125 to 0.125
- w_down: bfloat16 [64, 2048, 1408], P('grp', 'exp'), may hold values from -0.15625 to 0.15625
Outputs:
- layer_out: bfloat16 [32, 4, 4, 2048], P('grp', None, None, 'exp')
The draws below stay inside these ranges and needn't reach their ends.
Inputs may be any that keep to these rules, and one draw needn't show every extreme that they name: `prompt_keys`: keys of order a few units. `prompt_parts`: each part holds 1 to 1024 valid positions; in every draw some part holds exactly 1024. `routes`: within the rows of one slot no expert is named more than 3 times, and in every draw some expert is named exactly 3 times by the rows of some slot.
All inputs are finite; a program needn't handle non-finite values.
Results may differ from the reference program's by a relative error of at most 0.013.
Values may be sent and summed in bfloat16 or wider, within the bound.
A program may use at most 64 MiB of HBM per device.

```python
import math
from functools import partial
import jax
import jax.numpy as jnp
import numpy as np
from jax import lax

D = 2048
HEADS = 16
HDIM = 128
EXPERTS = 64
FFE = 1408
TOPK = 6
BEAMS = 8
STEPS = 4
TAIL = 64
CAP = 1024
CAP_E = 3
SLOTS = 32
HALF = 4
PREV = 60


def draw_step_inputs(key, part):
    shape = (SLOTS, STEPS, HALF, D)
    ramp = jnp.arange(D, dtype=jnp.float32) / (D - 1.0)
    profile = jnp.exp(jnp.log(0.5) + ramp * (jnp.log(1.5) - jnp.log(0.5)))
    values = jnp.clip(jax.random.normal(key, shape, jnp.float32), -6.0, 6.0) * profile
    return values.astype(jnp.bfloat16)


def draw_prompt_keys(key, part):
    shape = (SLOTS, CAP, HEADS * HDIM)
    values = jnp.clip(jax.random.normal(key, shape, jnp.float32), -6.0, 6.0) * 3.0
    return values.astype(jnp.bfloat16)


def draw_prompt_parts(key, part):
    counts = jax.random.randint(key, (SLOTS,), 1, CAP + 1)
    filled = jax.random.randint(jax.random.fold_in(key, 3), (), 0, SLOTS)
    return jnp.where(jnp.arange(SLOTS) == filled, CAP, counts).astype(jnp.int32)


def draw_w_router(key, part):
    shape = (D, EXPERTS)
    factor = 1.0 / D ** 0.5
    values = jnp.clip(jax.random.normal(key, shape, jnp.float32) * 0.4, -1.0, 1.0) * factor
    return values.astype(jnp.bfloat16)


def with_ends(values, own_key, smallest, top_value):
    shape = values.shape
    index_at = [jax.random.randint(jax.random.fold_in(own_key, axis), (), 0, shape[axis]) for axis in range(len(shape))]
    values = values.at[tuple(index_at)].set(smallest)
    longest = shape.index(max(shape))
    index_at[longest] = (index_at[longest] + 1) % shape[longest]
    return values.at[tuple(index_at)].set(top_value)


def block_levels(own_key, dims, shards, least, high):
    def one(dim, shards_of):
        steps = jax.random.uniform(jax.random.fold_in(jax.random.fold_in(own_key, 6), dim), (shards_of,), jnp.float32, least / len(shards), high / len(shards))
        return jnp.repeat(jnp.exp(steps), dims[dim] // shards_of).reshape((-1,) + (1,) * (len(dims) - dim - 1))

    gain = one(*shards[0])
    for cut in shards[1:]:
        gain = gain * one(*cut)
    return gain


def routed_block(rng, own, number, rows, amount, top, reach, skew):
    order = jax.random.permutation(rng, amount)
    crowded, usual = portions_of(amount, rows * top, reach, skew, True), portions_of(amount, rows * top, reach, skew, False)
    places = jnp.arange(amount)

    def named(tallies, turn):
        used = int((tallies > 0).sum())
        fixed = max(1, used // 4)
        shifted = fixed + (places - fixed + turn * (used - fixed)) % max(1, amount - fixed)
        return jnp.zeros((amount,), jnp.int32).at[order[jnp.where(places < fixed, places, shifted)]].set(jnp.asarray(tallies, jnp.int32))

    tallies = jnp.where(number % 4 == 0, named(crowded, number // 4), named(usual, number - number // 4 - 1))
    mixed = jax.random.permutation(jax.random.fold_in(own, 3), amount)
    giver, taker = mixed[0:amount // 2 * 2:2], mixed[1:amount // 2 * 2:2]
    slack = jnp.minimum(tallies[giver] - 1, reach - tallies[taker]) // 2
    slack = jnp.where((giver == order[0]) | (taker == order[0]) | (tallies[taker] == 0), 0, jnp.maximum(slack, 0))
    shifted = jax.random.randint(jax.random.fold_in(own, 4), (amount // 2,), 0, 1 << 20) % (slack + 1)
    tallies = tallies.at[giver].add(-shifted).at[taker].add(shifted)
    members = jnp.searchsorted(jnp.cumsum(tallies), jnp.arange(rows * top), side="right").astype(jnp.int32)
    listing = members.reshape(top, rows).T
    listing = listing[jax.random.permutation(jax.random.fold_in(own, 1), rows)]
    turn = jax.random.randint(jax.random.fold_in(own, 2), (rows, 1), 0, top)
    return jnp.take_along_axis(listing, (jnp.arange(top)[None, :] + turn) % top, axis=1)


def portions_of(number_of, total, limit, skew, full):
    loads = [(1 << 20) // math.isqrt(grade ** skew) + 1 for grade in range(1, number_of + 1)]
    largest = limit if full else min(limit, max(-(-total // number_of), total * loads[0] // sum(loads)))
    least = 1 if total - largest >= number_of - 1 else 0
    given, surplus = [largest] + [least] * (number_of - 1), total - largest - least * (number_of - 1)
    while surplus > 0:
        candidates = [i for i in range(1, number_of) if given[i] < largest] or [i for i in range(1, number_of) if given[i] < limit]
        whole, remaining = sum([loads[i] for i in candidates]), surplus
        for i in candidates:
            more = min(limit - given[i], max(1, remaining * loads[i] // whole), surplus)
            given[i] = given[i] + more
            surplus = surplus - more
    return np.array(given)


def scatter_about(key, extent, scale, reach, cuts=(), kind=jnp.bfloat16):
    loudness = block_levels(key, extent, cuts, -0.22, 0.18) if cuts else 1.0
    values = jax.random.normal(key, extent, jnp.float32) * scale * loudness
    return jnp.minimum(jnp.maximum(values, -reach), reach).astype(kind)


def setup_inputs(seed: int = 0) -> dict:
    streams_of = jax.random.split(jax.random.key(seed), 15)
    step_inputs = draw_step_inputs(jax.random.fold_in(streams_of[14], 71), 0)
    parents = with_ends(jax.random.randint(streams_of[1], (SLOTS, STEPS, HALF), 0, BEAMS), jax.random.fold_in(streams_of[1], 1), 0, BEAMS - 1).astype(jnp.int32)
    routes_keys = jax.random.split(jax.random.fold_in(streams_of[2], 1), SLOTS * STEPS * HALF // (STEPS * HALF))
    routes_turns = jax.random.permutation(jax.random.fold_in(streams_of[2], 3), SLOTS * STEPS * HALF // (STEPS * HALF))
    routes = jax.vmap(lambda own, number: routed_block(jax.random.fold_in(streams_of[2], 2), own, number, STEPS * HALF, EXPERTS, TOPK, CAP_E, 2))(routes_keys, routes_turns).reshape((SLOTS, STEPS, HALF, TOPK))
    w_qkv = scatter_about(streams_of[3], (D, 3, HEADS * HDIM), D ** -0.5, 0.125, ((2, 16),))
    w_out = scatter_about(streams_of[4], (HEADS * HDIM, D), (HEADS * HDIM) ** -0.5, 0.125, ((0, 16),))
    prompt_keys = draw_prompt_keys(jax.random.fold_in(streams_of[14], 71), 0)
    prompt_values = scatter_about(streams_of[6], (SLOTS, CAP, HEADS * HDIM), 1.0, 6.0, ((0, 32), (2, 16)))
    prompt_parts = draw_prompt_parts(jax.random.fold_in(streams_of[14], 71), 0)
    tail_keys = scatter_about(streams_of[8], (SLOTS, HALF, PREV, HEADS * HDIM), 3.0, 18.0, ((0, 32), (3, 16)))
    tail_values = scatter_about(streams_of[9], (SLOTS, HALF, PREV, HEADS * HDIM), 1.0, 6.0, ((0, 32), (3, 16)))
    w_router = draw_w_router(jax.random.fold_in(streams_of[14], 71), 0)
    norm_gain = jnp.clip(1.0 + 0.18 * jax.random.normal(streams_of[11], (D,), jnp.float32), 0.1, 1.9)
    w_gate_up = scatter_about(streams_of[12], (EXPERTS, D, 2 * FFE), D ** -0.5, 0.125, ((0, 32), (1, 16)))
    w_down = scatter_about(streams_of[13], (EXPERTS, D, FFE), FFE ** -0.5, 0.15625, ((0, 32), (1, 16)))
    return dict(step_inputs=step_inputs, parents=parents, routes=routes, w_qkv=w_qkv, w_out=w_out, prompt_keys=prompt_keys, prompt_values=prompt_values, prompt_parts=prompt_parts, tail_keys=tail_keys, tail_values=tail_values, w_router=w_router, norm_gain=norm_gain, w_gate_up=w_gate_up, w_down=w_down)


NEGATIVE = -1e+30
EPSILON = 1e-06

def pair_steps(array):
    shape = array.shape
    paired = array.reshape((shape[0] // 2, 2) + shape[1:])
    paired = jnp.swapaxes(paired, 1, 2)
    return paired.reshape((shape[0] // 2, shape[1], 2 * shape[2]) + shape[3:])

def split_steps(array):
    shape = array.shape
    halves = array.reshape((shape[0], shape[1], 2, shape[2] // 2) + shape[3:])
    halves = jnp.swapaxes(halves, 1, 2)
    return halves.reshape((2 * shape[0], shape[1], shape[2] // 2) + shape[3:])

def attend_request(request_args, w_qkv):
    inputs_req, parents_req, keys_req, values_req, parts_req, tail_k_req, tail_v_req = request_args
    width = HEADS * HDIM
    packed = jnp.dot(inputs_req.reshape(STEPS * BEAMS, D), w_qkv.reshape(D, 3 * width), preferred_element_type=jnp.float32)
    packed = lax.optimization_barrier(packed.astype(jnp.bfloat16)).astype(jnp.float32)
    packed = packed.reshape(STEPS, BEAMS, 3, HEADS, HDIM)
    query_all = packed[:, :, 0]
    key_new = packed[:, :, 1]
    value_new = packed[:, :, 2]
    score_scale = HDIM ** (-0.5)
    prompt_keys_f = keys_req.reshape(2 * CAP, HEADS, HDIM).astype(jnp.float32)
    prompt_vals_f = values_req.reshape(2 * CAP, HEADS, HDIM).astype(jnp.float32)
    positions = jnp.arange(CAP, dtype=jnp.int32)
    live_pos = (positions[None, :] < parts_req[:, None]).reshape(2 * CAP)
    prompt_scores = jnp.einsum('sbhd,nhd->sbhn', query_all, prompt_keys_f, precision=lax.Precision.HIGHEST) * score_scale
    prompt_scores = jnp.where(live_pos, prompt_scores, NEGATIVE)
    tail_keys_f = jnp.zeros((BEAMS, TAIL, HEADS, HDIM), jnp.float32).at[:, :PREV].set(tail_k_req.reshape(BEAMS, PREV, HEADS, HDIM).astype(jnp.float32))
    tail_vals_f = jnp.zeros((BEAMS, TAIL, HEADS, HDIM), jnp.float32).at[:, :PREV].set(tail_v_req.reshape(BEAMS, PREV, HEADS, HDIM).astype(jnp.float32))
    tail_pos = jnp.arange(TAIL, dtype=jnp.int32)
    outputs = []
    for step_index in range(STEPS):
        tail_keys_f = tail_keys_f[parents_req[step_index]].at[:, PREV + step_index].set(key_new[step_index])
        tail_vals_f = tail_vals_f[parents_req[step_index]].at[:, PREV + step_index].set(value_new[step_index])
        tail_scores = jnp.einsum('bhd,bnhd->bhn', query_all[step_index], tail_keys_f, precision=lax.Precision.HIGHEST) * score_scale
        tail_scores = jnp.where(tail_pos <= PREV + step_index, tail_scores, NEGATIVE)
        joined = jnp.concatenate([prompt_scores[step_index], tail_scores], axis=2)
        best_top = lax.optimization_barrier(jnp.max(joined, axis=2, keepdims=True))
        weights = jnp.exp(joined - best_top)
        part_total = lax.optimization_barrier(jnp.sum(weights, axis=2))
        part_mix = jnp.einsum('bhn,nhd->bhd', weights[:, :, :2 * CAP], prompt_vals_f, precision=lax.Precision.HIGHEST)
        part_mix = part_mix + jnp.einsum('bhn,bnhd->bhd', weights[:, :, 2 * CAP:], tail_vals_f, precision=lax.Precision.HIGHEST)
        outputs.append((part_mix / part_total[:, :, None]).reshape(BEAMS, width))
    return jnp.stack(outputs).astype(jnp.bfloat16)

def expert_rows(expert_args):
    rows_in, gate_up, down = expert_args
    flat = rows_in.reshape(SLOTS * CAP_E, D)
    mixed_units = jnp.dot(flat, gate_up, preferred_element_type=jnp.float32)
    hidden_units = (jax.nn.silu(mixed_units[:, :FFE]) * mixed_units[:, FFE:]).astype(jnp.bfloat16)
    result = jnp.dot(hidden_units, down.T, preferred_element_type=jnp.float32).astype(jnp.bfloat16)
    return result.reshape(SLOTS, CAP_E, D)

def reference(step_inputs, parents, routes, w_qkv, w_out, prompt_keys, prompt_values, prompt_parts, tail_keys, tail_values, w_router, norm_gain, w_gate_up, w_down):
    requests = SLOTS // 2
    width = HEADS * HDIM
    request_args = (pair_steps(step_inputs), pair_steps(parents), prompt_keys.reshape(requests, 2, CAP, width), prompt_values.reshape(requests, 2, CAP, width), prompt_parts.reshape(requests, 2), tail_keys.reshape(requests, BEAMS, PREV, width), tail_values.reshape(requests, BEAMS, PREV, width))
    attended = lax.map(partial(attend_request, w_qkv=w_qkv), request_args)
    row_count = SLOTS * STEPS * HALF
    attention = split_steps(attended).reshape(row_count, width)
    residual_rows = step_inputs.reshape(row_count, D).astype(jnp.float32) + jnp.dot(attention, w_out, preferred_element_type=jnp.float32)
    mean_square = lax.optimization_barrier(jnp.mean(residual_rows * residual_rows, axis=1, keepdims=True))
    normed = (residual_rows * lax.rsqrt(mean_square + EPSILON) * norm_gain).astype(jnp.bfloat16)
    logits = jnp.dot(normed, w_router, preferred_element_type=jnp.float32)
    probs = jax.nn.softmax(logits, axis=1)
    chosen = routes.reshape(row_count, TOPK)
    picked = jnp.take_along_axis(probs, chosen, axis=1)
    route_share = picked / lax.optimization_barrier(jnp.sum(picked, axis=1, keepdims=True))
    entries = routes.reshape(SLOTS, STEPS * HALF * TOPK)
    route_match = (entries[:, :, None] == jnp.arange(EXPERTS, dtype=jnp.int32)[None, None, :]).astype(jnp.int32)
    earlier = (jnp.cumsum(route_match, axis=1) - route_match).astype(jnp.int32)
    slot_rank = lax.optimization_barrier(jnp.sum(route_match * earlier, axis=2)).astype(jnp.int32)
    slot_ids = jnp.broadcast_to(jnp.arange(SLOTS, dtype=jnp.int32)[:, None], entries.shape)
    repeated = jnp.repeat(normed.reshape(SLOTS, STEPS * HALF, D), TOPK, axis=1)
    dispatch = jnp.zeros((EXPERTS, SLOTS, CAP_E, D), jnp.bfloat16).at[entries, slot_ids, slot_rank].set(repeated)
    expert_out = lax.map(expert_rows, (dispatch, w_gate_up, w_down))
    fetched = expert_out[entries, slot_ids, slot_rank].astype(jnp.float32).reshape(row_count, TOPK, D)
    expert_mix = lax.optimization_barrier(jnp.sum(route_share[:, :, None] * fetched, axis=1))
    return (residual_rows + expert_mix).astype(jnp.bfloat16).reshape(SLOTS, STEPS, HALF, D)
```

```python
import functools

import jax
import jax.numpy as jnp
from jax import lax
from jax.experimental import pallas as pl
from jax.experimental.pallas import tpu as pltpu
from jax.sharding import PartitionSpec as P

HDIM = 128
TOPK = 6
STEPS = 4
HALF = 4
ROWS = STEPS * HALF
CAP_E = 3
PREV = 60
TAILP = 64
SEND = 8
BLOCK = 12
PADB = 16

NEGATIVE = -1e30
EPSILON = 1e-06
F32 = jnp.float32
BF16 = jnp.bfloat16


def iota(shape, axis):
    return lax.broadcasted_iota(jnp.int32, shape, axis)


def dot(a, b, precision=None):
    return jnp.dot(a, b, preferred_element_type=F32, precision=precision)


def dot_t(a, b, precision=None):
    return lax.dot_general(
        a, b, (((1,), (1,)), ((), ())), preferred_element_type=F32, precision=precision
    )


def one_hot(cond):
    return jnp.where(cond, 1.0, 0.0).astype(BF16)


def split_high(value):
    high = value.astype(BF16)
    return high, (value - high.astype(F32)).astype(BF16)


def kernel(
    groups,
    columns,
    topk,
    x_ref,
    par_ref,
    routes_ref,
    parts_ref,
    gain_in,
    wr_in,
    wqkv_hbm,
    wout_hbm,
    pk_hbm,
    pv_hbm,
    tk_ref,
    tv_ref,
    wgu_hbm,
    wd_hbm,
    out_ref,
    xs,
    rts,
    gain,
    wr,
    wqkv,
    wout,
    kall,
    vall,
    wgu,
    wd,
    qkv,
    part_send,
    part_recv,
    proj_send,
    proj_recv,
    stat_send,
    stat_recv,
    disp_send,
    disp_recv,
    sq_send,
    sq_recv,
    gu_send,
    gu_recv,
    gsum,
    hid,
    ret_send,
    ret_recv,
    mix_send,
    mix_recv,
    local_sem,
    send_sem,
    recv_sem,
):
    chips = columns // 2
    ffe = wd.shape[1]
    cap = pk_hbm.shape[1]
    experts = wr.shape[1]
    depth = x_ref.shape[3]
    g = lax.axis_index("grp")
    e = lax.axis_index("exp")
    y = e // 2
    c = e % 2
    half = g % 2
    partner = g + 1 - 2 * half
    sibling = e + 1 - 2 * c
    own_rows = pl.ds(pl.multiple_of(c * HDIM, HDIM), HDIM)

    def local(src, dst, index):
        copy = pltpu.make_async_copy(src, dst, local_sem.at[index])
        copy.start()
        return copy

    def remote(src, dst, index, **where):
        return pltpu.make_async_remote_copy(
            src_ref=src,
            dst_ref=dst,
            send_sem=send_sem.at[index],
            recv_sem=recv_sem.at[index],
            device_id=where,
            device_id_type=pl.DeviceIdType.MESH,
        )

    def wait_bytes(ref, sem):
        pltpu.make_async_copy(ref, ref, sem).wait()

    load_qkv = local(wqkv_hbm, wqkv, 0)
    load_keys = local(pk_hbm.at[0], kall.at[pl.ds(0, cap)], 1)
    load_values = local(pv_hbm.at[0], vall.at[pl.ds(0, cap)], 2)
    load_out = local(wout_hbm, wout, 3)
    load_gu = local(wgu_hbm.at[c], wgu.at[own_rows], 4)
    load_down = local(wd_hbm.at[c], wd.at[own_rows], 5)

    barrier = pltpu.get_barrier_semaphore()

    def greet_group(k, carry):
        other = lax.rem(g + k, groups)
        pl.semaphore_signal(
            barrier, inc=1, device_id={"grp": other}, device_id_type=pl.DeviceIdType.MESH
        )
        return carry

    def greet_column(k, carry):
        other = lax.rem(e + k, columns)
        pl.semaphore_signal(
            barrier, inc=1, device_id={"exp": other}, device_id_type=pl.DeviceIdType.MESH
        )
        return carry

    lax.fori_loop(1, groups, greet_group, 0)
    lax.fori_loop(1, columns, greet_column, 0)

    for s in range(STEPS):
        xs[HALF * s : HALF * (s + 1), :] = x_ref[0, s].astype(F32)
        rts[HALF * s : HALF * (s + 1), :topk] = routes_ref[0, s]
    x16 = xs[...].astype(BF16)
    row_sub = iota((ROWS, HDIM), 0)
    row_lane = iota((ROWS, HDIM), 1)
    parent_hot = jnp.zeros((ROWS, HDIM), F32)
    for s in range(STEPS):
        for b in range(HALF):
            parent_hot = jnp.where(
                (row_sub == HALF * s + b) & (row_lane == par_ref[0, s, b]), 1.0, parent_hot
            )
    load_qkv.wait()
    qkv[0, :, 0 : 3 * HDIM] = dot(x16, wqkv[...]).astype(BF16)
    qkv[0, :, 3 * HDIM : 4 * HDIM] = parent_hot.astype(BF16)

    pl.semaphore_wait(barrier, groups + columns - 2)

    qkv_copy = remote(qkv.at[0], qkv.at[1], 0, grp=partner)
    qkv_copy.start()
    gain[pl.ds(c, 1)] = gain_in[...].reshape(1, 1, HDIM)
    wr[own_rows, :] = wr_in[...]
    swap_gain = remote(gain_in, gain.at[c], 1, exp=sibling)
    swap_router = remote(wr_in, wr.at[own_rows], 2, exp=sibling)
    swap_gu = remote(wgu_hbm.at[1 - c], wgu.at[own_rows], 3, exp=sibling)
    swap_down = remote(wd_hbm.at[1 - c], wd.at[own_rows], 4, exp=sibling)
    swap_gain.start()
    swap_router.start()
    swap_gu.start()
    swap_down.start()

    tail_at = cap
    new_at = cap + HALF * TAILP
    total = new_at + 2 * ROWS
    kall[tail_at:new_at, :] = jnp.zeros((HALF * TAILP, HDIM), BF16)
    vall[tail_at:new_at, :] = jnp.zeros((HALF * TAILP, HDIM), BF16)
    for b in range(HALF):
        at = tail_at + TAILP * b
        kall[at : at + PREV, :] = tk_ref[0, b]
        vall[at : at + PREV, :] = tv_ref[0, b]

    width = groups * SEND
    routes = rts[...]
    hit = jnp.zeros((ROWS, experts), jnp.bool_)
    expert_lane = iota((ROWS, experts), 1)
    for k in range(topk):
        hit = hit | (routes[:, k : k + 1] == expert_lane)
    hits = one_hot(hit)
    rank = dot(one_hot(iota((ROWS, ROWS), 1) < iota((ROWS, ROWS), 0)), hits)
    spread_row = iota((experts, width), 0)
    spread_lane = iota((experts, width), 1)
    spread = one_hot(spread_row == 2 * (spread_lane // SEND) + c)
    hit_wide = dot(hits, spread)
    rank_wide = dot(rank.astype(BF16), spread)
    slot_lane = (iota((ROWS, width), 1) % SEND).astype(F32)
    place = jnp.where((rank_wide == slot_lane) & (hit_wide > 0.5), 1.0, 0.0)

    load_keys.wait()
    load_values.wait()
    qkv_copy.wait_recv()
    for h in range(2):
        at = new_at + ROWS * h
        kall[at : at + ROWS, :] = qkv[h, :, HDIM : 2 * HDIM]
        vall[at : at + ROWS, :] = qkv[h, :, 2 * HDIM : 3 * HDIM]
    query = jnp.concatenate([qkv[0, :, 0:HDIM], qkv[1, :, 0:HDIM]], axis=0)
    parents = jnp.concatenate(
        [qkv[0, :, 3 * HDIM : 4 * HDIM], qkv[1, :, 3 * HDIM : 4 * HDIM]], axis=0
    )
    tokens = 2 * ROWS
    beam_row = iota((HDIM, tokens), 0)
    token_lane = iota((HDIM, tokens), 1)
    beam_of = HALF * ((token_lane // ROWS + half) % 2) + token_lane % HALF
    before = dot(parents, one_hot(beam_row == beam_of))
    step_row = (iota((tokens, tokens), 0) % ROWS) // HALF
    step_lane = (iota((tokens, tokens), 1) % ROWS) // HALF
    same = jnp.where(iota((tokens, tokens), 0) == iota((tokens, tokens), 1), 1.0, 0.0)
    back = jnp.where(step_lane + 1 == step_row, before, 0.0)
    back_bf = back.astype(BF16)
    near = (same + back).astype(BF16)
    back_two = dot(back_bf, back_bf)
    path = dot(near, (same + back_two).astype(BF16)).astype(BF16)
    first_row = iota((tokens, HDIM), 0) % ROWS
    first = jnp.where(first_row < HALF, parents.astype(F32), 0.0).astype(BF16)
    origin = dot(path, first).astype(BF16)
    tails = HALF * TAILP
    tail_row = iota((HDIM, tails), 0)
    tail_lane = iota((HDIM, tails), 1)
    tail_on = dot(
        origin,
        one_hot((tail_row == HALF * half + tail_lane // TAILP) & (tail_lane % TAILP < PREV)),
    )
    new_on = jnp.where(iota((tokens, tokens), 0) < ROWS, path.astype(F32), 0.0)

    score_scale = HDIM ** (-0.5)
    scores = dot_t(query, kall[...]) * score_scale
    prompt_live = iota((tokens, cap), 1) < parts_ref[0]
    prompt_s = jnp.where(prompt_live, scores[:, 0:cap], NEGATIVE)
    tail_s = jnp.where(tail_on > 0.5, scores[:, tail_at:new_at], NEGATIVE)
    new_s = jnp.where(new_on > 0.5, scores[:, new_at:total], NEGATIVE)
    top = jnp.maximum(
        jnp.maximum(
            jnp.max(prompt_s, axis=1, keepdims=True), jnp.max(tail_s, axis=1, keepdims=True)
        ),
        jnp.max(new_s, axis=1, keepdims=True),
    )
    prompt_w = jnp.exp(prompt_s - top)
    tail_w = jnp.exp(tail_s - top)
    new_w = jnp.exp(new_s - top)
    weight_sum = (
        jnp.sum(prompt_w, axis=1, keepdims=True)
        + jnp.sum(tail_w, axis=1, keepdims=True)
        + jnp.sum(new_w, axis=1, keepdims=True)
    )

    def weighted(weights, values):
        high, low = split_high(weights)
        both = dot(jnp.concatenate([high, low], axis=0), values)
        return both[0:tokens] + both[tokens : 2 * tokens]

    mix = (
        weighted(prompt_w, vall[0:cap, :])
        + weighted(tail_w, vall[tail_at:new_at, :])
        + weighted(new_w, vall[new_at:total, :])
    )
    part_send[:, 0:HDIM] = mix[ROWS:tokens]
    lane = iota((ROWS, HDIM), 1)
    part_send[:, HDIM : 2 * HDIM] = jnp.where(
        lane < HDIM // 2, top[ROWS:tokens], weight_sum[ROWS:tokens]
    )
    part_copy = remote(part_send, part_recv, 5, grp=partner)
    part_copy.start()
    load_out.wait()
    part_copy.wait_recv()
    far_mix = part_recv[:, 0:HDIM]
    far_top = part_recv[:, HDIM : HDIM + 1]
    far_sum = part_recv[:, HDIM + HDIM // 2 : HDIM + HDIM // 2 + 1]
    near_top = top[0:ROWS]
    best = jnp.maximum(near_top, far_top)
    near_factor = jnp.exp(near_top - best)
    far_factor = jnp.exp(far_top - best)
    attention = (
        (mix[0:ROWS] * near_factor + far_mix * far_factor)
        / (weight_sum[0:ROWS] * near_factor + far_sum * far_factor)
    ).astype(BF16)

    chip = 2 * HDIM
    proj = dot(attention, wout[...])
    for d in range(chips):
        proj_send[d] = proj[:, chip * d : chip * (d + 1)].astype(BF16)

    def send_proj(k, carry):
        other = lax.rem(e + k, columns)
        remote(proj_send.at[other // 2], proj_recv.at[e], 6, exp=other).start()
        return carry

    lax.fori_loop(1, columns, send_proj, 0)
    proj_recv[pl.ds(e, 1)] = proj_send[pl.ds(y, 1)]
    residual = xs[:, pl.ds(pl.multiple_of(y * chip, chip), chip)]
    wait_bytes(proj_recv.at[pl.ds(0, columns - 1)], recv_sem.at[6])
    residual = residual + jnp.sum(proj_recv[...].astype(F32), axis=0)

    rows_bf = residual.astype(BF16)
    outgoing = lax.dot_general(
        place.astype(BF16), rows_bf, (((0,), (0,)), ((), ())), preferred_element_type=F32
    ).astype(BF16)
    disp_send[...] = outgoing.reshape(groups, SEND, chip)

    def send_disp(k, carry):
        other = lax.rem(g + k, groups)
        remote(disp_send.at[other], disp_recv.at[g], 7, grp=other).start()
        return carry

    lax.fori_loop(1, groups, send_disp, 0)
    disp_recv[pl.ds(g, 1)] = disp_send[pl.ds(g, 1)]

    swap_gain.wait_recv()
    swap_router.wait_recv()
    gains = jnp.concatenate([gain[0], gain[1]], axis=1)
    logit_part = dot((residual * gains).astype(BF16), wr[...])
    stat_send[:, 0:experts] = logit_part
    stat_send[:, experts:HDIM] = jnp.broadcast_to(
        jnp.sum(residual * residual, axis=1, keepdims=True), (ROWS, HDIM - experts)
    )

    def send_stat(k, carry):
        other = lax.rem(y + k, chips)
        remote(stat_send, stat_recv.at[y], 8, exp=2 * other + c).start()
        return carry

    lax.fori_loop(1, chips, send_stat, 0)
    stat_recv[pl.ds(y, 1)] = stat_send[...].reshape(1, ROWS, stat_send.shape[1])

    wait_bytes(disp_recv.at[pl.ds(0, groups - 1)], recv_sem.at[7])
    arrived = disp_recv[...].reshape(groups * SEND, chip)
    packed = chips * PADB
    pick_row = iota((packed, groups * SEND), 0)
    pick_lane = iota((packed, groups * SEND), 1)
    per = BLOCK // CAP_E
    own_dest = pick_row // PADB

    def picks(shift):
        index = pick_row % PADB - shift
        safe = jnp.maximum(index, 0)
        source = (own_dest * per + safe // CAP_E) * SEND + safe % CAP_E
        return one_hot((index >= 0) & (index < BLOCK) & (pick_lane == source))

    gate_rows = dot(picks(0), arrived)
    up_rows = dot(picks(PADB - BLOCK), arrived)
    squares = dot_t(
        jnp.ones((8, chip), F32), gate_rows * gate_rows, precision=lax.Precision.HIGHEST
    )
    sq_send[...] = squares

    def send_sq(k, carry):
        other = lax.rem(y + k, chips)
        remote(sq_send, sq_recv.at[y], 9, exp=2 * other + c).start()
        return carry

    lax.fori_loop(1, chips, send_sq, 0)
    sq_recv[pl.ds(y, 1)] = squares.reshape(1, 8, packed)
    gate_in = (gate_rows * gains).astype(BF16)
    up_in = (up_rows * gains).astype(BF16)
    load_gu.wait()
    swap_gu.wait_recv()
    for t in range(ffe // HDIM):
        lanes = slice(HDIM * t, HDIM * (t + 1))
        gate = dot(gate_in, wgu[:, lanes]).reshape(chips, 2, 8, HDIM)
        up = dot(up_in, wgu[:, ffe + HDIM * t : ffe + HDIM * (t + 1)]).reshape(chips, 2, 8, HDIM)
        gu_send[:, 0:8, lanes] = gate[:, 0].astype(BF16)
        gu_send[:, 8:16, lanes] = (gate[:, 1] + up[:, 0]).astype(BF16)
        gu_send[:, 16:24, lanes] = up[:, 1].astype(BF16)

    def send_gu(k, carry):
        other = lax.rem(y + k, chips)
        remote(gu_send.at[other], gu_recv.at[y], 10, exp=2 * other + c).start()
        return carry

    lax.fori_loop(1, chips, send_gu, 0)
    gu_recv[pl.ds(y, 1)] = gu_send[pl.ds(y, 1)]

    wait_bytes(stat_recv.at[pl.ds(0, chips - 1)], recv_sem.at[8])
    stats = jnp.sum(stat_recv[...], axis=0)
    mean_square = stats[:, experts : experts + 1] / depth
    logits = stats[:, 0:experts] * lax.rsqrt(mean_square + EPSILON)
    picked_top = jnp.max(jnp.where(hit, logits, NEGATIVE), axis=1, keepdims=True)
    picked = jnp.where(hit, jnp.exp(jnp.minimum(logits - picked_top, 0.0)), 0.0)
    share = picked / jnp.sum(picked, axis=1, keepdims=True)
    share_high, share_low = split_high(share)
    shares = jnp.concatenate([share_high, share_low], axis=0)
    share_wide = dot(shares, spread)
    combine = jnp.concatenate(
        [
            (share_wide[0:ROWS] * place).astype(BF16),
            (share_wide[ROWS : 2 * ROWS] * place).astype(BF16),
        ],
        axis=0,
    )
    wait_bytes(sq_recv.at[pl.ds(0, chips - 1)], recv_sem.at[9])
    square_sums = jnp.sum(sq_recv[...], axis=0)[0:1, :]
    scale_row = iota((2 * BLOCK, packed), 0) % BLOCK
    scale_lane = iota((2 * BLOCK, packed), 1)
    own_square = jnp.sum(
        jnp.where(scale_lane == y * PADB + scale_row, square_sums, 0.0), axis=1, keepdims=True
    )
    scale = lax.rsqrt(own_square / depth + EPSILON)

    wait_bytes(gu_recv.at[pl.ds(0, chips - 1)], recv_sem.at[10])
    gsum[0 : 2 * BLOCK, :] = jnp.sum(gu_recv[...].astype(F32), axis=0) * scale
    gsum[2 * BLOCK : 2 * PADB, :] = jnp.zeros((2 * PADB - 2 * BLOCK, ffe), F32)
    gates = gsum[0:PADB, :]
    ups = gsum[BLOCK : BLOCK + PADB, :]
    hid[pl.ds(y, 1)] = (
        (gates / (1.0 + jnp.exp(-gates)) * ups).astype(BF16).reshape(1, PADB, ffe)
    )

    def send_hid(k, carry):
        other = lax.rem(y + k, chips)
        remote(hid.at[y], hid.at[y], 11, exp=2 * other + c).start()
        return carry

    lax.fori_loop(1, chips, send_hid, 0)
    load_down.wait()
    swap_down.wait_recv()
    back_row = iota((groups * SEND, packed), 0)
    back_lane = iota((groups * SEND, packed), 1)
    back_slot = back_row // SEND
    back_rank = back_row % SEND
    back_source = (back_slot // per) * PADB + (back_slot % per) * CAP_E + back_rank
    back_pick = one_hot((back_rank < CAP_E) & (back_lane == back_source))
    wait_bytes(hid.at[pl.ds(0, chips - 1)], recv_sem.at[11])
    result = dot_t(hid[...].reshape(packed, ffe), wd[...]).astype(BF16)
    ret_send[...] = dot(back_pick, result).astype(BF16).reshape(groups, SEND, chip)

    def send_ret(k, carry):
        other = lax.rem(g + k, groups)
        remote(ret_send.at[other], ret_recv.at[g], 12, grp=other).start()
        return carry

    lax.fori_loop(1, groups, send_ret, 0)
    ret_recv[pl.ds(g, 1)] = ret_send[pl.ds(g, 1)]
    wait_bytes(ret_recv.at[pl.ds(0, groups - 1)], recv_sem.at[12])
    both = dot(combine, ret_recv[...].reshape(groups * SEND, chip))
    expert_mix = both[0:ROWS] + both[ROWS : 2 * ROWS]
    mix_send[...] = jnp.where(c == 0, expert_mix[:, HDIM:chip], expert_mix[:, 0:HDIM])
    mix_copy = remote(mix_send, mix_recv, 13, exp=sibling)
    mix_copy.start()
    own = jnp.where(
        c == 0,
        residual[:, 0:HDIM] + expert_mix[:, 0:HDIM],
        residual[:, HDIM:chip] + expert_mix[:, HDIM:chip],
    )
    mix_copy.wait_recv()
    out_ref[...] = own + mix_recv[...]

    qkv_copy.wait_send()
    swap_gain.wait_send()
    swap_router.wait_send()
    swap_gu.wait_send()
    swap_down.wait_send()
    part_copy.wait_send()
    mix_copy.wait_send()
    wait_bytes(proj_recv.at[pl.ds(0, columns - 1)], send_sem.at[6])
    wait_bytes(disp_recv.at[pl.ds(0, groups - 1)], send_sem.at[7])
    wait_bytes(stat_recv.at[pl.ds(0, chips - 1)], send_sem.at[8])
    wait_bytes(sq_recv.at[pl.ds(0, chips - 1)], send_sem.at[9])
    wait_bytes(gu_recv.at[pl.ds(0, chips - 1)], send_sem.at[10])
    wait_bytes(hid.at[pl.ds(0, chips - 1)], send_sem.at[11])
    wait_bytes(ret_recv.at[pl.ds(0, groups - 1)], send_sem.at[12])


def on_device(
    step_inputs,
    parents,
    routes,
    w_qkv,
    w_out,
    prompt_keys,
    prompt_values,
    prompt_parts,
    tail_keys,
    tail_values,
    w_router,
    norm_gain,
    w_gate_up,
    w_down,
):
    groups = lax.axis_size("grp")
    columns = lax.axis_size("exp")
    chips = columns // 2
    depth = step_inputs.shape[3]
    cap = prompt_keys.shape[1]
    ffe = w_down.shape[2]
    experts = w_router.shape[1]
    topk = routes.shape[3]
    chip = 2 * HDIM
    keys = cap + HALF * TAILP + 2 * ROWS
    vmem = pl.BlockSpec(memory_space=pltpu.VMEM)
    smem = pl.BlockSpec(memory_space=pltpu.SMEM)
    anywhere = pl.BlockSpec(memory_space=pl.ANY)
    out = pl.pallas_call(
        functools.partial(kernel, groups, columns, topk),
        out_shape=jax.ShapeDtypeStruct((ROWS, HDIM), F32),
        in_specs=[
            vmem,
            smem,
            vmem,
            smem,
            vmem,
            vmem,
            anywhere,
            anywhere,
            anywhere,
            anywhere,
            vmem,
            vmem,
            anywhere,
            anywhere,
        ],
        out_specs=vmem,
        scratch_shapes=[
            pltpu.VMEM((ROWS, depth), F32),
            pltpu.VMEM((ROWS, HDIM), jnp.int32),
            pltpu.VMEM((2, 1, HDIM), F32),
            pltpu.VMEM((chip, experts), BF16),
            pltpu.VMEM((depth, 3 * HDIM), BF16),
            pltpu.VMEM((HDIM, depth), BF16),
            pltpu.VMEM((keys, HDIM), BF16),
            pltpu.VMEM((keys, HDIM), BF16),
            pltpu.VMEM((chip, 2 * ffe), BF16),
            pltpu.VMEM((chip, ffe), BF16),
            pltpu.VMEM((2, ROWS, 4 * HDIM), BF16),
            pltpu.VMEM((ROWS, chip), F32),
            pltpu.VMEM((ROWS, chip), F32),
            pltpu.VMEM((chips, ROWS, chip), BF16),
            pltpu.VMEM((columns, ROWS, chip), BF16),
            pltpu.VMEM((ROWS, HDIM), F32),
            pltpu.VMEM((chips, ROWS, HDIM), F32),
            pltpu.VMEM((groups, SEND, chip), BF16),
            pltpu.VMEM((groups, SEND, chip), BF16),
            pltpu.VMEM((8, chips * PADB), F32),
            pltpu.VMEM((chips, 8, chips * PADB), F32),
            pltpu.VMEM((chips, 2 * BLOCK, ffe), BF16),
            pltpu.VMEM((chips, 2 * BLOCK, ffe), BF16),
            pltpu.VMEM((2 * PADB, ffe), F32),
            pltpu.VMEM((chips, PADB, ffe), BF16),
            pltpu.VMEM((groups, SEND, chip), BF16),
            pltpu.VMEM((groups, SEND, chip), BF16),
            pltpu.VMEM((ROWS, HDIM), F32),
            pltpu.VMEM((ROWS, HDIM), F32),
            pltpu.SemaphoreType.DMA((6,)),
            pltpu.SemaphoreType.DMA((14,)),
            pltpu.SemaphoreType.DMA((14,)),
        ],
        compiler_params=pltpu.CompilerParams(
            collective_id=0, has_side_effects=True, vmem_limit_bytes=48 * 1024 * 1024
        ),
        name="layer",
    )(
        step_inputs,
        parents,
        routes,
        prompt_parts,
        norm_gain.reshape(1, HDIM),
        w_router,
        w_qkv.reshape(depth, 3 * HDIM),
        w_out,
        prompt_keys,
        prompt_values,
        tail_keys,
        tail_values,
        w_gate_up,
        w_down,
    )
    return out.astype(BF16).reshape(1, STEPS, HALF, HDIM)


def solution(mesh):
    placed = (
        P("grp", None, None, None),
        P("grp", None, None),
        P("grp", None, None, None),
        P(None, None, "exp"),
        P("exp", None),
        P("grp", None, "exp"),
        P("grp", None, "exp"),
        P("grp"),
        P("grp", None, None, "exp"),
        P("grp", None, None, "exp"),
        P("exp", None),
        P("exp"),
        P("grp", "exp", None),
        P("grp", "exp", None),
    )
    return jax.shard_map(
        on_device,
        mesh=mesh,
        in_specs=placed,
        out_specs=P("grp", None, None, "exp"),
        check_vma=False,
    )
```

```python
import functools

import jax
import jax.numpy as jnp
from jax import lax
from jax.experimental import pallas as pl
from jax.experimental.pallas import tpu as pltpu
from jax.sharding import PartitionSpec as P

HDIM = 128
TOPK = 6
STEPS = 4
HALF = 4
ROWS = STEPS * HALF
CAP_E = 3
PREV = 60
SEND = 8
BLOCK = 12
PADB = 16

NEGATIVE = -1e30
EPSILON = 1e-06
F32 = jnp.float32
BF16 = jnp.bfloat16


def iota(shape, axis):
    return lax.broadcasted_iota(jnp.int32, shape, axis)


def dot(a, b, precision=None):
    return jnp.dot(a, b, preferred_element_type=F32, precision=precision)


def dot_t(a, b, precision=None):
    return lax.dot_general(
        a, b, (((1,), (1,)), ((), ())), preferred_element_type=F32, precision=precision
    )


def one_hot(cond):
    return jnp.where(cond, 1.0, 0.0).astype(BF16)


def split_high(value):
    high = value.astype(BF16)
    return high, (value - high.astype(F32)).astype(BF16)


def kernel(
    groups,
    columns,
    topk,
    x_hbm,
    par_hbm,
    routes_hbm,
    parts_hbm,
    gain_hbm,
    wr_hbm,
    wqkv_hbm,
    wout_hbm,
    pk_hbm,
    pv_hbm,
    tk_hbm,
    tv_hbm,
    wgu_hbm,
    wd_hbm,
    out_ref,
    x_ref,
    par_ref,
    routes_ref,
    parts_ref,
    tk_ref,
    tv_ref,
    xs,
    rts,
    gain,
    wr,
    wqkv,
    wout,
    kall,
    vall,
    wgu,
    wd,
    qkv,
    part_send,
    part_recv,
    proj_send,
    proj_recv,
    stat_send,
    stat_recv,
    disp_send,
    disp_recv,
    sq_send,
    sq_recv,
    gu_send,
    gu_recv,
    gsum,
    hid,
    ret_send,
    ret_recv,
    mix_send,
    mix_recv,
    local_sem,
    send_sem,
    recv_sem,
):
    chips = columns // 2
    ffe = wd.shape[1]
    cap = pk_hbm.shape[1]
    experts = wr.shape[1]
    depth = x_ref.shape[2]
    g = lax.axis_index("grp")
    e = lax.axis_index("exp")
    y = e // 2
    c = e % 2
    half = g % 2
    partner = g + 1 - 2 * half
    sibling = e + 1 - 2 * c
    own_rows = pl.ds(pl.multiple_of(c * HDIM, HDIM), HDIM)

    def local(src, dst, index):
        copy = pltpu.make_async_copy(src, dst, local_sem.at[index])
        copy.start()
        return copy

    def remote(src, dst, index, **where):
        return pltpu.make_async_remote_copy(
            src_ref=src,
            dst_ref=dst,
            send_sem=send_sem.at[index],
            recv_sem=recv_sem.at[index],
            device_id=where,
            device_id_type=pl.DeviceIdType.MESH,
        )

    def wait_bytes(ref, sem):
        pltpu.make_async_copy(ref, ref, sem).wait()

    load_inputs = local(x_hbm.at[0], x_ref, 6)
    load_parents = local(par_hbm, par_ref, 7)
    load_routes = local(routes_hbm.at[0], routes_ref, 8)
    load_parts = local(parts_hbm, parts_ref, 9)
    load_qkv = local(wqkv_hbm, wqkv, 0)
    load_tail_k = local(tk_hbm.at[0], tk_ref, 10)
    load_tail_v = local(tv_hbm.at[0], tv_ref, 11)
    load_gain = local(gain_hbm, gain.at[c], 12)
    load_router = local(wr_hbm, wr.at[c], 13)
    load_keys = local(pk_hbm.at[0], kall.at[pl.ds(0, cap)], 1)
    load_values = local(pv_hbm.at[0], vall.at[pl.ds(0, cap)], 2)
    load_out = local(wout_hbm, wout, 3)
    load_gu = local(wgu_hbm.at[c], wgu.at[own_rows], 4)
    load_down = local(wd_hbm.at[c], wd.at[own_rows], 5)

    barrier = pltpu.get_barrier_semaphore()

    def greet_group(k, carry):
        other = lax.rem(g + k, groups)
        pl.semaphore_signal(
            barrier, inc=1, device_id={"grp": other}, device_id_type=pl.DeviceIdType.MESH
        )
        return carry

    def greet_column(k, carry):
        other = lax.rem(e + k, columns)
        pl.semaphore_signal(
            barrier, inc=1, device_id={"exp": other}, device_id_type=pl.DeviceIdType.MESH
        )
        return carry

    lax.fori_loop(1, groups, greet_group, 0)
    lax.fori_loop(1, columns, greet_column, 0)

    load_inputs.wait()
    load_routes.wait()
    load_parents.wait()
    for s in range(STEPS):
        xs[HALF * s : HALF * (s + 1), :] = x_ref[s].astype(F32)
        rts[HALF * s : HALF * (s + 1), :topk] = routes_ref[s]
    x16 = xs[...].astype(BF16)
    row_sub = iota((ROWS, HDIM), 0)
    row_lane = iota((ROWS, HDIM), 1)
    parent_hot = jnp.zeros((ROWS, HDIM), F32)
    for s in range(STEPS):
        for b in range(HALF):
            parent_hot = jnp.where(
                (row_sub == HALF * s + b) & (row_lane == par_ref[0, s, b]), 1.0, parent_hot
            )
    load_qkv.wait()
    for i in range(3):
        qkv[0, :, HDIM * i : HDIM * (i + 1)] = dot(x16, wqkv[i]).astype(BF16)
    qkv[0, :, 3 * HDIM : 4 * HDIM] = parent_hot.astype(BF16)

    pl.semaphore_wait(barrier, groups + columns - 2)

    qkv_copy = remote(qkv.at[0], qkv.at[1], 0, grp=partner)
    qkv_copy.start()
    swap_gain = remote(gain_hbm, gain.at[c], 1, exp=sibling)
    swap_router = remote(wr_hbm, wr.at[c], 2, exp=sibling)
    swap_gu = remote(wgu_hbm.at[1 - c], wgu.at[own_rows], 3, exp=sibling)
    swap_down = remote(wd_hbm.at[1 - c], wd.at[own_rows], 4, exp=sibling)
    swap_gain.start()
    swap_router.start()
    swap_gu.start()
    swap_down.start()

    tail_at = cap
    new_at = cap + HALF * PREV
    total = new_at + 2 * ROWS
    load_tail_k.wait()
    load_tail_v.wait()
    kall[tail_at:new_at, :] = tk_ref[...].astype(F32).reshape(HALF * PREV, HDIM).astype(BF16)
    vall[tail_at:new_at, :] = tv_ref[...].astype(F32).reshape(HALF * PREV, HDIM).astype(BF16)

    width = groups * SEND
    routes = rts[...]
    hit = jnp.zeros((ROWS, experts), jnp.bool_)
    expert_lane = iota((ROWS, experts), 1)
    for k in range(topk):
        hit = hit | (routes[:, k : k + 1] == expert_lane)
    hits = one_hot(hit)
    rank = dot(one_hot(iota((ROWS, ROWS), 1) < iota((ROWS, ROWS), 0)), hits)
    spread_row = iota((experts, width), 0)
    spread_lane = iota((experts, width), 1)
    spread = one_hot(spread_row == 2 * (spread_lane // SEND) + c)
    hit_wide = dot(hits, spread)
    rank_wide = dot(rank.astype(BF16), spread)
    slot_lane = (iota((ROWS, width), 1) % SEND).astype(F32)
    place = jnp.where((rank_wide == slot_lane) & (hit_wide > 0.5), 1.0, 0.0)

    load_keys.wait()
    load_values.wait()
    qkv_copy.wait_recv()
    for h in range(2):
        at = new_at + ROWS * h
        kall[at : at + ROWS, :] = qkv[h, :, HDIM : 2 * HDIM]
        vall[at : at + ROWS, :] = qkv[h, :, 2 * HDIM : 3 * HDIM]
    query = jnp.concatenate([qkv[0, :, 0:HDIM], qkv[1, :, 0:HDIM]], axis=0)
    parents = jnp.concatenate(
        [qkv[0, :, 3 * HDIM : 4 * HDIM], qkv[1, :, 3 * HDIM : 4 * HDIM]], axis=0
    )
    tokens = 2 * ROWS
    beam_row = iota((HDIM, tokens), 0)
    token_lane = iota((HDIM, tokens), 1)
    beam_of = HALF * ((token_lane // ROWS + half) % 2) + token_lane % HALF
    before = dot(parents, one_hot(beam_row == beam_of))
    step_row = (iota((tokens, tokens), 0) % ROWS) // HALF
    step_lane = (iota((tokens, tokens), 1) % ROWS) // HALF
    same = jnp.where(iota((tokens, tokens), 0) == iota((tokens, tokens), 1), 1.0, 0.0)
    back = jnp.where(step_lane + 1 == step_row, before, 0.0)
    back_bf = back.astype(BF16)
    near = (same + back).astype(BF16)
    back_two = dot(back_bf, back_bf)
    path = dot(near, (same + back_two).astype(BF16)).astype(BF16)
    first_row = iota((tokens, HDIM), 0) % ROWS
    first = jnp.where(first_row < HALF, parents.astype(F32), 0.0).astype(BF16)
    origin = dot(path, first).astype(BF16)
    tails = HALF * PREV
    tail_row = iota((HDIM, tails), 0)
    tail_lane = iota((HDIM, tails), 1)
    tail_on = dot(origin, one_hot(tail_row == HALF * half + tail_lane % HALF))
    new_on = jnp.where(iota((tokens, tokens), 0) < ROWS, path.astype(F32), 0.0)

    load_parts.wait()
    score_scale = HDIM ** (-0.5)
    scores = dot_t(query, kall[...]) * score_scale
    prompt_live = iota((tokens, cap), 1) < parts_ref[0]
    prompt_s = jnp.where(prompt_live, scores[:, 0:cap], NEGATIVE)
    tail_s = jnp.where(tail_on > 0.5, scores[:, tail_at:new_at], NEGATIVE)
    new_s = jnp.where(new_on > 0.5, scores[:, new_at:total], NEGATIVE)
    top = jnp.maximum(
        jnp.maximum(
            jnp.max(prompt_s, axis=1, keepdims=True), jnp.max(tail_s, axis=1, keepdims=True)
        ),
        jnp.max(new_s, axis=1, keepdims=True),
    )
    prompt_w = jnp.exp(prompt_s - top)
    tail_w = jnp.exp(tail_s - top)
    new_w = jnp.exp(new_s - top)
    weight_sum = (
        jnp.sum(prompt_w, axis=1, keepdims=True)
        + jnp.sum(tail_w, axis=1, keepdims=True)
        + jnp.sum(new_w, axis=1, keepdims=True)
    )

    def weighted(weights, values):
        high, low = split_high(weights)
        both = dot(jnp.concatenate([high, low], axis=0), values)
        return both[0:tokens] + both[tokens : 2 * tokens]

    mix = (
        weighted(prompt_w, vall[0:cap, :])
        + weighted(tail_w, vall[tail_at:new_at, :])
        + weighted(new_w, vall[new_at:total, :])
    )
    part_send[:, 0:HDIM] = mix[ROWS:tokens]
    lane = iota((ROWS, HDIM), 1)
    part_send[:, HDIM : 2 * HDIM] = jnp.where(
        lane < HDIM // 2, top[ROWS:tokens], weight_sum[ROWS:tokens]
    )
    part_copy = remote(part_send, part_recv, 5, grp=partner)
    part_copy.start()
    load_out.wait()
    part_copy.wait_recv()
    far_mix = part_recv[:, 0:HDIM]
    far_top = part_recv[:, HDIM : HDIM + 1]
    far_sum = part_recv[:, HDIM + HDIM // 2 : HDIM + HDIM // 2 + 1]
    near_top = top[0:ROWS]
    best = jnp.maximum(near_top, far_top)
    near_factor = jnp.exp(near_top - best)
    far_factor = jnp.exp(far_top - best)
    attention = (
        (mix[0:ROWS] * near_factor + far_mix * far_factor)
        / (weight_sum[0:ROWS] * near_factor + far_sum * far_factor)
    ).astype(BF16)

    chip = 2 * HDIM
    proj = dot(attention, wout[...])
    for d in range(chips):
        proj_send[d] = proj[:, chip * d : chip * (d + 1)].astype(BF16)

    def send_proj(k, carry):
        other = lax.rem(e + k, columns)
        remote(proj_send.at[other // 2], proj_recv.at[e], 6, exp=other).start()
        return carry

    lax.fori_loop(1, columns, send_proj, 0)
    proj_recv[pl.ds(e, 1)] = proj_send[pl.ds(y, 1)]
    residual = xs[:, pl.ds(pl.multiple_of(y * chip, chip), chip)]
    wait_bytes(proj_recv.at[pl.ds(0, columns - 1)], recv_sem.at[6])
    residual = residual + jnp.sum(proj_recv[...].astype(F32), axis=0)

    rows_bf = residual.astype(BF16)
    outgoing = lax.dot_general(
        place.astype(BF16), rows_bf, (((0,), (0,)), ((), ())), preferred_element_type=F32
    ).astype(BF16)
    disp_send[...] = outgoing.reshape(groups, SEND, chip)

    def send_disp(k, carry):
        other = lax.rem(g + k, groups)
        remote(disp_send.at[other], disp_recv.at[g], 7, grp=other).start()
        return carry

    lax.fori_loop(1, groups, send_disp, 0)
    disp_recv[pl.ds(g, 1)] = disp_send[pl.ds(g, 1)]

    load_gain.wait()
    load_router.wait()
    swap_gain.wait_recv()
    swap_router.wait_recv()
    gains = jnp.concatenate([gain[0], gain[1]], axis=1)
    scaled = (residual * gains).astype(BF16)
    logit_part = dot_t(scaled[:, 0:HDIM], wr[0]) + dot_t(scaled[:, HDIM:chip], wr[1])
    stat_send[:, 0:experts] = logit_part
    stat_send[:, experts:HDIM] = jnp.broadcast_to(
        jnp.sum(residual * residual, axis=1, keepdims=True), (ROWS, HDIM - experts)
    )

    def send_stat(k, carry):
        other = lax.rem(y + k, chips)
        remote(stat_send, stat_recv.at[y], 8, exp=2 * other + c).start()
        return carry

    lax.fori_loop(1, chips, send_stat, 0)
    stat_recv[pl.ds(y, 1)] = stat_send[...].reshape(1, ROWS, stat_send.shape[1])

    wait_bytes(disp_recv.at[pl.ds(0, groups - 1)], recv_sem.at[7])
    arrived = disp_recv[...].reshape(groups * SEND, chip)
    packed = chips * PADB
    pick_row = iota((packed, groups * SEND), 0)
    pick_lane = iota((packed, groups * SEND), 1)
    per = BLOCK // CAP_E
    own_dest = pick_row // PADB

    def picks(shift):
        index = pick_row % PADB - shift
        safe = jnp.maximum(index, 0)
        source = (own_dest * per + safe // CAP_E) * SEND + safe % CAP_E
        return one_hot((index >= 0) & (index < BLOCK) & (pick_lane == source))

    gate_rows = dot(picks(0), arrived)
    up_rows = dot(picks(PADB - BLOCK), arrived)
    squares = dot_t(
        jnp.ones((8, chip), F32), gate_rows * gate_rows, precision=lax.Precision.HIGHEST
    )
    sq_send[...] = squares

    def send_sq(k, carry):
        other = lax.rem(y + k, chips)
        remote(sq_send, sq_recv.at[y], 9, exp=2 * other + c).start()
        return carry

    lax.fori_loop(1, chips, send_sq, 0)
    sq_recv[pl.ds(y, 1)] = squares.reshape(1, 8, packed)
    gate_in = (gate_rows * gains).astype(BF16)
    up_in = (up_rows * gains).astype(BF16)
    load_gu.wait()
    swap_gu.wait_recv()
    for t in range(ffe // HDIM):
        lanes = slice(HDIM * t, HDIM * (t + 1))
        gate = dot(gate_in, wgu[:, lanes]).reshape(chips, 2, 8, HDIM)
        up = dot(up_in, wgu[:, ffe + HDIM * t : ffe + HDIM * (t + 1)]).reshape(chips, 2, 8, HDIM)
        gu_send[:, 0:8, lanes] = gate[:, 0].astype(BF16)
        gu_send[:, 8:16, lanes] = (gate[:, 1] + up[:, 0]).astype(BF16)
        gu_send[:, 16:24, lanes] = up[:, 1].astype(BF16)

    def send_gu(k, carry):
        other = lax.rem(y + k, chips)
        remote(gu_send.at[other], gu_recv.at[y], 10, exp=2 * other + c).start()
        return carry

    lax.fori_loop(1, chips, send_gu, 0)
    gu_recv[pl.ds(y, 1)] = gu_send[pl.ds(y, 1)]

    wait_bytes(stat_recv.at[pl.ds(0, chips - 1)], recv_sem.at[8])
    stats = jnp.sum(stat_recv[...], axis=0)
    mean_square = stats[:, experts : experts + 1] / depth
    logits = stats[:, 0:experts] * lax.rsqrt(mean_square + EPSILON)
    picked_top = jnp.max(jnp.where(hit, logits, NEGATIVE), axis=1, keepdims=True)
    picked = jnp.where(hit, jnp.exp(jnp.minimum(logits - picked_top, 0.0)), 0.0)
    share = picked / jnp.sum(picked, axis=1, keepdims=True)
    share_high, share_low = split_high(share)
    shares = jnp.concatenate([share_high, share_low], axis=0)
    share_wide = dot(shares, spread)
    combine = jnp.concatenate(
        [
            (share_wide[0:ROWS] * place).astype(BF16),
            (share_wide[ROWS : 2 * ROWS] * place).astype(BF16),
        ],
        axis=0,
    )
    wait_bytes(sq_recv.at[pl.ds(0, chips - 1)], recv_sem.at[9])
    square_sums = jnp.sum(sq_recv[...], axis=0)[0:1, :]
    scale_row = iota((2 * BLOCK, packed), 0) % BLOCK
    scale_lane = iota((2 * BLOCK, packed), 1)
    own_square = jnp.sum(
        jnp.where(scale_lane == y * PADB + scale_row, square_sums, 0.0), axis=1, keepdims=True
    )
    scale = lax.rsqrt(own_square / depth + EPSILON)

    wait_bytes(gu_recv.at[pl.ds(0, chips - 1)], recv_sem.at[10])
    gsum[0 : 2 * BLOCK, :] = jnp.sum(gu_recv[...].astype(F32), axis=0) * scale
    gsum[2 * BLOCK : 2 * PADB, :] = jnp.zeros((2 * PADB - 2 * BLOCK, ffe), F32)
    gates = gsum[0:PADB, :]
    ups = gsum[BLOCK : BLOCK + PADB, :]
    hid[pl.ds(y, 1)] = (
        (gates / (1.0 + jnp.exp(-gates)) * ups).astype(BF16).reshape(1, PADB, ffe)
    )

    def send_hid(k, carry):
        other = lax.rem(y + k, chips)
        remote(hid.at[y], hid.at[y], 11, exp=2 * other + c).start()
        return carry

    lax.fori_loop(1, chips, send_hid, 0)
    load_down.wait()
    swap_down.wait_recv()
    back_row = iota((groups * SEND, packed), 0)
    back_lane = iota((groups * SEND, packed), 1)
    back_slot = back_row // SEND
    back_rank = back_row % SEND
    back_source = (back_slot // per) * PADB + (back_slot % per) * CAP_E + back_rank
    back_pick = one_hot((back_rank < CAP_E) & (back_lane == back_source))
    wait_bytes(hid.at[pl.ds(0, chips - 1)], recv_sem.at[11])
    result = dot_t(hid[...].reshape(packed, ffe), wd[...]).astype(BF16)
    ret_send[...] = dot(back_pick, result).astype(BF16).reshape(groups, SEND, chip)

    def send_ret(k, carry):
        other = lax.rem(g + k, groups)
        remote(ret_send.at[other], ret_recv.at[g], 12, grp=other).start()
        return carry

    lax.fori_loop(1, groups, send_ret, 0)
    ret_recv[pl.ds(g, 1)] = ret_send[pl.ds(g, 1)]
    wait_bytes(ret_recv.at[pl.ds(0, groups - 1)], recv_sem.at[12])
    both = dot(combine, ret_recv[...].reshape(groups * SEND, chip))
    expert_mix = both[0:ROWS] + both[ROWS : 2 * ROWS]
    mix_send[...] = jnp.where(c == 0, expert_mix[:, HDIM:chip], expert_mix[:, 0:HDIM])
    mix_copy = remote(mix_send, mix_recv, 13, exp=sibling)
    mix_copy.start()
    own = jnp.where(
        c == 0,
        residual[:, 0:HDIM] + expert_mix[:, 0:HDIM],
        residual[:, HDIM:chip] + expert_mix[:, HDIM:chip],
    )
    mix_copy.wait_recv()
    out_ref[...] = own + mix_recv[...]

    qkv_copy.wait_send()
    swap_gain.wait_send()
    swap_router.wait_send()
    swap_gu.wait_send()
    swap_down.wait_send()
    part_copy.wait_send()
    mix_copy.wait_send()
    wait_bytes(proj_recv.at[pl.ds(0, columns - 1)], send_sem.at[6])
    wait_bytes(disp_recv.at[pl.ds(0, groups - 1)], send_sem.at[7])
    wait_bytes(stat_recv.at[pl.ds(0, chips - 1)], send_sem.at[8])
    wait_bytes(sq_recv.at[pl.ds(0, chips - 1)], send_sem.at[9])
    wait_bytes(gu_recv.at[pl.ds(0, chips - 1)], send_sem.at[10])
    wait_bytes(hid.at[pl.ds(0, chips - 1)], send_sem.at[11])
    wait_bytes(ret_recv.at[pl.ds(0, groups - 1)], send_sem.at[12])


def on_device(
    step_inputs,
    parents,
    routes,
    w_qkv,
    w_out,
    prompt_keys,
    prompt_values,
    prompt_parts,
    tail_keys,
    tail_values,
    w_router,
    norm_gain,
    w_gate_up,
    w_down,
):
    groups = lax.axis_size("grp")
    columns = lax.axis_size("exp")
    chips = columns // 2
    depth = step_inputs.shape[3]
    cap = prompt_keys.shape[1]
    ffe = w_down.shape[2]
    experts = w_router.shape[1]
    topk = routes.shape[3]
    chip = 2 * HDIM
    keys = cap + HALF * PREV + 2 * ROWS
    vmem = pl.BlockSpec(memory_space=pltpu.VMEM)
    out = pl.pallas_call(
        functools.partial(kernel, groups, columns, topk),
        out_shape=jax.ShapeDtypeStruct((ROWS, HDIM), F32),
        in_specs=[
            pl.BlockSpec(memory_space=pltpu.HBM)
        ]
        * 14,
        out_specs=vmem,
        scratch_shapes=[
            pltpu.VMEM((STEPS, HALF, depth), BF16),
            pltpu.SMEM((1, STEPS, HALF), jnp.int32),
            pltpu.VMEM((STEPS, HALF, topk), jnp.int32),
            pltpu.SMEM((1,), jnp.int32),
            pltpu.VMEM((PREV, HALF, HDIM), BF16),
            pltpu.VMEM((PREV, HALF, HDIM), BF16),
            pltpu.VMEM((ROWS, depth), F32),
            pltpu.VMEM((ROWS, HDIM), jnp.int32),
            pltpu.VMEM((2, 1, HDIM), F32),
            pltpu.VMEM((2, experts, HDIM), BF16),
            pltpu.VMEM((3, depth, HDIM), BF16),
            pltpu.VMEM((HDIM, depth), BF16),
            pltpu.VMEM((keys, HDIM), BF16),
            pltpu.VMEM((keys, HDIM), BF16),
            pltpu.VMEM((chip, 2 * ffe), BF16),
            pltpu.VMEM((chip, ffe), BF16),
            pltpu.VMEM((2, ROWS, 4 * HDIM), BF16),
            pltpu.VMEM((ROWS, chip), F32),
            pltpu.VMEM((ROWS, chip), F32),
            pltpu.VMEM((chips, ROWS, chip), BF16),
            pltpu.VMEM((columns, ROWS, chip), BF16),
            pltpu.VMEM((ROWS, HDIM), F32),
            pltpu.VMEM((chips, ROWS, HDIM), F32),
            pltpu.VMEM((groups, SEND, chip), BF16),
            pltpu.VMEM((groups, SEND, chip), BF16),
            pltpu.VMEM((8, chips * PADB), F32),
            pltpu.VMEM((chips, 8, chips * PADB), F32),
            pltpu.VMEM((chips, 2 * BLOCK, ffe), BF16),
            pltpu.VMEM((chips, 2 * BLOCK, ffe), BF16),
            pltpu.VMEM((2 * PADB, ffe), F32),
            pltpu.VMEM((chips, PADB, ffe), BF16),
            pltpu.VMEM((groups, SEND, chip), BF16),
            pltpu.VMEM((groups, SEND, chip), BF16),
            pltpu.VMEM((ROWS, HDIM), F32),
            pltpu.VMEM((ROWS, HDIM), F32),
            pltpu.SemaphoreType.DMA((14,)),
            pltpu.SemaphoreType.DMA((14,)),
            pltpu.SemaphoreType.DMA((14,)),
        ],
        compiler_params=pltpu.CompilerParams(
            collective_id=0, has_side_effects=True, vmem_limit_bytes=64 * 1024 * 1024
        ),
        name="layer",
    )(
        step_inputs,
        parents,
        routes,
        prompt_parts,
        norm_gain.reshape(1, HDIM),
        w_router.T,
        jnp.transpose(w_qkv, (1, 0, 2)),
        w_out,
        prompt_keys,
        prompt_values,
        jnp.transpose(tail_keys, (0, 2, 1, 3)),
        jnp.transpose(tail_values, (0, 2, 1, 3)),
        w_gate_up,
        w_down,
    )
    return out.astype(BF16).reshape(1, STEPS, HALF, HDIM)


def solution(mesh):
    placed = (
        P("grp", None, None, None),
        P("grp", None, None),
        P("grp", None, None, None),
        P(None, None, "exp"),
        P("exp", None),
        P("grp", None, "exp"),
        P("grp", None, "exp"),
        P("grp"),
        P("grp", None, None, "exp"),
        P("grp", None, None, "exp"),
        P("exp", None),
        P("exp"),
        P("grp", "exp", None),
        P("grp", "exp", None),
    )
    return jax.shard_map(
        on_device,
        mesh=mesh,
        in_specs=placed,
        out_specs=P("grp", None, None, "exp"),
        check_vma=False,
    )
```

```python
import functools

import jax
import jax.numpy as jnp
from jax import lax
from jax.experimental import pallas as pl
from jax.experimental.pallas import tpu as pltpu
from jax.sharding import PartitionSpec as P

HDIM = 128
TOPK = 6
STEPS = 4
HALF = 4
ROWS = STEPS * HALF
CAP_E = 3
PREV = 60
SEND = 4
BLOCK = 12
PADB = 16

NEGATIVE = -1e30
EPSILON = 1e-06
F32 = jnp.float32
BF16 = jnp.bfloat16


def iota(shape, axis):
    return lax.broadcasted_iota(jnp.int32, shape, axis)


def dot(a, b, precision=None):
    return jnp.dot(a, b, preferred_element_type=F32, precision=precision)


def dot_t(a, b, precision=None):
    return lax.dot_general(
        a, b, (((1,), (1,)), ((), ())), preferred_element_type=F32, precision=precision
    )


def one_hot(cond):
    return jnp.where(cond, 1.0, 0.0).astype(BF16)


def split_high(value):
    high = value.astype(BF16)
    return high, (value - high.astype(F32)).astype(BF16)


def column_spans(ffe):
    first = (ffe // HDIM + 1) // 2 * HDIM
    return (0, first), (first, ffe - first)


def kernel(
    groups,
    columns,
    topk,
    x_hbm,
    par_hbm,
    routes_hbm,
    parts_hbm,
    gain_hbm,
    wr_hbm,
    wqkv_hbm,
    wout_hbm,
    pk_hbm,
    pv_hbm,
    tk_hbm,
    tv_hbm,
    wgu_hbm,
    wd_hbm,
    out_ref,
    x_ref,
    par_ref,
    routes_ref,
    parts_ref,
    tk_ref,
    tv_ref,
    xs,
    rts,
    gain,
    wr,
    wqkv,
    wout,
    kall,
    vall,
    wgu,
    wd,
    qkv,
    part_send,
    part_recv,
    att,
    proj_send,
    proj_recv,
    stat_send,
    stat_recv,
    disp_send,
    disp_recv,
    sq_send,
    sq_recv,
    gu_send,
    gu_mid,
    gu_pass,
    gu_recv,
    gsum,
    hid,
    ret_send,
    ret_recv,
    mix_send,
    mix_recv,
    local_sem,
    send_sem,
    recv_sem,
):
    chips = columns // 2
    ffe = wd.shape[1]
    spans = column_spans(ffe)
    cap = pk_hbm.shape[1]
    experts = wr.shape[1]
    depth = x_ref.shape[2]
    g = lax.axis_index("grp")
    e = lax.axis_index("exp")
    y = e // 2
    c = e % 2
    half = g % 2
    partner = g + 1 - 2 * half
    sibling = e + 1 - 2 * c
    own_rows = pl.ds(pl.multiple_of(c * HDIM, HDIM), HDIM)

    waits = {}

    def done(kind, index):
        waits.pop((kind, index))()

    def finish():
        for key in list(waits):
            done(*key)

    def local(src, dst, index):
        copy = pltpu.make_async_copy(src, dst, local_sem.at[index])
        copy.start()
        waits["load", index] = copy.wait

    def remote(src, dst, index, **where):
        return pltpu.make_async_remote_copy(
            src_ref=src,
            dst_ref=dst,
            send_sem=send_sem.at[index],
            recv_sem=recv_sem.at[index],
            device_id=where,
            device_id_type=pl.DeviceIdType.MESH,
        )

    def send(src, dst, index, **where):
        copy = remote(src, dst, index, **where)
        copy.start()
        waits["recv", index] = copy.wait_recv
        waits["send", index] = copy.wait_send

    def send_each(count, one, landing, index):
        def step(k, carry):
            one(k).start()
            return carry

        lax.fori_loop(1, count, step, 0)
        whole = landing.at[pl.ds(0, count - 1)]
        waits["recv", index] = pltpu.make_async_copy(whole, whole, recv_sem.at[index]).wait
        waits["send", index] = pltpu.make_async_copy(whole, whole, send_sem.at[index]).wait

    def other_group(k):
        return lax.rem(g + k, groups)

    def other_column(k):
        return lax.rem(e + k, columns)

    def other_chip(k):
        return lax.rem(y + k, chips)

    local(x_hbm.at[0], x_ref, 6)
    local(par_hbm, par_ref, 7)
    local(routes_hbm.at[0], routes_ref, 8)
    local(parts_hbm, parts_ref, 9)
    local(wqkv_hbm, wqkv, 0)
    local(tk_hbm.at[0], tk_ref, 10)
    local(tv_hbm.at[0], tv_ref, 11)
    local(gain_hbm, gain.at[c], 12)
    local(wr_hbm, wr.at[c], 13)
    local(pk_hbm.at[0], kall.at[pl.ds(0, cap)], 1)
    local(pv_hbm.at[0], vall.at[pl.ds(0, cap)], 2)
    local(wout_hbm, wout.at[own_rows], 3)
    local(wgu_hbm.at[c], wgu.at[own_rows], 4)
    local(wd_hbm.at[c], wd.at[own_rows], 5)

    barrier = pltpu.get_barrier_semaphore()

    def greet_group(k, carry):
        other = lax.rem(g + k, groups)
        pl.semaphore_signal(
            barrier, inc=1, device_id={"grp": other}, device_id_type=pl.DeviceIdType.MESH
        )
        return carry

    def greet_column(k, carry):
        other = lax.rem(e + k, columns)
        pl.semaphore_signal(
            barrier, inc=1, device_id={"exp": other}, device_id_type=pl.DeviceIdType.MESH
        )
        return carry

    lax.fori_loop(1, groups, greet_group, 0)
    lax.fori_loop(1, columns, greet_column, 0)

    done("load", 6)
    done("load", 8)
    done("load", 7)
    for s in range(STEPS):
        xs[HALF * s : HALF * (s + 1), :] = x_ref[s].astype(F32)
        rts[HALF * s : HALF * (s + 1), :topk] = routes_ref[s]
    x16 = xs[...].astype(BF16)
    row_sub = iota((ROWS, HDIM), 0)
    row_lane = iota((ROWS, HDIM), 1)
    parent_hot = jnp.zeros((ROWS, HDIM), F32)
    for s in range(STEPS):
        for b in range(HALF):
            parent_hot = jnp.where(
                (row_sub == HALF * s + b) & (row_lane == par_ref[0, s, b]), 1.0, parent_hot
            )
    done("load", 0)
    for i in range(3):
        qkv[0, :, HDIM * i : HDIM * (i + 1)] = dot(x16, wqkv[i]).astype(BF16)
    qkv[0, :, 3 * HDIM : 4 * HDIM] = parent_hot.astype(BF16)

    pl.semaphore_wait(barrier, groups + columns - 2)

    send(qkv.at[0], qkv.at[1], 0, grp=partner)
    send(wout_hbm, wout.at[own_rows], 6, exp=sibling)
    send(gain_hbm, gain.at[c], 1, exp=sibling)
    send(wr_hbm, wr.at[c], 2, exp=sibling)
    send(wgu_hbm.at[1 - c], wgu.at[own_rows], 3, exp=sibling)
    send(wd_hbm.at[1 - c], wd.at[own_rows], 4, exp=sibling)

    tail_at = cap
    new_at = cap + HALF * PREV
    total = new_at + 2 * ROWS
    done("load", 10)
    done("load", 11)
    kall[tail_at:new_at, :] = tk_ref[...].astype(F32).reshape(HALF * PREV, HDIM).astype(BF16)
    vall[tail_at:new_at, :] = tv_ref[...].astype(F32).reshape(HALF * PREV, HDIM).astype(BF16)

    width = groups * SEND
    routes = rts[...]
    hit = jnp.zeros((ROWS, experts), jnp.bool_)
    expert_lane = iota((ROWS, experts), 1)
    for k in range(topk):
        hit = hit | (routes[:, k : k + 1] == expert_lane)
    hits = one_hot(hit)
    rank = dot(one_hot(iota((ROWS, ROWS), 1) < iota((ROWS, ROWS), 0)), hits)
    spread_row = iota((experts, width), 0)
    spread_lane = iota((experts, width), 1)
    spread = one_hot(spread_row == 2 * (spread_lane // SEND) + c)
    hit_wide = dot(hits, spread)
    rank_wide = dot(rank.astype(BF16), spread)
    slot_lane = (iota((ROWS, width), 1) % SEND).astype(F32)
    place = jnp.where((rank_wide == slot_lane) & (hit_wide > 0.5), 1.0, 0.0)

    done("load", 1)
    done("load", 2)
    done("recv", 0)
    for h in range(2):
        at = new_at + ROWS * h
        kall[at : at + ROWS, :] = qkv[h, :, HDIM : 2 * HDIM]
        vall[at : at + ROWS, :] = qkv[h, :, 2 * HDIM : 3 * HDIM]
    query = jnp.concatenate([qkv[0, :, 0:HDIM], qkv[1, :, 0:HDIM]], axis=0)
    parents = jnp.concatenate(
        [qkv[0, :, 3 * HDIM : 4 * HDIM], qkv[1, :, 3 * HDIM : 4 * HDIM]], axis=0
    )
    tokens = 2 * ROWS
    beam_row = iota((HDIM, tokens), 0)
    token_lane = iota((HDIM, tokens), 1)
    beam_of = HALF * ((token_lane // ROWS + half) % 2) + token_lane % HALF
    before = dot(parents, one_hot(beam_row == beam_of))
    step_row = (iota((tokens, tokens), 0) % ROWS) // HALF
    step_lane = (iota((tokens, tokens), 1) % ROWS) // HALF
    same = jnp.where(iota((tokens, tokens), 0) == iota((tokens, tokens), 1), 1.0, 0.0)
    back = jnp.where(step_lane + 1 == step_row, before, 0.0)
    back_bf = back.astype(BF16)
    near = (same + back).astype(BF16)
    back_two = dot(back_bf, back_bf)
    path = dot(near, (same + back_two).astype(BF16)).astype(BF16)
    first_row = iota((tokens, HDIM), 0) % ROWS
    first = jnp.where(first_row < HALF, parents.astype(F32), 0.0).astype(BF16)
    origin = dot(path, first).astype(BF16)
    tails = HALF * PREV
    tail_row = iota((HDIM, tails), 0)
    tail_lane = iota((HDIM, tails), 1)
    tail_on = dot(origin, one_hot(tail_row == HALF * half + tail_lane % HALF))
    new_on = jnp.where(iota((tokens, tokens), 0) < ROWS, path.astype(F32), 0.0)

    done("load", 9)
    score_scale = HDIM ** (-0.5)
    scores = dot_t(query, kall[...]) * score_scale
    prompt_live = iota((tokens, cap), 1) < parts_ref[0]
    prompt_s = jnp.where(prompt_live, scores[:, 0:cap], NEGATIVE)
    tail_s = jnp.where(tail_on > 0.5, scores[:, tail_at:new_at], NEGATIVE)
    new_s = jnp.where(new_on > 0.5, scores[:, new_at:total], NEGATIVE)
    top = jnp.maximum(
        jnp.maximum(
            jnp.max(prompt_s, axis=1, keepdims=True), jnp.max(tail_s, axis=1, keepdims=True)
        ),
        jnp.max(new_s, axis=1, keepdims=True),
    )
    prompt_w = jnp.exp(prompt_s - top)
    tail_w = jnp.exp(tail_s - top)
    new_w = jnp.exp(new_s - top)
    weight_sum = (
        jnp.sum(prompt_w, axis=1, keepdims=True)
        + jnp.sum(tail_w, axis=1, keepdims=True)
        + jnp.sum(new_w, axis=1, keepdims=True)
    )

    def weighted(weights, values):
        high, low = split_high(weights)
        both = dot(jnp.concatenate([high, low], axis=0), values)
        return both[0:tokens] + both[tokens : 2 * tokens]

    mix = (
        weighted(prompt_w, vall[0:cap, :])
        + weighted(tail_w, vall[tail_at:new_at, :])
        + weighted(new_w, vall[new_at:total, :])
    )
    part_send[:, 0:HDIM] = mix[ROWS:tokens]
    lane = iota((ROWS, HDIM), 1)
    part_send[:, HDIM : 2 * HDIM] = jnp.where(
        lane < HDIM // 2, top[ROWS:tokens], weight_sum[ROWS:tokens]
    )
    send(part_send, part_recv, 5, grp=partner)
    done("recv", 5)
    far_mix = part_recv[:, 0:HDIM]
    far_top = part_recv[:, HDIM : HDIM + 1]
    far_sum = part_recv[:, HDIM + HDIM // 2 : HDIM + HDIM // 2 + 1]
    near_top = top[0:ROWS]
    best = jnp.maximum(near_top, far_top)
    near_factor = jnp.exp(near_top - best)
    far_factor = jnp.exp(far_top - best)
    att[pl.ds(c, 1)] = (
        (mix[0:ROWS] * near_factor + far_mix * far_factor)
        / (weight_sum[0:ROWS] * near_factor + far_sum * far_factor)
    ).astype(BF16).reshape(1, ROWS, HDIM)
    send(att.at[c], att.at[c], 14, exp=sibling)
    done("load", 3)
    done("recv", 6)
    done("recv", 14)

    chip = 2 * HDIM
    proj = dot(jnp.concatenate([att[0], att[1]], axis=1), wout[...])
    for d in range(chips):
        proj_send[d] = proj[:, chip * d : chip * (d + 1)].astype(BF16)
    send_each(
        chips,
        lambda k: remote(
            proj_send.at[other_chip(k)], proj_recv.at[y], 15, exp=2 * other_chip(k) + c
        ),
        proj_recv,
        15,
    )
    proj_recv[pl.ds(y, 1)] = proj_send[pl.ds(y, 1)]
    residual = xs[:, pl.ds(pl.multiple_of(y * chip, chip), chip)]
    done("recv", 15)
    residual = residual + jnp.sum(proj_recv[...].astype(F32), axis=0)

    rows_bf = residual.astype(BF16)
    outgoing = lax.dot_general(
        place.astype(BF16), rows_bf, (((0,), (0,)), ((), ())), preferred_element_type=F32
    )
    disp_send[...] = outgoing.reshape(groups, SEND, chip).astype(BF16)

    send_each(
        groups,
        lambda k: remote(
            disp_send.at[other_group(k)], disp_recv.at[g], 7, grp=other_group(k)
        ),
        disp_recv,
        7,
    )
    disp_recv[pl.ds(g, 1)] = disp_send[pl.ds(g, 1)]

    done("load", 12)
    done("load", 13)
    done("recv", 1)
    done("recv", 2)
    gains = jnp.concatenate([gain[0], gain[1]], axis=1)
    scaled = (residual * gains).astype(BF16)
    logit_part = dot_t(scaled[:, 0:HDIM], wr[0]) + dot_t(scaled[:, HDIM:chip], wr[1])
    stat_send[:, 0:experts] = logit_part
    stat_send[:, experts:HDIM] = jnp.broadcast_to(
        jnp.sum(residual * residual, axis=1, keepdims=True), (ROWS, HDIM - experts)
    )

    send_each(
        chips,
        lambda k: remote(stat_send, stat_recv.at[y], 8, exp=2 * other_chip(k) + c),
        stat_recv,
        8,
    )
    stat_recv[pl.ds(y, 1)] = stat_send[...].reshape(1, ROWS, stat_send.shape[1])

    packed = chips * PADB
    pick_row = iota((packed, groups * SEND), 0)
    pick_lane = iota((packed, groups * SEND), 1)
    per = BLOCK // CAP_E
    own_dest = pick_row // PADB

    def picks(shift):
        index = pick_row % PADB - shift
        safe = jnp.maximum(index, 0)
        source = (own_dest * per + safe // CAP_E) * SEND + safe % CAP_E
        return one_hot((index >= 0) & (index < BLOCK) & (pick_lane == source))

    gate_pick = picks(0)
    up_pick = picks(PADB - BLOCK)
    done("recv", 7)
    arrived = disp_recv[...].astype(F32).reshape(groups * SEND, chip).astype(BF16)
    gate_rows = dot(gate_pick, arrived)
    up_rows = dot(up_pick, arrived)
    squares = dot_t(
        jnp.ones((8, chip), F32), gate_rows * gate_rows, precision=lax.Precision.HIGHEST
    )
    sq_send[...] = squares

    send_each(
        chips,
        lambda k: remote(sq_send, sq_recv.at[y], 9, exp=2 * other_chip(k) + c),
        sq_recv,
        9,
    )
    sq_recv[pl.ds(y, 1)] = squares.reshape(1, 8, packed)
    gate_in = (gate_rows * gains).astype(BF16)
    up_in = (up_rows * gains).astype(BF16)
    done("load", 4)
    done("recv", 3)
    def to_chip(src, dst, index, offset):
        send(src, dst, index, exp=2 * lax.rem(y + offset + chips, chips) + c)

    def rows_of(offset):
        return lax.rem(y + offset + chips, chips)

    for h in range(2):
        first, size = spans[h]
        for at in range(first, first + size, chip):
            wide = min(chip, first + size - at)
            gate = dot(gate_in, wgu[:, at : at + wide]).reshape(chips, 2, 8, wide)
            up = dot(up_in, wgu[:, ffe + at : ffe + at + wide]).reshape(chips, 2, 8, wide)
            lanes = slice(at - first, at - first + wide)
            gu_send[h][:, 0:8, lanes] = gate[:, 0].astype(BF16)
            gu_send[h][:, 8:16, lanes] = (gate[:, 1] + up[:, 0]).astype(BF16)
            gu_send[h][:, 16:24, lanes] = up[:, 1].astype(BF16)
        base = 16 + 7 * h
        far = 1 - 2 * h
        to_chip(gu_send[h].at[rows_of(4)], gu_mid[h].at[2], base + 2, 2 * far)
        to_chip(gu_send[h].at[rows_of(3)], gu_mid[h].at[0], base, 1)
        to_chip(gu_send[h].at[rows_of(-3)], gu_mid[h].at[1], base + 1, -1)
        to_chip(gu_send[h].at[rows_of(1)], gu_recv[h].at[0], base + 3, 1)
        to_chip(gu_send[h].at[rows_of(-1)], gu_recv[h].at[1], base + 4, -1)
    for h in range(2):
        base = 16 + 7 * h
        done("recv", base)
        done("recv", base + 1)
        done("recv", base + 2)
        for i in range(2):
            direction = 1 - 2 * i
            passing = gu_send[h][pl.ds(rows_of(2 * direction), 1)][0].astype(F32)
            passing = passing + gu_mid[h][i].astype(F32)
            if i == h:
                passing = passing + gu_mid[h][2].astype(F32)
            gu_pass[h][i] = passing.astype(BF16)
            to_chip(gu_pass[h].at[i], gu_recv[h].at[2 + i], base + 5 + i, 2 * direction)

    done("recv", 8)
    stats = jnp.sum(stat_recv[...], axis=0)
    mean_square = stats[:, experts : experts + 1] / depth
    logits = stats[:, 0:experts] * lax.rsqrt(mean_square + EPSILON)
    picked_top = jnp.max(jnp.where(hit, logits, NEGATIVE), axis=1, keepdims=True)
    picked = jnp.where(hit, jnp.exp(jnp.minimum(logits - picked_top, 0.0)), 0.0)
    share = picked / jnp.sum(picked, axis=1, keepdims=True)
    share_high, share_low = split_high(share)
    shares = jnp.concatenate([share_high, share_low], axis=0)
    share_wide = dot(shares, spread)
    combine = jnp.concatenate(
        [
            (share_wide[0:ROWS] * place).astype(BF16),
            (share_wide[ROWS : 2 * ROWS] * place).astype(BF16),
        ],
        axis=0,
    )
    done("recv", 9)
    square_sums = jnp.sum(sq_recv[...], axis=0)[0:1, :]
    scale_row = iota((2 * BLOCK, packed), 0) % BLOCK
    scale_lane = iota((2 * BLOCK, packed), 1)
    own_square = jnp.sum(
        jnp.where(scale_lane == y * PADB + scale_row, square_sums, 0.0), axis=1, keepdims=True
    )
    scale = lax.rsqrt(own_square / depth + EPSILON)

    back_row = iota((groups * SEND, packed), 0)
    back_lane = iota((groups * SEND, packed), 1)
    back_slot = back_row // SEND
    back_rank = back_row % SEND
    back_source = (back_slot // per) * PADB + (back_slot % per) * CAP_E + back_rank
    back_pick = one_hot((back_rank < CAP_E) & (back_lane == back_source))

    for h in range(2):
        first, size = spans[h]
        base = 16 + 7 * h
        for i in range(3, 7):
            done("recv", base + i)
        sums = gu_send[h][pl.ds(y, 1)][0].astype(F32)
        for i in range(4):
            sums = sums + gu_recv[h][i].astype(F32)
        gsum[0 : 2 * BLOCK, 0:size] = sums * scale
        gsum[2 * BLOCK : 2 * PADB, 0:size] = jnp.zeros((2 * PADB - 2 * BLOCK, size), F32)
        gates = gsum[0:PADB, 0:size]
        ups = gsum[BLOCK : BLOCK + PADB, 0:size]
        hid[h][pl.ds(y, 1)] = (
            (gates / (1.0 + jnp.exp(-gates)) * ups).astype(BF16).reshape(1, PADB, size)
        )
        send_each(
            chips,
            lambda k, h=h: remote(hid[h].at[y], hid[h].at[y], 11 - h, exp=2 * other_chip(k) + c),
            hid[h],
            11 - h,
        )
    done("load", 5)
    done("recv", 4)
    done("recv", 11)
    result = dot_t(hid[0][...].reshape(packed, spans[0][1]), wd[:, 0 : spans[0][1]])
    done("recv", 10)
    result = result + dot_t(hid[1][...].reshape(packed, spans[1][1]), wd[:, spans[1][0] : ffe])
    result = result.astype(BF16)
    ret_send[...] = dot(back_pick, result).reshape(groups, SEND, chip).astype(BF16)

    send_each(
        groups,
        lambda k: remote(
            ret_send.at[other_group(k)], ret_recv.at[g], 12, grp=other_group(k)
        ),
        ret_recv,
        12,
    )
    ret_recv[pl.ds(g, 1)] = ret_send[pl.ds(g, 1)]
    done("recv", 12)
    returned = ret_recv[...].astype(F32).reshape(groups * SEND, chip).astype(BF16)
    both = dot(combine, returned)
    expert_mix = both[0:ROWS] + both[ROWS : 2 * ROWS]
    mix_send[...] = jnp.where(c == 0, expert_mix[:, HDIM:chip], expert_mix[:, 0:HDIM])
    send(mix_send, mix_recv, 13, exp=sibling)
    own = jnp.where(
        c == 0,
        residual[:, 0:HDIM] + expert_mix[:, 0:HDIM],
        residual[:, HDIM:chip] + expert_mix[:, HDIM:chip],
    )
    done("recv", 13)
    out_ref[...] = own + mix_recv[...]

    finish()


def on_device(
    step_inputs,
    parents,
    routes,
    w_qkv,
    w_out,
    prompt_keys,
    prompt_values,
    prompt_parts,
    tail_keys,
    tail_values,
    w_router,
    norm_gain,
    w_gate_up,
    w_down,
):
    groups = lax.axis_size("grp")
    columns = lax.axis_size("exp")
    chips = columns // 2
    depth = step_inputs.shape[3]
    cap = prompt_keys.shape[1]
    ffe = w_down.shape[2]
    experts = w_router.shape[1]
    topk = routes.shape[3]
    chip = 2 * HDIM
    spans = column_spans(ffe)
    keys = cap + HALF * PREV + 2 * ROWS
    vmem = pl.BlockSpec(memory_space=pltpu.VMEM)
    out = pl.pallas_call(
        functools.partial(kernel, groups, columns, topk),
        out_shape=jax.ShapeDtypeStruct((ROWS, HDIM), F32),
        in_specs=[
            pl.BlockSpec(memory_space=pltpu.HBM)
        ]
        * 14,
        out_specs=vmem,
        scratch_shapes=[
            pltpu.VMEM((STEPS, HALF, depth), BF16),
            pltpu.SMEM((1, STEPS, HALF), jnp.int32),
            pltpu.VMEM((STEPS, HALF, topk), jnp.int32),
            pltpu.SMEM((1,), jnp.int32),
            pltpu.VMEM((PREV, HALF, HDIM), BF16),
            pltpu.VMEM((PREV, HALF, HDIM), BF16),
            pltpu.VMEM((ROWS, depth), F32),
            pltpu.VMEM((ROWS, HDIM), jnp.int32),
            pltpu.VMEM((2, 1, HDIM), F32),
            pltpu.VMEM((2, experts, HDIM), BF16),
            pltpu.VMEM((3, depth, HDIM), BF16),
            pltpu.VMEM((chip, depth), BF16),
            pltpu.VMEM((keys, HDIM), BF16),
            pltpu.VMEM((keys, HDIM), BF16),
            pltpu.VMEM((chip, 2 * ffe), BF16),
            pltpu.VMEM((chip, ffe), BF16),
            pltpu.VMEM((2, ROWS, 4 * HDIM), BF16),
            pltpu.VMEM((ROWS, chip), F32),
            pltpu.VMEM((ROWS, chip), F32),
            pltpu.VMEM((2, ROWS, HDIM), BF16),
            pltpu.VMEM((chips, ROWS, chip), BF16),
            pltpu.VMEM((chips, ROWS, chip), BF16),
            pltpu.VMEM((ROWS, HDIM), F32),
            pltpu.VMEM((chips, ROWS, HDIM), F32),
            pltpu.VMEM((groups, SEND, chip), BF16),
            pltpu.VMEM((groups, SEND, chip), BF16),
            pltpu.VMEM((8, chips * PADB), F32),
            pltpu.VMEM((chips, 8, chips * PADB), F32),
            [pltpu.VMEM((chips, 2 * BLOCK, size), BF16) for _, size in spans],
            [pltpu.VMEM((3, 2 * BLOCK, size), BF16) for _, size in spans],
            [pltpu.VMEM((2, 2 * BLOCK, size), BF16) for _, size in spans],
            [pltpu.VMEM((4, 2 * BLOCK, size), BF16) for _, size in spans],
            pltpu.VMEM((2 * PADB, spans[0][1]), F32),
            [pltpu.VMEM((chips, PADB, size), BF16) for _, size in spans],
            pltpu.VMEM((groups, SEND, chip), BF16),
            pltpu.VMEM((groups, SEND, chip), BF16),
            pltpu.VMEM((ROWS, HDIM), F32),
            pltpu.VMEM((ROWS, HDIM), F32),
            pltpu.SemaphoreType.DMA((14,)),
            pltpu.SemaphoreType.DMA((30,)),
            pltpu.SemaphoreType.DMA((30,)),
        ],
        compiler_params=pltpu.CompilerParams(
            collective_id=0, has_side_effects=True, vmem_limit_bytes=64 * 1024 * 1024
        ),
        name="layer",
    )(
        step_inputs,
        parents,
        routes,
        prompt_parts,
        norm_gain.reshape(1, HDIM),
        w_router.T,
        jnp.transpose(w_qkv, (1, 0, 2)),
        w_out,
        prompt_keys,
        prompt_values,
        jnp.transpose(tail_keys, (0, 2, 1, 3)),
        jnp.transpose(tail_values, (0, 2, 1, 3)),
        w_gate_up,
        w_down,
    )
    return out.astype(BF16).reshape(1, STEPS, HALF, HDIM)


def solution(mesh):
    placed = (
        P("grp", None, None, None),
        P("grp", None, None),
        P("grp", None, None, None),
        P(None, None, "exp"),
        P("exp", None),
        P("grp", None, "exp"),
        P("grp", None, "exp"),
        P("grp"),
        P("grp", None, None, "exp"),
        P("grp", None, None, "exp"),
        P("exp", None),
        P("exp"),
        P("grp", "exp", None),
        P("grp", "exp", None),
    )
    return jax.shard_map(
        on_device,
        mesh=mesh,
        in_specs=placed,
        out_specs=P("grp", None, None, "exp"),
        check_vma=False,
    )
```

```python
import functools

import jax
import jax.numpy as jnp
from jax import lax
from jax.experimental import pallas as pl
from jax.experimental.pallas import tpu as pltpu
from jax.sharding import PartitionSpec as P

HDIM = 128
TOPK = 6
STEPS = 4
HALF = 4
ROWS = STEPS * HALF
CAP_E = 3
PREV = 60
SEND = 4
BLOCK = 12
PADB = 16

NEGATIVE = -1e30
EPSILON = 1e-06
F32 = jnp.float32
BF16 = jnp.bfloat16


def iota(shape, axis):
    return lax.broadcasted_iota(jnp.int32, shape, axis)


def dot(a, b, precision=None):
    return jnp.dot(a, b, preferred_element_type=F32, precision=precision)


def dot_t(a, b, precision=None):
    return lax.dot_general(
        a, b, (((1,), (1,)), ((), ())), preferred_element_type=F32, precision=precision
    )


def one_hot(cond):
    return jnp.where(cond, 1.0, 0.0).astype(BF16)


def split_high(value):
    high = value.astype(BF16)
    return high, (value - high.astype(F32)).astype(BF16)


def column_spans(ffe, chunks=4):
    tiles = ffe // HDIM
    sizes = [HDIM * (tiles // chunks + (h < tiles % chunks)) for h in range(chunks)]
    return [(sum(sizes[:h]), sizes[h]) for h in range(chunks)]


def kernel(
    groups,
    columns,
    topk,
    x_hbm,
    par_hbm,
    routes_hbm,
    parts_hbm,
    gain_hbm,
    wr_hbm,
    wqkv_hbm,
    wout_hbm,
    pk_hbm,
    pv_hbm,
    tk_hbm,
    tv_hbm,
    wgu_hbm,
    wd_hbm,
    out_ref,
    x_ref,
    par_ref,
    routes_ref,
    parts_ref,
    tk_ref,
    tv_ref,
    xs,
    rts,
    gain,
    wr,
    wqkv,
    wout,
    kall,
    vall,
    wgu,
    wd,
    qkv,
    part_send,
    part_recv,
    proj_send,
    proj_recv,
    stat_send,
    stat_recv,
    disp_send,
    disp_recv,
    sq_send,
    sq_recv,
    gu_send,
    gu_mid,
    gu_pass,
    gu_recv,
    gsum,
    hid,
    ret_send,
    ret_recv,
    local_sem,
    send_sem,
    recv_sem,
):
    chips = columns // 2
    ffe = wd.shape[1]
    spans = column_spans(ffe)
    cap = pk_hbm.shape[1]
    experts = wr.shape[1]
    depth = x_ref.shape[2]
    g = lax.axis_index("grp")
    e = lax.axis_index("exp")
    y = e // 2
    c = e % 2
    half = g % 2
    partner = g + 1 - 2 * half
    sibling = e + 1 - 2 * c
    own_rows = pl.ds(pl.multiple_of(c * HDIM, HDIM), HDIM)

    waits = {}

    def done(kind, index):
        waits.pop((kind, index))()

    def finish():
        for key in list(waits):
            done(*key)

    def local(src, dst, index):
        copy = pltpu.make_async_copy(src, dst, local_sem.at[index])
        copy.start()
        waits["load", index] = copy.wait

    def remote(src, dst, index, **where):
        return pltpu.make_async_remote_copy(
            src_ref=src,
            dst_ref=dst,
            send_sem=send_sem.at[index],
            recv_sem=recv_sem.at[index],
            device_id=where,
            device_id_type=pl.DeviceIdType.MESH,
        )

    def send(src, dst, index, **where):
        copy = remote(src, dst, index, **where)
        copy.start()
        waits["recv", index] = copy.wait_recv
        waits["send", index] = copy.wait_send

    def track(count, landing, index):
        whole = landing.at[pl.ds(0, count)]
        waits["recv", index] = pltpu.make_async_copy(whole, whole, recv_sem.at[index]).wait
        waits["send", index] = pltpu.make_async_copy(whole, whole, send_sem.at[index]).wait

    def send_each(order, one, landing, index):
        for k in order:
            one(k).start()
        track(len(order), landing, index)

    deep = 8
    wide_groups = groups // deep
    group_order = [(i, j) for i in range(wide_groups) for j in range(deep) if i or j]
    group_order.sort(key=lambda k: -min(k[0], wide_groups - k[0]) - min(k[1], deep - k[1]))
    chip_order = sorted(range(1, chips), key=lambda k: -min(k, chips - k))

    def other_group(k):
        return lax.rem(g // deep + k[0], wide_groups) * deep + lax.rem(g % deep + k[1], deep)

    def other_chip(k):
        return lax.rem(y + k, chips)

    def to_chip(src, dst, index, offset):
        send(src, dst, index, exp=2 * other_chip(offset + chips) + c)

    local(x_hbm.at[0], x_ref, 6)
    local(par_hbm, par_ref, 7)
    local(routes_hbm.at[0], routes_ref, 8)
    local(parts_hbm, parts_ref, 9)
    for i in range(3):
        local(wqkv_hbm.at[i], wqkv.at[:, pl.ds(HDIM * i, HDIM)], (0, 14, 15)[i])
    local(tk_hbm.at[0], tk_ref, 10)
    local(tv_hbm.at[0], tv_ref, 11)
    local(gain_hbm, gain.at[c], 12)
    local(wr_hbm, wr.at[c], 13)
    local(pk_hbm.at[0], kall.at[pl.ds(0, cap)], 1)
    local(pv_hbm.at[0], vall.at[pl.ds(0, cap)], 2)
    local(wout_hbm, wout.at[pl.ds(0, HDIM)], 3)
    local(wgu_hbm.at[c], wgu.at[own_rows], 4)
    local(wd_hbm.at[c], wd.at[own_rows], 5)

    barrier = pltpu.get_barrier_semaphore()

    def greet(**where):
        pl.semaphore_signal(
            barrier, inc=1, device_id=where, device_id_type=pl.DeviceIdType.MESH
        )

    for k in group_order:
        greet(grp=other_group(k))
    for k in chip_order:
        greet(exp=2 * other_chip(k) + c)
    greet(exp=sibling)
    for k in group_order:
        greet(grp=other_group(k), exp=sibling)

    done("load", 6)
    done("load", 8)
    done("load", 7)
    for s in range(STEPS):
        xs[HALF * s : HALF * (s + 1), :] = x_ref[s].astype(F32)
        rts[HALF * s : HALF * (s + 1), :topk] = routes_ref[s]
    x16 = xs[...].astype(BF16)
    row_sub = iota((ROWS, HDIM), 0)
    row_lane = iota((ROWS, HDIM), 1)
    parent_hot = jnp.zeros((ROWS, HDIM), F32)
    for s in range(STEPS):
        for b in range(HALF):
            parent_hot = jnp.where(
                (row_sub == HALF * s + b) & (row_lane == par_ref[0, s, b]), 1.0, parent_hot
            )
    done("load", 0)
    done("load", 14)
    done("load", 15)
    qkv[0, :, 0 : 3 * HDIM] = dot(x16, wqkv[...]).astype(BF16)
    qkv[0, :, 3 * HDIM : 4 * HDIM] = parent_hot.astype(BF16)

    pl.semaphore_wait(barrier, 2 * groups + chips - 2)

    send(qkv.at[0], qkv.at[1], 0, grp=partner)
    send(wout_hbm, wout.at[pl.ds(HDIM, HDIM)], 6, exp=sibling)
    send(gain_hbm, gain.at[c], 1, exp=sibling)
    send(wr_hbm, wr.at[c], 2, exp=sibling)
    send(wgu_hbm.at[1 - c], wgu.at[own_rows], 3, exp=sibling)
    send(wd_hbm.at[1 - c], wd.at[own_rows], 4, exp=sibling)

    tail_at = cap
    new_at = cap + HALF * PREV
    total = new_at + 2 * ROWS
    done("load", 10)
    done("load", 11)
    kall[tail_at:new_at, :] = tk_ref[...].astype(F32).reshape(HALF * PREV, HDIM).astype(BF16)
    vall[tail_at:new_at, :] = tv_ref[...].astype(F32).reshape(HALF * PREV, HDIM).astype(BF16)

    done("load", 1)
    done("load", 2)
    done("recv", 0)
    for h in range(2):
        at = new_at + ROWS * h
        kall[at : at + ROWS, :] = qkv[h, :, HDIM : 2 * HDIM]
        vall[at : at + ROWS, :] = qkv[h, :, 2 * HDIM : 3 * HDIM]
    query = jnp.concatenate([qkv[0, :, 0:HDIM], qkv[1, :, 0:HDIM]], axis=0)
    parents = jnp.concatenate(
        [qkv[0, :, 3 * HDIM : 4 * HDIM], qkv[1, :, 3 * HDIM : 4 * HDIM]], axis=0
    )
    tokens = 2 * ROWS
    beam_row = iota((HDIM, tokens), 0)
    token_lane = iota((HDIM, tokens), 1)
    beam_of = HALF * ((token_lane // ROWS + half) % 2) + token_lane % HALF
    before = dot(parents, one_hot(beam_row == beam_of))
    step_row = (iota((tokens, tokens), 0) % ROWS) // HALF
    step_lane = (iota((tokens, tokens), 1) % ROWS) // HALF
    same = jnp.where(iota((tokens, tokens), 0) == iota((tokens, tokens), 1), 1.0, 0.0)
    back = jnp.where(step_lane + 1 == step_row, before, 0.0)
    back_bf = back.astype(BF16)
    near = (same + back).astype(BF16)
    back_two = dot(back_bf, back_bf)
    path = dot(near, (same + back_two).astype(BF16)).astype(BF16)
    first_row = iota((tokens, HDIM), 0) % ROWS
    first = jnp.where(first_row < HALF, parents.astype(F32), 0.0).astype(BF16)
    origin = dot(path, first).astype(BF16)
    tails = HALF * PREV
    tail_row = iota((HDIM, tails), 0)
    tail_lane = iota((HDIM, tails), 1)
    tail_on = dot(origin, one_hot(tail_row == HALF * half + tail_lane % HALF))
    new_on = jnp.where(iota((tokens, tokens), 0) < ROWS, path.astype(F32), 0.0)

    done("load", 9)
    score_scale = HDIM ** (-0.5)
    scores = dot_t(query, kall[...]) * score_scale
    prompt_live = iota((tokens, cap), 1) < parts_ref[0]
    prompt_s = jnp.where(prompt_live, scores[:, 0:cap], NEGATIVE)
    tail_s = jnp.where(tail_on > 0.5, scores[:, tail_at:new_at], NEGATIVE)
    new_s = jnp.where(new_on > 0.5, scores[:, new_at:total], NEGATIVE)
    top = jnp.maximum(
        jnp.maximum(
            jnp.max(prompt_s, axis=1, keepdims=True), jnp.max(tail_s, axis=1, keepdims=True)
        ),
        jnp.max(new_s, axis=1, keepdims=True),
    )
    prompt_w = jnp.exp(prompt_s - top)
    tail_w = jnp.exp(tail_s - top)
    new_w = jnp.exp(new_s - top)
    weight_sum = (
        jnp.sum(prompt_w, axis=1, keepdims=True)
        + jnp.sum(tail_w, axis=1, keepdims=True)
        + jnp.sum(new_w, axis=1, keepdims=True)
    )

    def weighted(weights, values):
        high, low = split_high(weights)
        both = dot(jnp.concatenate([high, low], axis=0), values)
        return both[0:tokens] + both[tokens : 2 * tokens]

    mix = (
        weighted(prompt_w, vall[0:cap, :])
        + weighted(tail_w, vall[tail_at:new_at, :])
        + weighted(new_w, vall[new_at:total, :])
    )
    lane = iota((ROWS, HDIM), 1)
    for h in (1, 0):
        rows = slice(ROWS * h, ROWS * (h + 1))
        part_send[h, :, 0:HDIM] = mix[rows]
        part_send[h, :, HDIM : 2 * HDIM] = jnp.where(
            lane < HDIM // 2, top[rows], weight_sum[rows]
        )
        if h == 1:
            send(part_send.at[1], part_recv.at[2], 5, grp=partner, exp=sibling)
            send(part_send.at[1], part_recv.at[0], 14, grp=partner)
    send(part_send.at[0], part_recv.at[1], 15, exp=sibling)

    width = groups * SEND
    routes = rts[...]
    hit = jnp.zeros((ROWS, experts), jnp.bool_)
    expert_lane = iota((ROWS, experts), 1)
    for k in range(topk):
        hit = hit | (routes[:, k : k + 1] == expert_lane)
    hits = one_hot(hit)
    rank = dot(one_hot(iota((ROWS, ROWS), 1) < iota((ROWS, ROWS), 0)), hits)
    spread_row = iota((experts, 2 * width), 0)
    spread_lane = iota((experts, 2 * width), 1)
    spread = one_hot(
        spread_row == 2 * (spread_lane % width // SEND) + spread_lane // width
    )
    hit_wide = dot(hits, spread)
    rank_wide = dot(rank.astype(BF16), spread)
    slot_lane = (iota((ROWS, 2 * width), 1) % SEND).astype(F32)
    place = jnp.where((rank_wide == slot_lane) & (hit_wide > 0.5), 1.0, 0.0)
    own_place = jnp.where(c == 0, place[:, 0:width], place[:, width : 2 * width])

    def joined(near_mix, near_tail, far_mix, far_tail):
        near_top, near_sum = near_tail[:, 0:1], near_tail[:, HDIM // 2 : HDIM // 2 + 1]
        far_top, far_sum = far_tail[:, 0:1], far_tail[:, HDIM // 2 : HDIM // 2 + 1]
        best = jnp.maximum(near_top, far_top)
        near_factor = jnp.exp(near_top - best)
        far_factor = jnp.exp(far_top - best)
        return (
            (near_mix * near_factor + far_mix * far_factor)
            / (near_sum * near_factor + far_sum * far_factor)
        ).astype(BF16)

    def halves(ref, index):
        return ref[index, :, 0:HDIM], ref[index, :, HDIM : 2 * HDIM]

    done("recv", 15)
    done("recv", 14)
    own_head = joined(*halves(part_send, 0), *halves(part_recv, 0))
    done("recv", 5)
    other_head = joined(*halves(part_recv, 1), *halves(part_recv, 2))
    attention = jnp.concatenate([own_head, other_head], axis=1)
    done("load", 3)
    done("recv", 6)

    chip = 2 * HDIM

    def features(at):
        return pl.ds(pl.multiple_of(at * chip, chip), chip)

    for k in chip_order:
        at = other_chip(k)
        proj_send[pl.ds(at, 1)] = (
            dot(attention, wout[:, features(at)]).astype(BF16).reshape(1, ROWS, chip)
        )
        remote(proj_send.at[at], proj_recv.at[y], 16, exp=2 * at + c).start()
    track(chips - 1, proj_recv, 16)
    residual = xs[:, features(y)] + dot(attention, wout[:, features(y)])
    proj_recv[pl.ds(y, 1)] = jnp.zeros((1, ROWS, chip), BF16)
    done("recv", 16)
    residual = residual + jnp.sum(proj_recv[...].astype(F32), axis=0)

    rows_bf = residual.astype(BF16)
    outgoing = lax.dot_general(
        own_place.astype(BF16), rows_bf, (((0,), (0,)), ((), ())), preferred_element_type=F32
    )
    disp_send[...] = outgoing.reshape(groups, SEND, chip).astype(BF16)

    send_each(
        group_order,
        lambda k: remote(
            disp_send.at[other_group(k)], disp_recv.at[g], 7, grp=other_group(k)
        ),
        disp_recv,
        7,
    )
    disp_recv[pl.ds(g, 1)] = disp_send[pl.ds(g, 1)]

    done("load", 12)
    done("load", 13)
    done("recv", 1)
    done("recv", 2)
    gains = jnp.concatenate([gain[0], gain[1]], axis=1)
    scaled = (residual * gains).astype(BF16)
    logit_part = dot_t(scaled[:, 0:HDIM], wr[0]) + dot_t(scaled[:, HDIM:chip], wr[1])
    stat_send[:, 0:experts] = logit_part
    stat_send[:, experts:HDIM] = jnp.broadcast_to(
        jnp.sum(residual * residual, axis=1, keepdims=True), (ROWS, HDIM - experts)
    )

    send_each(
        chip_order,
        lambda k: remote(stat_send, stat_recv.at[y], 8, exp=2 * other_chip(k) + c),
        stat_recv,
        8,
    )
    stat_recv[pl.ds(y, 1)] = stat_send[...].reshape(1, ROWS, stat_send.shape[1])

    packed = chips * PADB
    pick_row = iota((packed, groups * SEND), 0)
    pick_lane = iota((packed, groups * SEND), 1)
    per = BLOCK // CAP_E
    own_dest = pick_row // PADB

    def picks(shift):
        index = pick_row % PADB - shift
        safe = jnp.maximum(index, 0)
        source = (own_dest * per + safe // CAP_E) * SEND + safe % CAP_E
        return one_hot((index >= 0) & (index < BLOCK) & (pick_lane == source))

    gate_pick = picks(0)
    up_pick = picks(PADB - BLOCK)
    done("recv", 7)
    arrived = disp_recv[...].astype(F32).reshape(groups * SEND, chip).astype(BF16)
    gate_rows = dot(gate_pick, arrived)
    up_rows = dot(up_pick, arrived)
    squares = dot_t(
        jnp.ones((8, chip), F32), gate_rows * gate_rows, precision=lax.Precision.HIGHEST
    )
    sq_send[...] = squares

    send_each(
        chip_order,
        lambda k: remote(sq_send, sq_recv.at[y], 9, exp=2 * other_chip(k) + c),
        sq_recv,
        9,
    )
    sq_recv[pl.ds(y, 1)] = squares.reshape(1, 8, packed)
    gate_in = (gate_rows * gains).astype(BF16)
    up_in = (up_rows * gains).astype(BF16)
    done("load", 4)
    done("recv", 3)
    def rows_of(offset):
        return other_chip(offset + chips)

    chunks = len(spans)
    for h in range(chunks):
        first, size = spans[h]
        gate = dot(gate_in, wgu[:, first : first + size]).reshape(chips, 2, 8, size)
        up = dot(up_in, wgu[:, ffe + first : ffe + first + size]).reshape(chips, 2, 8, size)
        gu_send[h][:, 0:8] = gate[:, 0].astype(BF16)
        gu_send[h][:, 8:16] = (gate[:, 1] + up[:, 0]).astype(BF16)
        gu_send[h][:, 16:24] = up[:, 1].astype(BF16)
        base = 17 + 14 * h
        to_chip(gu_send[h].at[rows_of(4)], gu_mid[h].at[2], base + 2, 2 - 4 * (h % 2))
        to_chip(gu_send[h].at[rows_of(3)], gu_mid[h].at[0], base, 1)
        to_chip(gu_send[h].at[rows_of(-3)], gu_mid[h].at[1], base + 1, -1)
    for h in range(chunks):
        base = 17 + 14 * h
        for i in range(3):
            done("recv", base + i)
        for i in range(2):
            direction = 1 - 2 * i
            passing = gu_send[h][pl.ds(rows_of(2 * direction), 1)][0].astype(F32)
            passing = passing + gu_mid[h][i].astype(F32)
            if i == h % 2:
                passing = passing + gu_mid[h][2].astype(F32)
            gu_pass[h][i] = passing.astype(BF16)
            to_chip(gu_pass[h].at[i], gu_recv[h].at[2 + i], base + 5 + i, 2 * direction)
        to_chip(gu_send[h].at[rows_of(1)], gu_recv[h].at[0], base + 3, 1)
        to_chip(gu_send[h].at[rows_of(-1)], gu_recv[h].at[1], base + 4, -1)

    done("recv", 8)
    stats = jnp.sum(stat_recv[...], axis=0)
    mean_square = stats[:, experts : experts + 1] / depth
    logits = stats[:, 0:experts] * lax.rsqrt(mean_square + EPSILON)
    picked_top = jnp.max(jnp.where(hit, logits, NEGATIVE), axis=1, keepdims=True)
    picked = jnp.where(hit, jnp.exp(jnp.minimum(logits - picked_top, 0.0)), 0.0)
    share = picked / jnp.sum(picked, axis=1, keepdims=True)
    share_high, share_low = split_high(share)
    shares = jnp.concatenate([share_high, share_low], axis=0)
    share_wide = dot(shares, spread)
    combine = jnp.concatenate(
        [
            (share_wide[0:ROWS] * place).astype(BF16),
            (share_wide[ROWS : 2 * ROWS] * place).astype(BF16),
        ],
        axis=0,
    )
    done("recv", 9)
    square_sums = jnp.sum(sq_recv[...], axis=0)[0:1, :]
    scale_row = iota((2 * BLOCK, packed), 0) % BLOCK
    scale_lane = iota((2 * BLOCK, packed), 1)
    own_square = jnp.sum(
        jnp.where(scale_lane == y * PADB + scale_row, square_sums, 0.0), axis=1, keepdims=True
    )
    scale = lax.rsqrt(own_square / depth + EPSILON)

    back_row = iota((groups * SEND, chips * BLOCK), 0)
    back_lane = iota((groups * SEND, chips * BLOCK), 1)
    back_rank = back_row % SEND
    back_source = (back_row // SEND) * CAP_E + back_rank
    back_pick = one_hot((back_rank < CAP_E) & (back_lane == back_source))

    def forward(h):
        base = 17 + 14 * h
        for i in range(2):
            direction = 1 - 2 * i
            done("recv", base + 7 + i)
            origin_chip = rows_of(-2 * direction)
            held = hid[h].at[origin_chip]
            if i == h % 2:
                to_chip(held, held, base + 13, 2 * direction)
            to_chip(held, held, base + 11 + i, direction)

    for h in range(chunks):
        first, size = spans[h]
        base = 17 + 14 * h
        for i in range(3, 7):
            done("recv", base + i)
        sums = gu_send[h][pl.ds(y, 1)][0].astype(F32)
        for i in range(4):
            sums = sums + gu_recv[h][i].astype(F32)
        gsum[:, 0:size] = sums * scale
        gates = gsum[0:BLOCK, 0:size]
        ups = gsum[BLOCK : 2 * BLOCK, 0:size]
        hidden = gates / (1.0 + jnp.exp(-gates)) * ups
        hid[h][pl.ds(y, 1)] = hidden.reshape(1, BLOCK // HALF, HALF, size).astype(BF16)
        offsets = (2, -2, 1, -1) if h < chunks - 1 else (2, -2, 1, -1, 3, -3, 4)
        for i, offset in sorted(enumerate(offsets), key=lambda k: -abs(k[1])):
            to_chip(hid[h].at[y], hid[h].at[y], base + 7 + i, offset)
        if h == chunks - 2:
            forward(0)
    for h in range(1, chunks - 1):
        forward(h)
    done("load", 5)
    done("recv", 4)
    result = jnp.zeros((chips * BLOCK, chip), F32)
    for h in range(chunks):
        first, size = spans[h]
        for i in range(9 if h < chunks - 1 else 7, 14):
            done("recv", 17 + 14 * h + i)
        rows = hid[h][...].astype(F32).reshape(chips * BLOCK, size).astype(BF16)
        result = result + dot_t(rows, wd[:, first : first + size])
    result = result.astype(BF16)
    outcome = dot(back_pick, result)
    for h in range(2):
        ret_send[h] = outcome[:, HDIM * h : HDIM * (h + 1)].reshape(groups, SEND, HDIM).astype(BF16)
    landing = c * groups + g
    for k in group_order:
        at = other_group(k)
        remote(ret_send.at[c, at], ret_recv.at[landing], 12, grp=at).start()
        remote(ret_send.at[1 - c, at], ret_recv.at[landing], 12, grp=at, exp=sibling).start()
    remote(ret_send.at[1 - c, g], ret_recv.at[landing], 12, exp=sibling).start()
    track(2 * groups - 1, ret_recv, 12)
    ret_recv[pl.ds(landing, 1)] = ret_send[c, pl.ds(g, 1)]
    own = jnp.where(c == 0, residual[:, 0:HDIM], residual[:, HDIM:chip])
    done("recv", 12)
    returned = ret_recv[...].astype(F32).reshape(2 * groups * SEND, HDIM).astype(BF16)
    both = dot(combine, returned)
    out_ref[0] = (
        (own + both[0:ROWS] + both[ROWS : 2 * ROWS]).reshape(STEPS, HALF, HDIM).astype(BF16)
    )

    finish()


def on_device(
    step_inputs,
    parents,
    routes,
    w_qkv,
    w_out,
    prompt_keys,
    prompt_values,
    prompt_parts,
    tail_keys,
    tail_values,
    w_router,
    norm_gain,
    w_gate_up,
    w_down,
):
    groups = lax.axis_size("grp")
    columns = lax.axis_size("exp")
    chips = columns // 2
    depth = step_inputs.shape[3]
    cap = prompt_keys.shape[1]
    ffe = w_down.shape[2]
    experts = w_router.shape[1]
    topk = routes.shape[3]
    chip = 2 * HDIM
    spans = column_spans(ffe)
    keys = cap + HALF * PREV + 2 * ROWS
    vmem = pl.BlockSpec(memory_space=pltpu.VMEM)
    out = pl.pallas_call(
        functools.partial(kernel, groups, columns, topk),
        out_shape=jax.ShapeDtypeStruct((1, STEPS, HALF, HDIM), BF16),
        in_specs=[
            pl.BlockSpec(memory_space=pltpu.HBM)
        ]
        * 14,
        out_specs=vmem,
        scratch_shapes=[
            pltpu.VMEM((STEPS, HALF, depth), BF16),
            pltpu.SMEM((1, STEPS, HALF), jnp.int32),
            pltpu.VMEM((STEPS, HALF, topk), jnp.int32),
            pltpu.SMEM((1,), jnp.int32),
            pltpu.VMEM((PREV, HALF, HDIM), BF16),
            pltpu.VMEM((PREV, HALF, HDIM), BF16),
            pltpu.VMEM((ROWS, depth), F32),
            pltpu.VMEM((ROWS, HDIM), jnp.int32),
            pltpu.VMEM((2, 1, HDIM), F32),
            pltpu.VMEM((2, experts, HDIM), BF16),
            pltpu.VMEM((depth, 3 * HDIM), BF16),
            pltpu.VMEM((chip, depth), BF16),
            pltpu.VMEM((keys, HDIM), BF16),
            pltpu.VMEM((keys, HDIM), BF16),
            pltpu.VMEM((chip, 2 * ffe), BF16),
            pltpu.VMEM((chip, ffe), BF16),
            pltpu.VMEM((2, ROWS, 4 * HDIM), BF16),
            pltpu.VMEM((2, ROWS, chip), F32),
            pltpu.VMEM((3, ROWS, chip), F32),
            pltpu.VMEM((chips, ROWS, chip), BF16),
            pltpu.VMEM((chips, ROWS, chip), BF16),
            pltpu.VMEM((ROWS, HDIM), F32),
            pltpu.VMEM((chips, ROWS, HDIM), F32),
            pltpu.VMEM((groups, SEND, chip), BF16),
            pltpu.VMEM((groups, SEND, chip), BF16),
            pltpu.VMEM((8, chips * PADB), F32),
            pltpu.VMEM((chips, 8, chips * PADB), F32),
            [pltpu.VMEM((chips, 2 * BLOCK, size), BF16) for _, size in spans],
            [pltpu.VMEM((3, 2 * BLOCK, size), BF16) for _, size in spans],
            [pltpu.VMEM((2, 2 * BLOCK, size), BF16) for _, size in spans],
            [pltpu.VMEM((4, 2 * BLOCK, size), BF16) for _, size in spans],
            pltpu.VMEM((2 * BLOCK, spans[0][1]), F32),
            [pltpu.VMEM((chips, BLOCK // HALF, HALF, size), BF16) for _, size in spans],
            pltpu.VMEM((2, groups, SEND, HDIM), BF16),
            pltpu.VMEM((2 * groups, SEND, HDIM), BF16),
            pltpu.SemaphoreType.DMA((16,)),
            pltpu.SemaphoreType.DMA((17 + 14 * len(spans),)),
            pltpu.SemaphoreType.DMA((17 + 14 * len(spans),)),
        ],
        compiler_params=pltpu.CompilerParams(
            collective_id=0, has_side_effects=True, vmem_limit_bytes=64 * 1024 * 1024
        ),
        name="layer",
    )(
        step_inputs,
        parents,
        routes,
        prompt_parts,
        norm_gain.reshape(1, HDIM),
        w_router.T,
        jnp.transpose(w_qkv, (1, 0, 2)),
        w_out,
        prompt_keys,
        prompt_values,
        jnp.transpose(tail_keys, (0, 2, 1, 3)),
        jnp.transpose(tail_values, (0, 2, 1, 3)),
        w_gate_up,
        w_down,
    )
    return out


def solution(mesh):
    placed = (
        P("grp", None, None, None),
        P("grp", None, None),
        P("grp", None, None, None),
        P(None, None, "exp"),
        P("exp", None),
        P("grp", None, "exp"),
        P("grp", None, "exp"),
        P("grp"),
        P("grp", None, None, "exp"),
        P("grp", None, None, "exp"),
        P("exp", None),
        P("exp"),
        P("grp", "exp", None),
        P("grp", "exp", None),
    )
    return jax.shard_map(
        on_device,
        mesh=mesh,
        in_specs=placed,
        out_specs=P("grp", None, None, "exp"),
        check_vma=False,
    )
```

```python
import functools

import jax
import jax.numpy as jnp
from jax import lax
from jax.experimental import pallas as pl
from jax.experimental.pallas import tpu as pltpu
from jax.sharding import PartitionSpec as P

HDIM = 128
TOPK = 6
STEPS = 4
HALF = 4
ROWS = STEPS * HALF
CAP_E = 3
PREV = 60
SEND = 4
BLOCK = 12
PADB = 16

NEGATIVE = -1e30
EPSILON = 1e-06
F32 = jnp.float32
BF16 = jnp.bfloat16


def iota(shape, axis):
    return lax.broadcasted_iota(jnp.int32, shape, axis)


def dot(a, b, precision=None):
    return jnp.dot(a, b, preferred_element_type=F32, precision=precision)


def dot_t(a, b, precision=None):
    return lax.dot_general(
        a, b, (((1,), (1,)), ((), ())), preferred_element_type=F32, precision=precision
    )


def one_hot(cond):
    return jnp.where(cond, 1.0, 0.0).astype(BF16)


def split_high(value):
    high = value.astype(BF16)
    return high, (value - high.astype(F32)).astype(BF16)


def column_spans(ffe, chunks=3):
    tiles = ffe // HDIM
    sizes = [HDIM * (tiles // chunks + (h < tiles % chunks)) for h in range(chunks)]
    return [(sum(sizes[:h]), sizes[h]) for h in range(chunks)]


def kernel(
    groups,
    columns,
    topk,
    x_hbm,
    par_hbm,
    routes_hbm,
    parts_hbm,
    gain_hbm,
    wr_hbm,
    wqkv_hbm,
    wout_hbm,
    pk_hbm,
    pv_hbm,
    tk_hbm,
    tv_hbm,
    wgu_hbm,
    wd_hbm,
    out_ref,
    x_ref,
    par_ref,
    routes_ref,
    parts_ref,
    tk_ref,
    tv_ref,
    xs,
    rts,
    gain,
    wr,
    wqkv,
    wout,
    kall,
    vall,
    wgu,
    wd,
    qkv,
    part_send,
    part_recv,
    proj_send,
    proj_recv,
    stat_send,
    stat_recv,
    disp_send,
    disp_recv,
    sq_send,
    sq_recv,
    gu_send,
    gu_mid,
    gu_pass,
    gu_recv,
    gsum,
    hid,
    ret_send,
    ret_recv,
    local_sem,
    send_sem,
    recv_sem,
    rounds,
):
    chips = columns // 2
    ffe = wd.shape[1]
    spans = column_spans(ffe)
    cap = pk_hbm.shape[1]
    experts = wr.shape[1]
    depth = x_ref.shape[2]
    g = lax.axis_index("grp")
    e = lax.axis_index("exp")
    y = e // 2
    c = e % 2
    half = g % 2
    partner = g + 1 - 2 * half
    sibling = e + 1 - 2 * c
    own_rows = pl.ds(pl.multiple_of(c * HDIM, HDIM), HDIM)

    waits = {}

    def done(kind, index):
        waits.pop((kind, index))()

    def finish():
        for key in list(waits):
            done(*key)

    def local(src, dst, index):
        copy = pltpu.make_async_copy(src, dst, local_sem.at[index])
        copy.start()
        waits["load", index] = copy.wait

    def remote(src, dst, index, **where):
        return pltpu.make_async_remote_copy(
            src_ref=src,
            dst_ref=dst,
            send_sem=send_sem.at[index],
            recv_sem=recv_sem.at[index],
            device_id=where,
            device_id_type=pl.DeviceIdType.MESH,
        )

    def send(src, dst, index, **where):
        copy = remote(src, dst, index, **where)
        copy.start()
        waits["recv", index] = copy.wait_recv
        waits["send", index] = copy.wait_send

    def track(count, landing, index):
        whole = landing.at[pl.ds(0, count)]
        waits["recv", index] = pltpu.make_async_copy(whole, whole, recv_sem.at[index]).wait
        waits["send", index] = pltpu.make_async_copy(whole, whole, send_sem.at[index]).wait

    def send_each(order, one, landing, index):
        for k in order:
            one(k).start()
        track(len(order), landing, index)

    deep = 8
    wide_groups = groups // deep
    group_order = [(i, j) for i in range(wide_groups) for j in range(deep) if i or j]
    group_order.sort(key=lambda k: -min(k[0], wide_groups - k[0]) - min(k[1], deep - k[1]))
    chip_order = sorted(range(1, chips), key=lambda k: -min(k, chips - k))

    def other_group(k):
        return lax.rem(g // deep + k[0], wide_groups) * deep + lax.rem(g % deep + k[1], deep)

    def other_chip(k):
        return lax.rem(y + k, chips)

    def to_chip(src, dst, index, offset):
        send(src, dst, index, exp=2 * other_chip(offset + chips) + c)

    local(x_hbm.at[0], x_ref, 6)
    local(par_hbm, par_ref, 7)
    local(routes_hbm.at[0], routes_ref, 8)
    local(parts_hbm, parts_ref, 9)
    for i in range(3):
        local(wqkv_hbm.at[i], wqkv.at[:, pl.ds(HDIM * i, HDIM)], (0, 14, 15)[i])
    local(tk_hbm.at[0], tk_ref, 10)
    local(tv_hbm.at[0], tv_ref, 11)
    local(gain_hbm, gain.at[c], 12)
    local(wr_hbm, wr.at[c], 13)
    local(pk_hbm.at[0], kall.at[pl.ds(0, cap)], 1)
    local(pv_hbm.at[0], vall.at[pl.ds(0, cap)], 2)
    local(wout_hbm, wout.at[pl.ds(0, HDIM)], 3)
    local(wgu_hbm.at[c], wgu.at[own_rows], 4)
    local(wd_hbm.at[c], wd.at[own_rows], 5)

    barrier = pltpu.get_barrier_semaphore()

    def greet(semaphore, **where):
        pl.semaphore_signal(
            semaphore, inc=1, device_id=where, device_id_type=pl.DeviceIdType.MESH
        )

    def along_y(semaphore):
        for k in (1, chips - 1):
            greet(semaphore, exp=2 * other_chip(k) + c)

    def along_z(semaphore):
        for k in (1, deep - 1):
            greet(semaphore, grp=other_group((0, k)))

    def along_x(semaphore):
        for k in (1, wide_groups - 1):
            greet(semaphore, grp=other_group((k, 0)))

    along_x(barrier)
    along_y(barrier)
    along_z(barrier)
    greet(barrier, exp=sibling)
    greet(barrier, grp=partner, exp=sibling)

    def pass_word(index):
        along_y(rounds.at[index])
        along_z(rounds.at[3 + index])

    def hear_word(index):
        pl.semaphore_wait(rounds.at[index], 2)
        pl.semaphore_wait(rounds.at[3 + index], 2)

    done("load", 6)
    done("load", 8)
    done("load", 7)
    for s in range(STEPS):
        xs[HALF * s : HALF * (s + 1), :] = x_ref[s].astype(F32)
        rts[HALF * s : HALF * (s + 1), :topk] = routes_ref[s]
    x16 = xs[...].astype(BF16)
    row_sub = iota((ROWS, HDIM), 0)
    row_lane = iota((ROWS, HDIM), 1)
    parent_hot = jnp.zeros((ROWS, HDIM), F32)
    for s in range(STEPS):
        for b in range(HALF):
            parent_hot = jnp.where(
                (row_sub == HALF * s + b) & (row_lane == par_ref[0, s, b]), 1.0, parent_hot
            )
    done("load", 0)
    done("load", 14)
    done("load", 15)
    qkv[0, :, 0 : 3 * HDIM] = dot(x16, wqkv[...]).astype(BF16)
    qkv[0, :, 3 * HDIM : 4 * HDIM] = parent_hot.astype(BF16)

    pl.semaphore_wait(barrier, 8)
    pass_word(0)

    send(qkv.at[0], qkv.at[1], 0, grp=partner)
    send(wout_hbm, wout.at[pl.ds(HDIM, HDIM)], 6, exp=sibling)
    send(gain_hbm, gain.at[c], 1, exp=sibling)
    send(wr_hbm, wr.at[c], 2, exp=sibling)
    send(wgu_hbm.at[1 - c], wgu.at[own_rows], 3, exp=sibling)
    send(wd_hbm.at[1 - c], wd.at[own_rows], 4, exp=sibling)

    tail_at = cap
    new_at = cap + HALF * PREV
    total = new_at + 2 * ROWS
    done("load", 10)
    done("load", 11)
    kall[tail_at:new_at, :] = tk_ref[...].astype(F32).reshape(HALF * PREV, HDIM).astype(BF16)
    vall[tail_at:new_at, :] = tv_ref[...].astype(F32).reshape(HALF * PREV, HDIM).astype(BF16)

    done("load", 1)
    done("load", 2)
    hear_word(0)
    pass_word(1)
    done("recv", 0)
    for h in range(2):
        at = new_at + ROWS * h
        kall[at : at + ROWS, :] = qkv[h, :, HDIM : 2 * HDIM]
        vall[at : at + ROWS, :] = qkv[h, :, 2 * HDIM : 3 * HDIM]
    query = jnp.concatenate([qkv[0, :, 0:HDIM], qkv[1, :, 0:HDIM]], axis=0)
    parents = jnp.concatenate(
        [qkv[0, :, 3 * HDIM : 4 * HDIM], qkv[1, :, 3 * HDIM : 4 * HDIM]], axis=0
    )
    tokens = 2 * ROWS
    beam_row = iota((HDIM, tokens), 0)
    token_lane = iota((HDIM, tokens), 1)
    beam_of = HALF * ((token_lane // ROWS + half) % 2) + token_lane % HALF
    before = dot(parents, one_hot(beam_row == beam_of))
    step_row = (iota((tokens, tokens), 0) % ROWS) // HALF
    step_lane = (iota((tokens, tokens), 1) % ROWS) // HALF
    same = jnp.where(iota((tokens, tokens), 0) == iota((tokens, tokens), 1), 1.0, 0.0)
    back = jnp.where(step_lane + 1 == step_row, before, 0.0)
    back_bf = back.astype(BF16)
    near = (same + back).astype(BF16)
    back_two = dot(back_bf, back_bf)
    path = dot(near, (same + back_two).astype(BF16)).astype(BF16)
    first_row = iota((tokens, HDIM), 0) % ROWS
    first = jnp.where(first_row < HALF, parents.astype(F32), 0.0).astype(BF16)
    origin = dot(path, first).astype(BF16)
    tails = HALF * PREV
    tail_row = iota((HDIM, tails), 0)
    tail_lane = iota((HDIM, tails), 1)
    tail_on = dot(origin, one_hot(tail_row == HALF * half + tail_lane % HALF))
    new_on = jnp.where(iota((tokens, tokens), 0) < ROWS, path.astype(F32), 0.0)

    done("load", 9)
    score_scale = HDIM ** (-0.5)
    scores = dot_t(query, kall[...]) * score_scale
    prompt_live = iota((tokens, cap), 1) < parts_ref[0]
    prompt_s = jnp.where(prompt_live, scores[:, 0:cap], NEGATIVE)
    tail_s = jnp.where(tail_on > 0.5, scores[:, tail_at:new_at], NEGATIVE)
    new_s = jnp.where(new_on > 0.5, scores[:, new_at:total], NEGATIVE)
    top = jnp.maximum(
        jnp.maximum(
            jnp.max(prompt_s, axis=1, keepdims=True), jnp.max(tail_s, axis=1, keepdims=True)
        ),
        jnp.max(new_s, axis=1, keepdims=True),
    )
    prompt_w = jnp.exp(prompt_s - top)
    tail_w = jnp.exp(tail_s - top)
    new_w = jnp.exp(new_s - top)
    weight_sum = (
        jnp.sum(prompt_w, axis=1, keepdims=True)
        + jnp.sum(tail_w, axis=1, keepdims=True)
        + jnp.sum(new_w, axis=1, keepdims=True)
    )

    def weighted(weights, values):
        high, low = split_high(weights)
        both = dot(jnp.concatenate([high, low], axis=0), values)
        return both[0:tokens] + both[tokens : 2 * tokens]

    mix = (
        weighted(prompt_w, vall[0:cap, :])
        + weighted(tail_w, vall[tail_at:new_at, :])
        + weighted(new_w, vall[new_at:total, :])
    )
    lane = iota((ROWS, HDIM), 1)
    for h in (1, 0):
        rows = slice(ROWS * h, ROWS * (h + 1))
        part_send[h, :, 0:HDIM] = mix[rows]
        part_send[h, :, HDIM : 2 * HDIM] = jnp.where(
            lane < HDIM // 2, top[rows], weight_sum[rows]
        )
        if h == 1:
            send(part_send.at[1], part_recv.at[2], 5, grp=partner, exp=sibling)
            send(part_send.at[1], part_recv.at[0], 14, grp=partner)
    send(part_send.at[0], part_recv.at[1], 15, exp=sibling)
    hear_word(1)
    pass_word(2)

    width = groups * SEND
    routes = rts[...]
    hit = jnp.zeros((ROWS, experts), jnp.bool_)
    expert_lane = iota((ROWS, experts), 1)
    for k in range(topk):
        hit = hit | (routes[:, k : k + 1] == expert_lane)
    hits = one_hot(hit)
    rank = dot(one_hot(iota((ROWS, ROWS), 1) < iota((ROWS, ROWS), 0)), hits)
    spread_row = iota((experts, 2 * width), 0)
    spread_lane = iota((experts, 2 * width), 1)
    spread = one_hot(
        spread_row == 2 * (spread_lane % width // SEND) + spread_lane // width
    )
    hit_wide = dot(hits, spread)
    rank_wide = dot(rank.astype(BF16), spread)
    slot_lane = (iota((ROWS, 2 * width), 1) % SEND).astype(F32)
    place = jnp.where((rank_wide == slot_lane) & (hit_wide > 0.5), 1.0, 0.0)
    own_place = jnp.where(c == 0, place[:, 0:width], place[:, width : 2 * width])

    def joined(near_mix, near_tail, far_mix, far_tail):
        near_top, near_sum = near_tail[:, 0:1], near_tail[:, HDIM // 2 : HDIM // 2 + 1]
        far_top, far_sum = far_tail[:, 0:1], far_tail[:, HDIM // 2 : HDIM // 2 + 1]
        best = jnp.maximum(near_top, far_top)
        near_factor = jnp.exp(near_top - best)
        far_factor = jnp.exp(far_top - best)
        return (
            (near_mix * near_factor + far_mix * far_factor)
            / (near_sum * near_factor + far_sum * far_factor)
        ).astype(BF16)

    def halves(ref, index):
        return ref[index, :, 0:HDIM], ref[index, :, HDIM : 2 * HDIM]

    done("recv", 15)
    done("recv", 14)
    own_head = joined(*halves(part_send, 0), *halves(part_recv, 0))
    done("recv", 5)
    other_head = joined(*halves(part_recv, 1), *halves(part_recv, 2))
    attention = jnp.concatenate([own_head, other_head], axis=1)
    done("load", 3)
    done("recv", 6)
    hear_word(2)
    along_x(rounds.at[6])

    chip = 2 * HDIM

    def features(at):
        return pl.ds(pl.multiple_of(at * chip, chip), chip)

    for k in chip_order:
        at = other_chip(k)
        proj_send[pl.ds(at, 1)] = (
            dot(attention, wout[:, features(at)]).astype(BF16).reshape(1, ROWS, chip)
        )
        remote(proj_send.at[at], proj_recv.at[y], 16, exp=2 * at + c).start()
    track(chips - 1, proj_recv, 16)
    pl.semaphore_wait(rounds.at[6], 2)
    along_x(rounds.at[7])
    residual = xs[:, features(y)] + dot(attention, wout[:, features(y)])
    proj_recv[pl.ds(y, 1)] = jnp.zeros((1, ROWS, chip), BF16)
    done("recv", 16)
    pl.semaphore_wait(rounds.at[7], 2)
    residual = residual + jnp.sum(proj_recv[...].astype(F32), axis=0)

    rows_bf = residual.astype(BF16)
    outgoing = lax.dot_general(
        own_place.astype(BF16), rows_bf, (((0,), (0,)), ((), ())), preferred_element_type=F32
    )
    disp_send[...] = outgoing.reshape(groups, SEND, chip).astype(BF16)

    send_each(
        group_order,
        lambda k: remote(
            disp_send.at[other_group(k)], disp_recv.at[g], 7, grp=other_group(k)
        ),
        disp_recv,
        7,
    )
    disp_recv[pl.ds(g, 1)] = disp_send[pl.ds(g, 1)]
    greet(rounds.at[8], exp=sibling)

    done("load", 12)
    done("load", 13)
    done("recv", 1)
    done("recv", 2)
    gains = jnp.concatenate([gain[0], gain[1]], axis=1)
    scaled = (residual * gains).astype(BF16)
    logit_part = dot_t(scaled[:, 0:HDIM], wr[0]) + dot_t(scaled[:, HDIM:chip], wr[1])
    stat_send[:, 0:experts] = logit_part
    stat_send[:, experts:HDIM] = jnp.broadcast_to(
        jnp.sum(residual * residual, axis=1, keepdims=True), (ROWS, HDIM - experts)
    )

    send_each(
        chip_order,
        lambda k: remote(stat_send, stat_recv.at[y], 8, exp=2 * other_chip(k) + c),
        stat_recv,
        8,
    )
    stat_recv[pl.ds(y, 1)] = stat_send[...].reshape(1, ROWS, stat_send.shape[1])

    packed = chips * PADB
    pick_row = iota((packed, groups * SEND), 0)
    pick_lane = iota((packed, groups * SEND), 1)
    per = BLOCK // CAP_E
    own_dest = pick_row // PADB

    def picks(shift):
        index = pick_row % PADB - shift
        safe = jnp.maximum(index, 0)
        source = (own_dest * per + safe // CAP_E) * SEND + safe % CAP_E
        return one_hot((index >= 0) & (index < BLOCK) & (pick_lane == source))

    gate_pick = picks(0)
    up_pick = picks(PADB - BLOCK)
    done("recv", 7)
    arrived = disp_recv[...].astype(F32).reshape(groups * SEND, chip).astype(BF16)
    gate_rows = dot(gate_pick, arrived)
    up_rows = dot(up_pick, arrived)
    squares = dot_t(
        jnp.ones((8, chip), F32), gate_rows * gate_rows, precision=lax.Precision.HIGHEST
    )
    sq_send[...] = squares

    send_each(
        chip_order,
        lambda k: remote(sq_send, sq_recv.at[y], 9, exp=2 * other_chip(k) + c),
        sq_recv,
        9,
    )
    sq_recv[pl.ds(y, 1)] = squares.reshape(1, 8, packed)
    gate_in = (gate_rows * gains).astype(BF16)
    up_in = (up_rows * gains).astype(BF16)
    done("load", 4)
    done("recv", 3)
    def rows_of(offset):
        return other_chip(offset + chips)

    chunks = len(spans)
    for h in range(chunks):
        first, size = spans[h]
        gate = dot(gate_in, wgu[:, first : first + size]).reshape(chips, 2, 8, size)
        up = dot(up_in, wgu[:, ffe + first : ffe + first + size]).reshape(chips, 2, 8, size)
        gu_send[h][:, 0:8] = gate[:, 0].astype(BF16)
        gu_send[h][:, 8:16] = (gate[:, 1] + up[:, 0]).astype(BF16)
        gu_send[h][:, 16:24] = up[:, 1].astype(BF16)
        base = 17 + 14 * h
        to_chip(gu_send[h].at[rows_of(4)], gu_mid[h].at[2], base + 2, 2 - 4 * (h % 2))
        to_chip(gu_send[h].at[rows_of(3)], gu_mid[h].at[0], base, 1)
        to_chip(gu_send[h].at[rows_of(-3)], gu_mid[h].at[1], base + 1, -1)
    for h in range(chunks):
        base = 17 + 14 * h
        for i in range(3):
            done("recv", base + i)
        for i in range(2):
            direction = 1 - 2 * i
            passing = gu_send[h][pl.ds(rows_of(2 * direction), 1)][0].astype(F32)
            passing = passing + gu_mid[h][i].astype(F32)
            if i == h % 2:
                passing = passing + gu_mid[h][2].astype(F32)
            gu_pass[h][i] = passing.astype(BF16)
            to_chip(gu_pass[h].at[i], gu_recv[h].at[2 + i], base + 5 + i, 2 * direction)
        to_chip(gu_send[h].at[rows_of(1)], gu_recv[h].at[0], base + 3, 1)
        to_chip(gu_send[h].at[rows_of(-1)], gu_recv[h].at[1], base + 4, -1)

    done("recv", 8)
    stats = jnp.sum(stat_recv[...], axis=0)
    mean_square = stats[:, experts : experts + 1] / depth
    logits = stats[:, 0:experts] * lax.rsqrt(mean_square + EPSILON)
    picked_top = jnp.max(jnp.where(hit, logits, NEGATIVE), axis=1, keepdims=True)
    picked = jnp.where(hit, jnp.exp(jnp.minimum(logits - picked_top, 0.0)), 0.0)
    share = picked / jnp.sum(picked, axis=1, keepdims=True)
    share_high, share_low = split_high(share)
    shares = jnp.concatenate([share_high, share_low], axis=0)
    share_wide = dot(shares, spread)
    combine = jnp.concatenate(
        [
            (share_wide[0:ROWS] * place).astype(BF16),
            (share_wide[ROWS : 2 * ROWS] * place).astype(BF16),
        ],
        axis=0,
    )
    done("recv", 9)
    square_sums = jnp.sum(sq_recv[...], axis=0)[0:1, :]
    scale_row = iota((2 * BLOCK, packed), 0) % BLOCK
    scale_lane = iota((2 * BLOCK, packed), 1)
    own_square = jnp.sum(
        jnp.where(scale_lane == y * PADB + scale_row, square_sums, 0.0), axis=1, keepdims=True
    )
    scale = lax.rsqrt(own_square / depth + EPSILON)

    back_row = iota((groups * SEND, chips * BLOCK), 0)
    back_lane = iota((groups * SEND, chips * BLOCK), 1)
    back_rank = back_row % SEND
    back_source = (back_row // SEND) * CAP_E + back_rank
    back_pick = one_hot((back_rank < CAP_E) & (back_lane == back_source))

    for h in range(chunks):
        first, size = spans[h]
        base = 17 + 14 * h
        for i in range(3, 7):
            done("recv", base + i)
        sums = gu_send[h][pl.ds(y, 1)][0].astype(F32)
        for i in range(4):
            sums = sums + gu_recv[h][i].astype(F32)
        gsum[:, 0:size] = sums * scale
        gates = gsum[0:BLOCK, 0:size]
        ups = gsum[BLOCK : 2 * BLOCK, 0:size]
        hidden = gates / (1.0 + jnp.exp(-gates)) * ups
        hid[h][pl.ds(y, 1)] = hidden.reshape(1, BLOCK // HALF, HALF, size).astype(BF16)
        for i, offset in enumerate((4, 3, -3, 2, -2, 1, -1)):
            to_chip(hid[h].at[y], hid[h].at[y], base + 7 + i, offset)
    done("load", 5)
    done("recv", 4)
    result = jnp.zeros((chips * BLOCK, chip), F32)
    for h in range(chunks):
        first, size = spans[h]
        for i in range(7, 14):
            done("recv", 17 + 14 * h + i)
        rows = hid[h][...].astype(F32).reshape(chips * BLOCK, size).astype(BF16)
        result = result + dot_t(rows, wd[:, first : first + size])
    result = result.astype(BF16)
    outcome = dot(back_pick, result)
    for h in range(2):
        ret_send[h] = outcome[:, HDIM * h : HDIM * (h + 1)].reshape(groups, SEND, HDIM).astype(BF16)
    landing = c * groups + g
    pl.semaphore_wait(rounds.at[8], 1)
    for k in group_order:
        at = other_group(k)
        remote(ret_send.at[c, at], ret_recv.at[landing], 12, grp=at).start()
        remote(ret_send.at[1 - c, at], ret_recv.at[landing], 12, grp=at, exp=sibling).start()
    remote(ret_send.at[1 - c, g], ret_recv.at[landing], 12, exp=sibling).start()
    track(2 * groups - 1, ret_recv, 12)
    ret_recv[pl.ds(landing, 1)] = ret_send[c, pl.ds(g, 1)]
    own = jnp.where(c == 0, residual[:, 0:HDIM], residual[:, HDIM:chip])
    done("recv", 12)
    returned = ret_recv[...].astype(F32).reshape(2 * groups * SEND, HDIM).astype(BF16)
    both = dot(combine, returned)
    out_ref[0] = (
        (own + both[0:ROWS] + both[ROWS : 2 * ROWS]).reshape(STEPS, HALF, HDIM).astype(BF16)
    )

    finish()


def on_device(
    step_inputs,
    parents,
    routes,
    w_qkv,
    w_out,
    prompt_keys,
    prompt_values,
    prompt_parts,
    tail_keys,
    tail_values,
    w_router,
    norm_gain,
    w_gate_up,
    w_down,
):
    groups = lax.axis_size("grp")
    columns = lax.axis_size("exp")
    chips = columns // 2
    depth = step_inputs.shape[3]
    cap = prompt_keys.shape[1]
    ffe = w_down.shape[2]
    experts = w_router.shape[1]
    topk = routes.shape[3]
    chip = 2 * HDIM
    spans = column_spans(ffe)
    keys = cap + HALF * PREV + 2 * ROWS
    vmem = pl.BlockSpec(memory_space=pltpu.VMEM)
    out = pl.pallas_call(
        functools.partial(kernel, groups, columns, topk),
        out_shape=jax.ShapeDtypeStruct((1, STEPS, HALF, HDIM), BF16),
        in_specs=[
            pl.BlockSpec(memory_space=pltpu.HBM)
        ]
        * 14,
        out_specs=vmem,
        scratch_shapes=[
            pltpu.VMEM((STEPS, HALF, depth), BF16),
            pltpu.SMEM((1, STEPS, HALF), jnp.int32),
            pltpu.VMEM((STEPS, HALF, topk), jnp.int32),
            pltpu.SMEM((1,), jnp.int32),
            pltpu.VMEM((PREV, HALF, HDIM), BF16),
            pltpu.VMEM((PREV, HALF, HDIM), BF16),
            pltpu.VMEM((ROWS, depth), F32),
            pltpu.VMEM((ROWS, HDIM), jnp.int32),
            pltpu.VMEM((2, 1, HDIM), F32),
            pltpu.VMEM((2, experts, HDIM), BF16),
            pltpu.VMEM((depth, 3 * HDIM), BF16),
            pltpu.VMEM((chip, depth), BF16),
            pltpu.VMEM((keys, HDIM), BF16),
            pltpu.VMEM((keys, HDIM), BF16),
            pltpu.VMEM((chip, 2 * ffe), BF16),
            pltpu.VMEM((chip, ffe), BF16),
            pltpu.VMEM((2, ROWS, 4 * HDIM), BF16),
            pltpu.VMEM((2, ROWS, chip), F32),
            pltpu.VMEM((3, ROWS, chip), F32),
            pltpu.VMEM((chips, ROWS, chip), BF16),
            pltpu.VMEM((chips, ROWS, chip), BF16),
            pltpu.VMEM((ROWS, HDIM), F32),
            pltpu.VMEM((chips, ROWS, HDIM), F32),
            pltpu.VMEM((groups, SEND, chip), BF16),
            pltpu.VMEM((groups, SEND, chip), BF16),
            pltpu.VMEM((8, chips * PADB), F32),
            pltpu.VMEM((chips, 8, chips * PADB), F32),
            [pltpu.VMEM((chips, 2 * BLOCK, size), BF16) for _, size in spans],
            [pltpu.VMEM((3, 2 * BLOCK, size), BF16) for _, size in spans],
            [pltpu.VMEM((2, 2 * BLOCK, size), BF16) for _, size in spans],
            [pltpu.VMEM((4, 2 * BLOCK, size), BF16) for _, size in spans],
            pltpu.VMEM((2 * BLOCK, spans[0][1]), F32),
            [pltpu.VMEM((chips, BLOCK // HALF, HALF, size), BF16) for _, size in spans],
            pltpu.VMEM((2, groups, SEND, HDIM), BF16),
            pltpu.VMEM((2 * groups, SEND, HDIM), BF16),
            pltpu.SemaphoreType.DMA((16,)),
            pltpu.SemaphoreType.DMA((17 + 14 * len(spans),)),
            pltpu.SemaphoreType.DMA((17 + 14 * len(spans),)),
            pltpu.SemaphoreType.REGULAR((9,)),
        ],
        compiler_params=pltpu.CompilerParams(
            collective_id=0, has_side_effects=True, vmem_limit_bytes=64 * 1024 * 1024
        ),
        name="layer",
    )(
        step_inputs,
        parents,
        routes,
        prompt_parts,
        norm_gain.reshape(1, HDIM),
        w_router.T,
        jnp.transpose(w_qkv, (1, 0, 2)),
        w_out,
        prompt_keys,
        prompt_values,
        jnp.transpose(tail_keys, (0, 2, 1, 3)),
        jnp.transpose(tail_values, (0, 2, 1, 3)),
        w_gate_up,
        w_down,
    )
    return out


def solution(mesh):
    placed = (
        P("grp", None, None, None),
        P("grp", None, None),
        P("grp", None, None, None),
        P(None, None, "exp"),
        P("exp", None),
        P("grp", None, "exp"),
        P("grp", None, "exp"),
        P("grp"),
        P("grp", None, None, "exp"),
        P("grp", None, None, "exp"),
        P("exp", None),
        P("exp"),
        P("grp", "exp", None),
        P("grp", "exp", None),
    )
    return jax.shard_map(
        on_device,
        mesh=mesh,
        in_specs=placed,
        out_specs=P("grp", None, None, "exp"),
        check_vma=False,
    )
```

```python
import functools

import jax
import jax.numpy as jnp
from jax import lax
from jax.experimental import pallas as pl
from jax.experimental.pallas import tpu as pltpu
from jax.sharding import PartitionSpec as P

HDIM = 128
TOPK = 6
STEPS = 4
HALF = 4
ROWS = STEPS * HALF
CAP_E = 3
PREV = 60
SEND = 4
BLOCK = 12
PADB = 16

NEGATIVE = -1e30
EPSILON = 1e-06
F32 = jnp.float32
BF16 = jnp.bfloat16


def iota(shape, axis):
    return lax.broadcasted_iota(jnp.int32, shape, axis)


def dot(a, b, precision=None):
    return jnp.dot(a, b, preferred_element_type=F32, precision=precision)


def dot_t(a, b, precision=None):
    return lax.dot_general(
        a, b, (((1,), (1,)), ((), ())), preferred_element_type=F32, precision=precision
    )


def one_hot(cond):
    return jnp.where(cond, 1.0, 0.0).astype(BF16)


def split_high(value):
    high = value.astype(BF16)
    return high, (value - high.astype(F32)).astype(BF16)


def column_spans(ffe, chunks=3):
    tiles = ffe // HDIM
    sizes = [HDIM * (tiles // chunks + (h < tiles % chunks)) for h in range(chunks)]
    return [(sum(sizes[:h]), sizes[h]) for h in range(chunks)]


def kernel(
    groups,
    columns,
    topk,
    x_hbm,
    par_hbm,
    routes_hbm,
    parts_hbm,
    gain_hbm,
    wr_hbm,
    wqkv_hbm,
    wout_hbm,
    pk_hbm,
    pv_hbm,
    tk_hbm,
    tv_hbm,
    wgu_hbm,
    wd_hbm,
    out_ref,
    x_ref,
    par_ref,
    routes_ref,
    parts_ref,
    tk_ref,
    tv_ref,
    xs,
    rts,
    gain,
    wr,
    wqkv,
    wout,
    kall,
    vall,
    wgu,
    wd,
    qkv,
    part_send,
    part_recv,
    proj_send,
    proj_recv,
    stat_send,
    stat_recv,
    disp_send,
    disp_recv,
    sq_send,
    sq_recv,
    gu_send,
    gu_mid,
    gu_pass,
    gu_recv,
    gsum,
    hid,
    ret_send,
    ret_recv,
    local_sem,
    send_sem,
    recv_sem,
    rounds,
):
    chips = columns // 2
    ffe = wd.shape[1]
    spans = column_spans(ffe)
    cap = pk_hbm.shape[1]
    experts = wr.shape[1]
    depth = x_ref.shape[2]
    g = lax.axis_index("grp")
    e = lax.axis_index("exp")
    y = e // 2
    c = e % 2
    half = g % 2
    partner = g + 1 - 2 * half
    sibling = e + 1 - 2 * c
    own_rows = pl.ds(pl.multiple_of(c * HDIM, HDIM), HDIM)

    waits = {}

    def done(kind, index):
        waits.pop((kind, index))()

    def finish():
        for key in list(waits):
            done(*key)

    def local(src, dst, index):
        copy = pltpu.make_async_copy(src, dst, local_sem.at[index])
        copy.start()
        waits["load", index] = copy.wait

    def remote(src, dst, index, **where):
        return pltpu.make_async_remote_copy(
            src_ref=src,
            dst_ref=dst,
            send_sem=send_sem.at[index],
            recv_sem=recv_sem.at[index],
            device_id=where,
            device_id_type=pl.DeviceIdType.MESH,
        )

    def send(src, dst, index, **where):
        copy = remote(src, dst, index, **where)
        copy.start()
        waits["recv", index] = copy.wait_recv
        waits["send", index] = copy.wait_send

    def track(count, landing, index):
        whole = landing.at[pl.ds(0, count)]
        waits["recv", index] = pltpu.make_async_copy(whole, whole, recv_sem.at[index]).wait
        waits["send", index] = pltpu.make_async_copy(whole, whole, send_sem.at[index]).wait

    def send_each(order, one, landing, index):
        for k in order:
            one(k).start()
        track(len(order), landing, index)

    deep = 8
    wide_groups = groups // deep
    group_order = [(i, j) for i in range(wide_groups) for j in range(deep) if i or j]
    group_order.sort(key=lambda k: -min(k[0], wide_groups - k[0]) - min(k[1], deep - k[1]))
    chip_order = sorted(range(1, chips), key=lambda k: -min(k, chips - k))

    def other_group(k):
        return lax.rem(g // deep + k[0], wide_groups) * deep + lax.rem(g % deep + k[1], deep)

    def other_chip(k):
        return lax.rem(y + k, chips)

    def to_chip(src, dst, index, offset):
        send(src, dst, index, exp=2 * other_chip(offset + chips) + c)

    local(x_hbm.at[0], x_ref, 6)
    local(par_hbm, par_ref, 7)
    local(routes_hbm.at[0], routes_ref, 8)
    local(parts_hbm, parts_ref, 9)
    for i in range(3):
        local(wqkv_hbm.at[i], wqkv.at[:, pl.ds(HDIM * i, HDIM)], (0, 14, 15)[i])
    local(tk_hbm.at[0], tk_ref, 10)
    local(tv_hbm.at[0], tv_ref, 11)
    local(gain_hbm, gain.at[c], 12)
    local(wr_hbm, wr.at[c], 13)
    local(pk_hbm.at[0], kall.at[pl.ds(0, cap)], 1)
    local(pv_hbm.at[0], vall.at[pl.ds(0, cap)], 2)
    local(wout_hbm, wout.at[pl.ds(0, HDIM)], 3)
    local(wgu_hbm.at[c], wgu.at[own_rows], 4)
    local(wd_hbm.at[c], wd.at[own_rows], 5)

    barrier = pltpu.get_barrier_semaphore()

    def greet(semaphore, **where):
        pl.semaphore_signal(
            semaphore, inc=1, device_id=where, device_id_type=pl.DeviceIdType.MESH
        )

    def along_y(semaphore):
        for k in (1, chips - 1):
            greet(semaphore, exp=2 * other_chip(k) + c)

    def along_z(semaphore):
        for k in (1, deep - 1):
            greet(semaphore, grp=other_group((0, k)))

    def along_x(semaphore):
        for k in (1, wide_groups - 1):
            greet(semaphore, grp=other_group((k, 0)))

    along_x(barrier)
    along_y(barrier)
    along_z(barrier)
    greet(barrier, exp=sibling)
    greet(barrier, grp=partner, exp=sibling)

    def pass_word(index):
        along_y(rounds.at[index])
        along_z(rounds.at[3 + index])

    def hear_word(index):
        pl.semaphore_wait(rounds.at[index], 2)
        pl.semaphore_wait(rounds.at[3 + index], 2)

    done("load", 6)
    done("load", 8)
    done("load", 7)
    for s in range(STEPS):
        xs[HALF * s : HALF * (s + 1), :] = x_ref[s].astype(F32)
        rts[HALF * s : HALF * (s + 1), :topk] = routes_ref[s]
    x16 = xs[...].astype(BF16)
    row_sub = iota((ROWS, HDIM), 0)
    row_lane = iota((ROWS, HDIM), 1)
    parent_hot = jnp.zeros((ROWS, HDIM), F32)
    for s in range(STEPS):
        for b in range(HALF):
            parent_hot = jnp.where(
                (row_sub == HALF * s + b) & (row_lane == par_ref[0, s, b]), 1.0, parent_hot
            )
    done("load", 0)
    done("load", 14)
    done("load", 15)
    qkv[0, :, 0 : 3 * HDIM] = dot(x16, wqkv[...]).astype(BF16)
    qkv[0, :, 3 * HDIM : 4 * HDIM] = parent_hot.astype(BF16)

    pl.semaphore_wait(barrier, 8)
    pass_word(0)

    send(qkv.at[0], qkv.at[1], 0, grp=partner)
    send(wout_hbm, wout.at[pl.ds(HDIM, HDIM)], 6, exp=sibling)
    send(gain_hbm, gain.at[c], 1, exp=sibling)
    send(wr_hbm, wr.at[c], 2, exp=sibling)
    send(wgu_hbm.at[1 - c], wgu.at[own_rows], 3, exp=sibling)
    send(wd_hbm.at[1 - c], wd.at[own_rows], 4, exp=sibling)

    tail_at = cap
    new_at = cap + HALF * PREV
    total = new_at + 2 * ROWS
    done("load", 10)
    done("load", 11)
    kall[tail_at:new_at, :] = tk_ref[...].astype(F32).reshape(HALF * PREV, HDIM).astype(BF16)
    vall[tail_at:new_at, :] = tv_ref[...].astype(F32).reshape(HALF * PREV, HDIM).astype(BF16)

    done("load", 1)
    done("load", 2)
    hear_word(0)
    pass_word(1)
    done("recv", 0)
    for h in range(2):
        at = new_at + ROWS * h
        kall[at : at + ROWS, :] = qkv[h, :, HDIM : 2 * HDIM]
        vall[at : at + ROWS, :] = qkv[h, :, 2 * HDIM : 3 * HDIM]
    query = jnp.concatenate([qkv[0, :, 0:HDIM], qkv[1, :, 0:HDIM]], axis=0)
    parents = jnp.concatenate(
        [qkv[0, :, 3 * HDIM : 4 * HDIM], qkv[1, :, 3 * HDIM : 4 * HDIM]], axis=0
    )
    tokens = 2 * ROWS
    beam_row = iota((HDIM, tokens), 0)
    token_lane = iota((HDIM, tokens), 1)
    beam_of = HALF * ((token_lane // ROWS + half) % 2) + token_lane % HALF
    before = dot(parents, one_hot(beam_row == beam_of))
    step_row = (iota((tokens, tokens), 0) % ROWS) // HALF
    step_lane = (iota((tokens, tokens), 1) % ROWS) // HALF
    same = jnp.where(iota((tokens, tokens), 0) == iota((tokens, tokens), 1), 1.0, 0.0)
    back = jnp.where(step_lane + 1 == step_row, before, 0.0)
    back_bf = back.astype(BF16)
    near = (same + back).astype(BF16)
    back_two = dot(back_bf, back_bf)
    path = dot(near, (same + back_two).astype(BF16)).astype(BF16)
    first_row = iota((tokens, HDIM), 0) % ROWS
    first = jnp.where(first_row < HALF, parents.astype(F32), 0.0).astype(BF16)
    origin = dot(path, first).astype(BF16)
    tails = HALF * PREV
    tail_row = iota((HDIM, tails), 0)
    tail_lane = iota((HDIM, tails), 1)
    tail_on = dot(origin, one_hot(tail_row == HALF * half + tail_lane % HALF))
    new_on = jnp.where(iota((tokens, tokens), 0) < ROWS, path.astype(F32), 0.0)

    done("load", 9)
    score_scale = HDIM ** (-0.5)
    scores = dot_t(query, kall[...]) * score_scale
    prompt_live = iota((tokens, cap), 1) < parts_ref[0]
    prompt_s = jnp.where(prompt_live, scores[:, 0:cap], NEGATIVE)
    tail_s = jnp.where(tail_on > 0.5, scores[:, tail_at:new_at], NEGATIVE)
    new_s = jnp.where(new_on > 0.5, scores[:, new_at:total], NEGATIVE)
    top = jnp.maximum(
        jnp.maximum(
            jnp.max(prompt_s, axis=1, keepdims=True), jnp.max(tail_s, axis=1, keepdims=True)
        ),
        jnp.max(new_s, axis=1, keepdims=True),
    )
    prompt_w = jnp.exp(prompt_s - top)
    tail_w = jnp.exp(tail_s - top)
    new_w = jnp.exp(new_s - top)
    weight_sum = (
        jnp.sum(prompt_w, axis=1, keepdims=True)
        + jnp.sum(tail_w, axis=1, keepdims=True)
        + jnp.sum(new_w, axis=1, keepdims=True)
    )

    def weighted(weights, values):
        high, low = split_high(weights)
        both = dot(jnp.concatenate([high, low], axis=0), values)
        return both[0:tokens] + both[tokens : 2 * tokens]

    mix = (
        weighted(prompt_w, vall[0:cap, :])
        + weighted(tail_w, vall[tail_at:new_at, :])
        + weighted(new_w, vall[new_at:total, :])
    )
    lane = iota((ROWS, HDIM), 1)
    for h in (1, 0):
        rows = slice(ROWS * h, ROWS * (h + 1))
        part_send[h, :, 0:HDIM] = mix[rows]
        part_send[h, :, HDIM : 2 * HDIM] = jnp.where(
            lane < HDIM // 2, top[rows], weight_sum[rows]
        )
        if h == 1:
            send(part_send.at[1], part_recv.at[2], 5, grp=partner, exp=sibling)
            send(part_send.at[1], part_recv.at[0], 14, grp=partner)
    send(part_send.at[0], part_recv.at[1], 15, exp=sibling)
    hear_word(1)
    pass_word(2)

    width = groups * SEND
    routes = rts[...]
    hit = jnp.zeros((ROWS, experts), jnp.bool_)
    expert_lane = iota((ROWS, experts), 1)
    for k in range(topk):
        hit = hit | (routes[:, k : k + 1] == expert_lane)
    hits = one_hot(hit)
    rank = dot(one_hot(iota((ROWS, ROWS), 1) < iota((ROWS, ROWS), 0)), hits)
    spread_row = iota((experts, 2 * width), 0)
    spread_lane = iota((experts, 2 * width), 1)
    spread = one_hot(
        spread_row == 2 * (spread_lane % width // SEND) + spread_lane // width
    )
    hit_wide = dot(hits, spread)
    rank_wide = dot(rank.astype(BF16), spread)
    slot_lane = (iota((ROWS, 2 * width), 1) % SEND).astype(F32)
    place = jnp.where((rank_wide == slot_lane) & (hit_wide > 0.5), 1.0, 0.0)
    own_place = jnp.where(c == 0, place[:, 0:width], place[:, width : 2 * width])

    def joined(near_mix, near_tail, far_mix, far_tail):
        near_top, near_sum = near_tail[:, 0:1], near_tail[:, HDIM // 2 : HDIM // 2 + 1]
        far_top, far_sum = far_tail[:, 0:1], far_tail[:, HDIM // 2 : HDIM // 2 + 1]
        best = jnp.maximum(near_top, far_top)
        near_factor = jnp.exp(near_top - best)
        far_factor = jnp.exp(far_top - best)
        return (
            (near_mix * near_factor + far_mix * far_factor)
            / (near_sum * near_factor + far_sum * far_factor)
        ).astype(BF16)

    def halves(ref, index):
        return ref[index, :, 0:HDIM], ref[index, :, HDIM : 2 * HDIM]

    done("recv", 15)
    done("recv", 14)
    own_head = joined(*halves(part_send, 0), *halves(part_recv, 0))
    done("recv", 5)
    other_head = joined(*halves(part_recv, 1), *halves(part_recv, 2))
    attention = jnp.concatenate([own_head, other_head], axis=1)
    done("load", 3)
    done("recv", 6)
    hear_word(2)
    along_x(rounds.at[6])

    chip = 2 * HDIM

    def features(at):
        return pl.ds(pl.multiple_of(at * chip, chip), chip)

    for k in chip_order:
        at = other_chip(k)
        proj_send[pl.ds(at, 1)] = (
            dot(attention, wout[:, features(at)]).astype(BF16).reshape(1, ROWS, chip)
        )
        remote(proj_send.at[at], proj_recv.at[y], 16, exp=2 * at + c).start()
    track(chips - 1, proj_recv, 16)
    pl.semaphore_wait(rounds.at[6], 2)
    along_x(rounds.at[7])
    residual = xs[:, features(y)] + dot(attention, wout[:, features(y)])
    proj_recv[pl.ds(y, 1)] = jnp.zeros((1, ROWS, chip), BF16)
    done("recv", 16)
    pl.semaphore_wait(rounds.at[7], 2)
    residual = residual + jnp.sum(proj_recv[...].astype(F32), axis=0)

    rows_bf = residual.astype(BF16)
    outgoing = lax.dot_general(
        own_place.astype(BF16), rows_bf, (((0,), (0,)), ((), ())), preferred_element_type=F32
    )
    disp_send[...] = outgoing.reshape(groups, SEND, chip).astype(BF16)

    send_each(
        group_order,
        lambda k: remote(
            disp_send.at[other_group(k)], disp_recv.at[g], 7, grp=other_group(k)
        ),
        disp_recv,
        7,
    )
    disp_recv[pl.ds(g, 1)] = disp_send[pl.ds(g, 1)]
    greet(rounds.at[8], exp=sibling)

    done("load", 12)
    done("load", 13)
    done("recv", 1)
    done("recv", 2)
    gains = jnp.concatenate([gain[0], gain[1]], axis=1)
    scaled = (residual * gains).astype(BF16)
    logit_part = dot_t(scaled[:, 0:HDIM], wr[0]) + dot_t(scaled[:, HDIM:chip], wr[1])
    stat_send[:, 0:experts] = logit_part
    stat_send[:, experts:HDIM] = jnp.broadcast_to(
        jnp.sum(residual * residual, axis=1, keepdims=True), (ROWS, HDIM - experts)
    )

    send_each(
        chip_order,
        lambda k: remote(stat_send, stat_recv.at[y], 8, exp=2 * other_chip(k) + c),
        stat_recv,
        8,
    )
    stat_recv[pl.ds(y, 1)] = stat_send[...].reshape(1, ROWS, stat_send.shape[1])

    packed = chips * PADB
    pick_row = iota((packed, groups * SEND), 0)
    pick_lane = iota((packed, groups * SEND), 1)
    per = BLOCK // CAP_E
    own_dest = pick_row // PADB

    def picks(shift):
        index = pick_row % PADB - shift
        safe = jnp.maximum(index, 0)
        source = (own_dest * per + safe // CAP_E) * SEND + safe % CAP_E
        return one_hot((index >= 0) & (index < BLOCK) & (pick_lane == source))

    gate_pick = picks(0)
    up_pick = picks(PADB - BLOCK)
    done("recv", 7)
    arrived = disp_recv[...].astype(F32).reshape(groups * SEND, chip).astype(BF16)
    gate_rows = dot(gate_pick, arrived)
    up_rows = dot(up_pick, arrived)
    squares = dot_t(
        jnp.ones((8, chip), F32), gate_rows * gate_rows, precision=lax.Precision.HIGHEST
    )
    sq_send[...] = squares

    send_each(
        chip_order,
        lambda k: remote(sq_send, sq_recv.at[y], 9, exp=2 * other_chip(k) + c),
        sq_recv,
        9,
    )
    sq_recv[pl.ds(y, 1)] = squares.reshape(1, 8, packed)
    gate_in = (gate_rows * gains).astype(BF16)
    up_in = (up_rows * gains).astype(BF16)
    done("load", 4)
    done("recv", 3)
    def rows_of(offset):
        return other_chip(offset + chips)

    chunks = len(spans)
    for h in range(chunks):
        first, size = spans[h]
        gate = dot(gate_in, wgu[:, first : first + size]).reshape(chips, 2, 8, size)
        up = dot(up_in, wgu[:, ffe + first : ffe + first + size]).reshape(chips, 2, 8, size)
        gu_send[h][:, 0:8] = gate[:, 0].astype(BF16)
        gu_send[h][:, 8:16] = (gate[:, 1] + up[:, 0]).astype(BF16)
        gu_send[h][:, 16:24] = up[:, 1].astype(BF16)
        base = 17 + 14 * h
        to_chip(gu_send[h].at[rows_of(4)], gu_mid[h].at[2], base + 2, 2 - 4 * (h % 2))
        to_chip(gu_send[h].at[rows_of(3)], gu_mid[h].at[0], base, 1)
        to_chip(gu_send[h].at[rows_of(-3)], gu_mid[h].at[1], base + 1, -1)
    for h in range(chunks):
        base = 17 + 14 * h
        for i in range(3):
            done("recv", base + i)
        for i in range(2):
            direction = 1 - 2 * i
            passing = gu_send[h][pl.ds(rows_of(2 * direction), 1)][0].astype(F32)
            passing = passing + gu_mid[h][i].astype(F32)
            if i == h % 2:
                passing = passing + gu_mid[h][2].astype(F32)
            gu_pass[h][i] = passing.astype(BF16)
            to_chip(gu_pass[h].at[i], gu_recv[h].at[2 + i], base + 5 + i, 2 * direction)
        to_chip(gu_send[h].at[rows_of(1)], gu_recv[h].at[0], base + 3, 1)
        to_chip(gu_send[h].at[rows_of(-1)], gu_recv[h].at[1], base + 4, -1)

    done("recv", 8)
    stats = jnp.sum(stat_recv[...], axis=0)
    mean_square = stats[:, experts : experts + 1] / depth
    logits = stats[:, 0:experts] * lax.rsqrt(mean_square + EPSILON)
    picked_top = jnp.max(jnp.where(hit, logits, NEGATIVE), axis=1, keepdims=True)
    picked = jnp.where(hit, jnp.exp(jnp.minimum(logits - picked_top, 0.0)), 0.0)
    share = picked / jnp.sum(picked, axis=1, keepdims=True)
    share_high, share_low = split_high(share)
    shares = jnp.concatenate([share_high, share_low], axis=0)
    share_wide = dot(shares, spread)
    combine = jnp.concatenate(
        [
            (share_wide[0:ROWS] * place).astype(BF16),
            (share_wide[ROWS : 2 * ROWS] * place).astype(BF16),
        ],
        axis=0,
    )
    done("recv", 9)
    square_sums = jnp.sum(sq_recv[...], axis=0)[0:1, :]
    scale_row = iota((2 * BLOCK, packed), 0) % BLOCK
    scale_lane = iota((2 * BLOCK, packed), 1)
    own_square = jnp.sum(
        jnp.where(scale_lane == y * PADB + scale_row, square_sums, 0.0), axis=1, keepdims=True
    )
    scale = lax.rsqrt(own_square / depth + EPSILON)

    back_row = iota((groups * SEND, chips * BLOCK), 0)
    back_lane = iota((groups * SEND, chips * BLOCK), 1)
    back_rank = back_row % SEND
    back_source = (back_row // SEND) * CAP_E + back_rank
    back_pick = one_hot((back_rank < CAP_E) & (back_lane == back_source))

    for h in range(chunks):
        first, size = spans[h]
        base = 17 + 14 * h
        for i in range(3, 7):
            done("recv", base + i)
        sums = gu_send[h][pl.ds(y, 1)][0].astype(F32)
        for i in range(4):
            sums = sums + gu_recv[h][i].astype(F32)
        gsum[:, 0:size] = sums * scale
        gates = gsum[0:BLOCK, 0:size]
        ups = gsum[BLOCK : 2 * BLOCK, 0:size]
        hidden = gates / (1.0 + jnp.exp(-gates)) * ups
        hid[h][pl.ds(y, 1)] = hidden.reshape(1, BLOCK // HALF, HALF, size).astype(BF16)
        for i, offset in enumerate((4, 3, -3, 2, -2, 1, -1)):
            to_chip(hid[h].at[y], hid[h].at[y], base + 7 + i, offset)
    done("load", 5)
    done("recv", 4)
    result = jnp.zeros((chips * BLOCK, chip), F32)
    for h in range(chunks):
        first, size = spans[h]
        for i in range(7, 14):
            done("recv", 17 + 14 * h + i)
        rows = hid[h][...].astype(F32).reshape(chips * BLOCK, size).astype(BF16)
        result = result + dot_t(rows, wd[:, first : first + size])
    result = result.astype(BF16)
    outcome = dot(back_pick, result)
    for h in range(2):
        ret_send[h] = outcome[:, HDIM * h : HDIM * (h + 1)].reshape(groups, SEND, HDIM).astype(BF16)
    landing = c * groups + g
    pl.semaphore_wait(rounds.at[8], 1)
    for k in group_order:
        at = other_group(k)
        remote(ret_send.at[c, at], ret_recv.at[landing], 12, grp=at).start()
        remote(ret_send.at[1 - c, at], ret_recv.at[landing], 12, grp=at, exp=sibling).start()
    remote(ret_send.at[1 - c, g], ret_recv.at[landing], 12, exp=sibling).start()
    track(2 * groups - 1, ret_recv, 12)
    ret_recv[pl.ds(landing, 1)] = ret_send[c, pl.ds(g, 1)]
    own = jnp.where(c == 0, residual[:, 0:HDIM], residual[:, HDIM:chip])
    done("recv", 12)
    returned = ret_recv[...].astype(F32).reshape(2 * groups * SEND, HDIM).astype(BF16)
    both = dot(combine, returned)
    out_ref[0] = (
        (own + both[0:ROWS] + both[ROWS : 2 * ROWS]).reshape(STEPS, HALF, HDIM).astype(BF16)
    )

    finish()


def in_hbm(value):
    return pltpu.with_memory_space_constraint(value, pltpu.HBM)


def on_device(
    step_inputs,
    parents,
    routes,
    w_qkv,
    w_out,
    prompt_keys,
    prompt_values,
    prompt_parts,
    tail_keys,
    tail_values,
    w_router,
    norm_gain,
    w_gate_up,
    w_down,
):
    groups = lax.axis_size("grp")
    columns = lax.axis_size("exp")
    chips = columns // 2
    depth = step_inputs.shape[3]
    cap = prompt_keys.shape[1]
    ffe = w_down.shape[2]
    experts = w_router.shape[1]
    topk = routes.shape[3]
    chip = 2 * HDIM
    spans = column_spans(ffe)
    keys = cap + HALF * PREV + 2 * ROWS
    vmem = pl.BlockSpec(memory_space=pltpu.VMEM)
    out = pl.pallas_call(
        functools.partial(kernel, groups, columns, topk),
        out_shape=jax.ShapeDtypeStruct((1, STEPS, HALF, HDIM), BF16),
        in_specs=[
            pl.BlockSpec(memory_space=pltpu.HBM)
        ]
        * 14,
        out_specs=vmem,
        scratch_shapes=[
            pltpu.VMEM((STEPS, HALF, depth), BF16),
            pltpu.SMEM((1, STEPS, HALF), jnp.int32),
            pltpu.VMEM((STEPS, HALF, topk), jnp.int32),
            pltpu.SMEM((1,), jnp.int32),
            pltpu.VMEM((PREV, HALF, HDIM), BF16),
            pltpu.VMEM((PREV, HALF, HDIM), BF16),
            pltpu.VMEM((ROWS, depth), F32),
            pltpu.VMEM((ROWS, HDIM), jnp.int32),
            pltpu.VMEM((2, 1, HDIM), F32),
            pltpu.VMEM((2, experts, HDIM), BF16),
            pltpu.VMEM((depth, 3 * HDIM), BF16),
            pltpu.VMEM((chip, depth), BF16),
            pltpu.VMEM((keys, HDIM), BF16),
            pltpu.VMEM((keys, HDIM), BF16),
            pltpu.VMEM((chip, 2 * ffe), BF16),
            pltpu.VMEM((chip, ffe), BF16),
            pltpu.VMEM((2, ROWS, 4 * HDIM), BF16),
            pltpu.VMEM((2, ROWS, chip), F32),
            pltpu.VMEM((3, ROWS, chip), F32),
            pltpu.VMEM((chips, ROWS, chip), BF16),
            pltpu.VMEM((chips, ROWS, chip), BF16),
            pltpu.VMEM((ROWS, HDIM), F32),
            pltpu.VMEM((chips, ROWS, HDIM), F32),
            pltpu.VMEM((groups, SEND, chip), BF16),
            pltpu.VMEM((groups, SEND, chip), BF16),
            pltpu.VMEM((8, chips * PADB), F32),
            pltpu.VMEM((chips, 8, chips * PADB), F32),
            [pltpu.VMEM((chips, 2 * BLOCK, size), BF16) for _, size in spans],
            [pltpu.VMEM((3, 2 * BLOCK, size), BF16) for _, size in spans],
            [pltpu.VMEM((2, 2 * BLOCK, size), BF16) for _, size in spans],
            [pltpu.VMEM((4, 2 * BLOCK, size), BF16) for _, size in spans],
            pltpu.VMEM((2 * BLOCK, max(size for _, size in spans)), F32),
            [pltpu.VMEM((chips, BLOCK // HALF, HALF, size), BF16) for _, size in spans],
            pltpu.VMEM((2, groups, SEND, HDIM), BF16),
            pltpu.VMEM((2 * groups, SEND, HDIM), BF16),
            pltpu.SemaphoreType.DMA((16,)),
            pltpu.SemaphoreType.DMA((17 + 14 * len(spans),)),
            pltpu.SemaphoreType.DMA((17 + 14 * len(spans),)),
            pltpu.SemaphoreType.REGULAR((9,)),
        ],
        compiler_params=pltpu.CompilerParams(
            collective_id=0, has_side_effects=True, vmem_limit_bytes=48 * 1024 * 1024
        ),
        name="layer",
    )(
        in_hbm(step_inputs),
        in_hbm(parents),
        in_hbm(routes),
        prompt_parts,
        in_hbm(norm_gain.reshape(1, HDIM)),
        in_hbm(w_router.T),
        in_hbm(jnp.transpose(w_qkv, (1, 0, 2))),
        in_hbm(w_out),
        in_hbm(prompt_keys),
        in_hbm(prompt_values),
        in_hbm(jnp.transpose(tail_keys, (0, 2, 1, 3))),
        in_hbm(jnp.transpose(tail_values, (0, 2, 1, 3))),
        in_hbm(w_gate_up),
        in_hbm(w_down),
    )
    return out


def solution(mesh):
    placed = (
        P("grp", None, None, None),
        P("grp", None, None),
        P("grp", None, None, None),
        P(None, None, "exp"),
        P("exp", None),
        P("grp", None, "exp"),
        P("grp", None, "exp"),
        P("grp"),
        P("grp", None, None, "exp"),
        P("grp", None, None, "exp"),
        P("exp", None),
        P("exp"),
        P("grp", "exp", None),
        P("grp", "exp", None),
    )
    return jax.shard_map(
        on_device,
        mesh=mesh,
        in_specs=placed,
        out_specs=P("grp", None, None, "exp"),
        check_vma=False,
    )
```

```python
import functools

import jax
import jax.numpy as jnp
from jax import lax
from jax.experimental import pallas as pl
from jax.experimental.pallas import tpu as pltpu
from jax.sharding import PartitionSpec as P

HDIM = 128
TOPK = 6
STEPS = 4
HALF = 4
ROWS = STEPS * HALF
CAP_E = 3
PREV = 60
SEND = 4
BLOCK = 12
PADB = 16

NEGATIVE = -1e30
EPSILON = 1e-06
F32 = jnp.float32
BF16 = jnp.bfloat16


def iota(shape, axis):
    return lax.broadcasted_iota(jnp.int32, shape, axis)


def dot(a, b, precision=None):
    return jnp.dot(a, b, preferred_element_type=F32, precision=precision)


def dot_t(a, b, precision=None):
    return lax.dot_general(
        a, b, (((1,), (1,)), ((), ())), preferred_element_type=F32, precision=precision
    )


def one_hot(cond):
    return jnp.where(cond, 1.0, 0.0).astype(BF16)


def split_high(value):
    high = value.astype(BF16)
    return high, (value - high.astype(F32)).astype(BF16)


def column_spans(ffe, chunks=3):
    tiles = ffe // HDIM
    sizes = [HDIM * (tiles // chunks + (h < tiles % chunks)) for h in range(chunks)]
    return [(sum(sizes[:h]), sizes[h]) for h in range(chunks)]


def kernel(
    groups,
    columns,
    topk,
    x_hbm,
    par_hbm,
    routes_hbm,
    parts_hbm,
    gain_hbm,
    wr_hbm,
    wqkv_hbm,
    wout_hbm,
    pk_hbm,
    pv_hbm,
    tk_hbm,
    tv_hbm,
    wgu_hbm,
    wd_hbm,
    out_ref,
    x_ref,
    par_ref,
    routes_ref,
    parts_ref,
    tk_ref,
    tv_ref,
    xs,
    rts,
    gain,
    wr,
    wqkv,
    wout,
    kall,
    vall,
    wgu,
    wd,
    qkv,
    part_send,
    part_recv,
    proj_send,
    proj_recv,
    stat_send,
    stat_recv,
    disp_send,
    disp_recv,
    sq_send,
    sq_recv,
    gu_send,
    gu_mid,
    gu_pass,
    gu_recv,
    gsum,
    hid,
    ret_send,
    ret_recv,
    local_sem,
    send_sem,
    recv_sem,
    rounds,
):
    chips = columns // 2
    ffe = wd.shape[1]
    spans = column_spans(ffe)
    cap = pk_hbm.shape[1]
    experts = wr.shape[1]
    depth = x_ref.shape[2]
    g = lax.axis_index("grp")
    e = lax.axis_index("exp")
    y = e // 2
    c = e % 2
    half = g % 2
    partner = g + 1 - 2 * half
    sibling = e + 1 - 2 * c
    own_rows = pl.ds(pl.multiple_of(c * HDIM, HDIM), HDIM)

    waits = {}

    def done(kind, index):
        waits.pop((kind, index))()

    def finish():
        for key in list(waits):
            done(*key)

    def local(src, dst, index):
        copy = pltpu.make_async_copy(src, dst, local_sem.at[index])
        copy.start()
        waits["load", index] = copy.wait

    def remote(src, dst, index, **where):
        return pltpu.make_async_remote_copy(
            src_ref=src,
            dst_ref=dst,
            send_sem=send_sem.at[index],
            recv_sem=recv_sem.at[index],
            device_id=where,
            device_id_type=pl.DeviceIdType.MESH,
        )

    def send(src, dst, index, **where):
        copy = remote(src, dst, index, **where)
        copy.start()
        waits["recv", index] = copy.wait_recv
        waits["send", index] = copy.wait_send

    def track(count, landing, index):
        whole = landing.at[pl.ds(0, count)]
        waits["recv", index] = pltpu.make_async_copy(whole, whole, recv_sem.at[index]).wait
        waits["send", index] = pltpu.make_async_copy(whole, whole, send_sem.at[index]).wait

    def send_each(order, one, landing, index):
        for k in order:
            one(k).start()
        track(len(order), landing, index)

    deep = 8
    wide_groups = groups // deep
    group_order = [(i, j) for i in range(wide_groups) for j in range(deep) if i or j]
    group_order.sort(key=lambda k: -min(k[0], wide_groups - k[0]) - min(k[1], deep - k[1]))
    chip_order = sorted(range(1, chips), key=lambda k: -min(k, chips - k))

    def other_group(k):
        return lax.rem(g // deep + k[0], wide_groups) * deep + lax.rem(g % deep + k[1], deep)

    def other_chip(k):
        return lax.rem(y + k, chips)

    def to_chip(src, dst, index, offset):
        send(src, dst, index, exp=2 * other_chip(offset + chips) + c)

    local(x_hbm.at[0], x_ref, 6)
    local(par_hbm, par_ref, 7)
    local(routes_hbm.at[0], routes_ref, 8)
    local(parts_hbm, parts_ref, 9)
    for i in range(3):
        local(wqkv_hbm.at[i], wqkv.at[:, pl.ds(HDIM * i, HDIM)], (0, 14, 15)[i])
    local(tk_hbm.at[0], tk_ref, 10)
    local(tv_hbm.at[0], tv_ref, 11)
    local(gain_hbm, gain.at[c], 12)
    local(wr_hbm, wr.at[c], 13)
    local(pk_hbm.at[0], kall.at[pl.ds(0, cap)], 1)
    local(pv_hbm.at[0], vall.at[pl.ds(0, cap)], 2)
    local(wout_hbm, wout.at[pl.ds(0, HDIM)], 3)
    local(wgu_hbm.at[c], wgu.at[own_rows], 4)
    local(wd_hbm.at[c], wd.at[own_rows], 5)

    barrier = pltpu.get_barrier_semaphore()

    def greet(semaphore, **where):
        pl.semaphore_signal(
            semaphore, inc=1, device_id=where, device_id_type=pl.DeviceIdType.MESH
        )

    def along_y(semaphore):
        for k in (1, chips - 1):
            greet(semaphore, exp=2 * other_chip(k) + c)

    def along_z(semaphore):
        for k in (1, deep - 1):
            greet(semaphore, grp=other_group((0, k)))

    def along_x(semaphore):
        for k in (1, wide_groups - 1):
            greet(semaphore, grp=other_group((k, 0)))

    along_x(barrier)
    along_y(barrier)
    along_z(barrier)
    greet(barrier, exp=sibling)
    greet(barrier, grp=partner, exp=sibling)

    def pass_word(index):
        along_y(rounds.at[index])
        along_z(rounds.at[3 + index])

    def hear_word(index):
        pl.semaphore_wait(rounds.at[index], 2)
        pl.semaphore_wait(rounds.at[3 + index], 2)

    done("load", 6)
    done("load", 8)
    done("load", 7)
    for s in range(STEPS):
        xs[HALF * s : HALF * (s + 1), :] = x_ref[s].astype(F32)
        rts[HALF * s : HALF * (s + 1), :topk] = routes_ref[s]
    x16 = xs[...].astype(BF16)
    row_sub = iota((ROWS, HDIM), 0)
    row_lane = iota((ROWS, HDIM), 1)
    parent_hot = jnp.zeros((ROWS, HDIM), F32)
    for s in range(STEPS):
        for b in range(HALF):
            parent_hot = jnp.where(
                (row_sub == HALF * s + b) & (row_lane == par_ref[0, s, b]), 1.0, parent_hot
            )
    done("load", 0)
    done("load", 14)
    done("load", 15)
    qkv[0, :, 0 : 3 * HDIM] = dot(x16, wqkv[...]).astype(BF16)
    qkv[0, :, 3 * HDIM : 4 * HDIM] = parent_hot.astype(BF16)

    pl.semaphore_wait(barrier, 8)
    pass_word(0)

    send(qkv.at[0], qkv.at[1], 0, grp=partner)
    send(wout_hbm, wout.at[pl.ds(HDIM, HDIM)], 6, exp=sibling)
    send(gain_hbm, gain.at[c], 1, exp=sibling)
    send(wr_hbm, wr.at[c], 2, exp=sibling)
    send(wgu_hbm.at[1 - c], wgu.at[own_rows], 3, exp=sibling)
    send(wd_hbm.at[1 - c], wd.at[own_rows], 4, exp=sibling)

    tail_at = cap
    new_at = cap + HALF * PREV
    total = new_at + 2 * ROWS
    done("load", 10)
    done("load", 11)
    kall[tail_at:new_at, :] = tk_ref[...].astype(F32).reshape(HALF * PREV, HDIM).astype(BF16)
    vall[tail_at:new_at, :] = tv_ref[...].astype(F32).reshape(HALF * PREV, HDIM).astype(BF16)

    done("load", 1)
    done("load", 2)
    hear_word(0)
    pass_word(1)
    done("recv", 0)
    for h in range(2):
        at = new_at + ROWS * h
        kall[at : at + ROWS, :] = qkv[h, :, HDIM : 2 * HDIM]
        vall[at : at + ROWS, :] = qkv[h, :, 2 * HDIM : 3 * HDIM]
    query = jnp.concatenate([qkv[0, :, 0:HDIM], qkv[1, :, 0:HDIM]], axis=0)
    parents = jnp.concatenate(
        [qkv[0, :, 3 * HDIM : 4 * HDIM], qkv[1, :, 3 * HDIM : 4 * HDIM]], axis=0
    )
    tokens = 2 * ROWS
    beam_row = iota((HDIM, tokens), 0)
    token_lane = iota((HDIM, tokens), 1)
    beam_of = HALF * ((token_lane // ROWS + half) % 2) + token_lane % HALF
    before = dot(parents, one_hot(beam_row == beam_of))
    step_row = (iota((tokens, tokens), 0) % ROWS) // HALF
    step_lane = (iota((tokens, tokens), 1) % ROWS) // HALF
    same = jnp.where(iota((tokens, tokens), 0) == iota((tokens, tokens), 1), 1.0, 0.0)
    back = jnp.where(step_lane + 1 == step_row, before, 0.0)
    back_bf = back.astype(BF16)
    near = (same + back).astype(BF16)
    back_two = dot(back_bf, back_bf)
    path = dot(near, (same + back_two).astype(BF16)).astype(BF16)
    first_row = iota((tokens, HDIM), 0) % ROWS
    first = jnp.where(first_row < HALF, parents.astype(F32), 0.0).astype(BF16)
    origin = dot(path, first).astype(BF16)
    tails = HALF * PREV
    tail_row = iota((HDIM, tails), 0)
    tail_lane = iota((HDIM, tails), 1)
    tail_on = dot(origin, one_hot(tail_row == HALF * half + tail_lane % HALF))
    new_on = jnp.where(iota((tokens, tokens), 0) < ROWS, path.astype(F32), 0.0)

    done("load", 9)
    score_scale = HDIM ** (-0.5)
    scores = dot_t(query, kall[...]) * score_scale
    prompt_live = iota((tokens, cap), 1) < parts_ref[0]
    prompt_s = jnp.where(prompt_live, scores[:, 0:cap], NEGATIVE)
    tail_s = jnp.where(tail_on > 0.5, scores[:, tail_at:new_at], NEGATIVE)
    new_s = jnp.where(new_on > 0.5, scores[:, new_at:total], NEGATIVE)
    top = jnp.maximum(
        jnp.maximum(
            jnp.max(prompt_s, axis=1, keepdims=True), jnp.max(tail_s, axis=1, keepdims=True)
        ),
        jnp.max(new_s, axis=1, keepdims=True),
    )
    prompt_w = jnp.exp(prompt_s - top)
    tail_w = jnp.exp(tail_s - top)
    new_w = jnp.exp(new_s - top)
    weight_sum = (
        jnp.sum(prompt_w, axis=1, keepdims=True)
        + jnp.sum(tail_w, axis=1, keepdims=True)
        + jnp.sum(new_w, axis=1, keepdims=True)
    )

    def weighted(weights, values):
        high, low = split_high(weights)
        both = dot(jnp.concatenate([high, low], axis=0), values)
        return both[0:tokens] + both[tokens : 2 * tokens]

    mix = (
        weighted(prompt_w, vall[0:cap, :])
        + weighted(tail_w, vall[tail_at:new_at, :])
        + weighted(new_w, vall[new_at:total, :])
    )
    lane = iota((ROWS, HDIM), 1)
    for h in (1, 0):
        rows = slice(ROWS * h, ROWS * (h + 1))
        part_send[h, :, 0:HDIM] = mix[rows]
        part_send[h, :, HDIM : 2 * HDIM] = jnp.where(
            lane < HDIM // 2, top[rows], weight_sum[rows]
        )
        if h == 1:
            send(part_send.at[1], part_recv.at[2], 5, grp=partner, exp=sibling)
            send(part_send.at[1], part_recv.at[0], 14, grp=partner)
    send(part_send.at[0], part_recv.at[1], 15, exp=sibling)
    hear_word(1)
    pass_word(2)

    width = groups * SEND
    routes = rts[...]
    hit = jnp.zeros((ROWS, experts), jnp.bool_)
    expert_lane = iota((ROWS, experts), 1)
    for k in range(topk):
        hit = hit | (routes[:, k : k + 1] == expert_lane)
    hits = one_hot(hit)
    rank = dot(one_hot(iota((ROWS, ROWS), 1) < iota((ROWS, ROWS), 0)), hits)
    spread_row = iota((experts, 2 * width), 0)
    spread_lane = iota((experts, 2 * width), 1)
    spread = one_hot(
        spread_row == 2 * (spread_lane % width // SEND) + spread_lane // width
    )
    hit_wide = dot(hits, spread)
    rank_wide = dot(rank.astype(BF16), spread)
    slot_lane = (iota((ROWS, 2 * width), 1) % SEND).astype(F32)
    place = jnp.where((rank_wide == slot_lane) & (hit_wide > 0.5), 1.0, 0.0)
    own_place = jnp.where(c == 0, place[:, 0:width], place[:, width : 2 * width])

    def joined(near_mix, near_tail, far_mix, far_tail):
        near_top, near_sum = near_tail[:, 0:1], near_tail[:, HDIM // 2 : HDIM // 2 + 1]
        far_top, far_sum = far_tail[:, 0:1], far_tail[:, HDIM // 2 : HDIM // 2 + 1]
        best = jnp.maximum(near_top, far_top)
        near_factor = jnp.exp(near_top - best)
        far_factor = jnp.exp(far_top - best)
        return (
            (near_mix * near_factor + far_mix * far_factor)
            / (near_sum * near_factor + far_sum * far_factor)
        ).astype(BF16)

    def halves(ref, index):
        return ref[index, :, 0:HDIM], ref[index, :, HDIM : 2 * HDIM]

    done("recv", 15)
    done("recv", 14)
    own_head = joined(*halves(part_send, 0), *halves(part_recv, 0))
    done("recv", 5)
    other_head = joined(*halves(part_recv, 1), *halves(part_recv, 2))
    attention = jnp.concatenate([own_head, other_head], axis=1)
    done("load", 3)
    done("recv", 6)
    hear_word(2)
    along_x(rounds.at[6])

    chip = 2 * HDIM

    def features(at):
        return pl.ds(pl.multiple_of(at * chip, chip), chip)

    for k in chip_order:
        at = other_chip(k)
        proj_send[pl.ds(at, 1)] = (
            dot(attention, wout[:, features(at)]).astype(BF16).reshape(1, ROWS, chip)
        )
        remote(proj_send.at[at], proj_recv.at[y], 16, exp=2 * at + c).start()
    track(chips - 1, proj_recv, 16)
    pl.semaphore_wait(rounds.at[6], 2)
    along_x(rounds.at[7])
    residual = xs[:, features(y)] + dot(attention, wout[:, features(y)])
    proj_recv[pl.ds(y, 1)] = jnp.zeros((1, ROWS, chip), BF16)
    done("recv", 16)
    pl.semaphore_wait(rounds.at[7], 2)
    residual = residual + jnp.sum(proj_recv[...].astype(F32), axis=0)

    rows_bf = residual.astype(BF16)
    outgoing = lax.dot_general(
        own_place.astype(BF16), rows_bf, (((0,), (0,)), ((), ())), preferred_element_type=F32
    )
    disp_send[...] = outgoing.reshape(groups, SEND, chip).astype(BF16)

    send_each(
        group_order,
        lambda k: remote(
            disp_send.at[other_group(k)], disp_recv.at[g], 7, grp=other_group(k)
        ),
        disp_recv,
        7,
    )
    disp_recv[pl.ds(g, 1)] = disp_send[pl.ds(g, 1)]
    greet(rounds.at[8], exp=sibling)

    done("load", 12)
    done("load", 13)
    done("recv", 1)
    done("recv", 2)
    gains = jnp.concatenate([gain[0], gain[1]], axis=1)
    scaled = (residual * gains).astype(BF16)
    logit_part = dot_t(scaled[:, 0:HDIM], wr[0]) + dot_t(scaled[:, HDIM:chip], wr[1])
    stat_send[:, 0:experts] = logit_part
    stat_send[:, experts:HDIM] = jnp.broadcast_to(
        jnp.sum(residual * residual, axis=1, keepdims=True), (ROWS, HDIM - experts)
    )

    send_each(
        chip_order,
        lambda k: remote(stat_send, stat_recv.at[y], 8, exp=2 * other_chip(k) + c),
        stat_recv,
        8,
    )
    stat_recv[pl.ds(y, 1)] = stat_send[...].reshape(1, ROWS, stat_send.shape[1])

    packed = chips * PADB
    pick_row = iota((packed, groups * SEND), 0)
    pick_lane = iota((packed, groups * SEND), 1)
    per = BLOCK // CAP_E
    own_dest = pick_row // PADB

    def picks(shift):
        index = pick_row % PADB - shift
        safe = jnp.maximum(index, 0)
        source = (own_dest * per + safe // CAP_E) * SEND + safe % CAP_E
        return one_hot((index >= 0) & (index < BLOCK) & (pick_lane == source))

    gate_pick = picks(0)
    up_pick = picks(PADB - BLOCK)
    done("recv", 7)
    arrived = disp_recv[...].astype(F32).reshape(groups * SEND, chip).astype(BF16)
    gate_rows = dot(gate_pick, arrived)
    up_rows = dot(up_pick, arrived)
    gate_in = (gate_rows * gains).astype(BF16)
    up_in = (up_rows * gains).astype(BF16)
    done("load", 4)
    done("recv", 3)
    def rows_of(offset):
        return other_chip(offset + chips)

    chunks = len(spans)
    for h in range(chunks):
        first, size = spans[h]
        gate = dot(gate_in, wgu[:, first : first + size]).reshape(chips, 2, 8, size)
        up = dot(up_in, wgu[:, ffe + first : ffe + first + size]).reshape(chips, 2, 8, size)
        gu_send[h][:, 0:8] = gate[:, 0].astype(BF16)
        gu_send[h][:, 8:16] = (gate[:, 1] + up[:, 0]).astype(BF16)
        gu_send[h][:, 16:24] = up[:, 1].astype(BF16)
        base = 17 + 14 * h
        to_chip(gu_send[h].at[rows_of(4)], gu_mid[h].at[2], base + 2, 2 - 4 * (h % 2))
        to_chip(gu_send[h].at[rows_of(3)], gu_mid[h].at[0], base, 1)
        to_chip(gu_send[h].at[rows_of(-3)], gu_mid[h].at[1], base + 1, -1)
    squares = dot_t(
        jnp.ones((8, chip), F32), gate_rows * gate_rows, precision=lax.Precision.HIGHEST
    )
    sq_send[...] = squares

    send_each(
        chip_order,
        lambda k: remote(sq_send, sq_recv.at[y], 9, exp=2 * other_chip(k) + c),
        sq_recv,
        9,
    )
    sq_recv[pl.ds(y, 1)] = squares.reshape(1, 8, packed)

    for h in range(chunks):
        base = 17 + 14 * h
        for i in range(3):
            done("recv", base + i)
        for i in range(2):
            direction = 1 - 2 * i
            passing = gu_send[h][pl.ds(rows_of(2 * direction), 1)][0].astype(F32)
            passing = passing + gu_mid[h][i].astype(F32)
            if i == h % 2:
                passing = passing + gu_mid[h][2].astype(F32)
            gu_pass[h][i] = passing.astype(BF16)
            to_chip(gu_pass[h].at[i], gu_recv[h].at[2 + i], base + 5 + i, 2 * direction)
        to_chip(gu_send[h].at[rows_of(1)], gu_recv[h].at[0], base + 3, 1)
        to_chip(gu_send[h].at[rows_of(-1)], gu_recv[h].at[1], base + 4, -1)

    done("recv", 8)
    stats = jnp.sum(stat_recv[...], axis=0)
    mean_square = stats[:, experts : experts + 1] / depth
    logits = stats[:, 0:experts] * lax.rsqrt(mean_square + EPSILON)
    picked_top = jnp.max(jnp.where(hit, logits, NEGATIVE), axis=1, keepdims=True)
    picked = jnp.where(hit, jnp.exp(jnp.minimum(logits - picked_top, 0.0)), 0.0)
    share = picked / jnp.sum(picked, axis=1, keepdims=True)
    share_high, share_low = split_high(share)
    shares = jnp.concatenate([share_high, share_low], axis=0)
    share_wide = dot(shares, spread)
    combine = jnp.concatenate(
        [
            (share_wide[0:ROWS] * place).astype(BF16),
            (share_wide[ROWS : 2 * ROWS] * place).astype(BF16),
        ],
        axis=0,
    )
    done("recv", 9)
    square_sums = jnp.sum(sq_recv[...], axis=0)[0:1, :]
    scale_row = iota((2 * BLOCK, packed), 0) % BLOCK
    scale_lane = iota((2 * BLOCK, packed), 1)
    own_square = jnp.sum(
        jnp.where(scale_lane == y * PADB + scale_row, square_sums, 0.0), axis=1, keepdims=True
    )
    scale = lax.rsqrt(own_square / depth + EPSILON)

    back_row = iota((groups * SEND, chips * BLOCK), 0)
    back_lane = iota((groups * SEND, chips * BLOCK), 1)
    back_rank = back_row % SEND
    back_source = (back_row // SEND) * CAP_E + back_rank
    back_pick = one_hot((back_rank < CAP_E) & (back_lane == back_source))

    for h in range(chunks):
        first, size = spans[h]
        base = 17 + 14 * h
        for i in range(3, 7):
            done("recv", base + i)
        sums = gu_send[h][pl.ds(y, 1)][0].astype(F32)
        for i in range(4):
            sums = sums + gu_recv[h][i].astype(F32)
        gsum[:, 0:size] = sums * scale
        gates = gsum[0:BLOCK, 0:size]
        ups = gsum[BLOCK : 2 * BLOCK, 0:size]
        hidden = gates / (1.0 + jnp.exp(-gates)) * ups
        hid[h][pl.ds(y, 1)] = hidden.reshape(1, BLOCK // HALF, HALF, size).astype(BF16)
        for i, offset in enumerate((4, 3, -3, 2, -2, 1, -1)):
            to_chip(hid[h].at[y], hid[h].at[y], base + 7 + i, offset)
    done("load", 5)
    done("recv", 4)
    result = jnp.zeros((chips * BLOCK, chip), F32)
    for h in range(chunks):
        first, size = spans[h]
        for i in range(7, 14):
            done("recv", 17 + 14 * h + i)
        rows = hid[h][...].astype(F32).reshape(chips * BLOCK, size).astype(BF16)
        result = result + dot_t(rows, wd[:, first : first + size])
    result = result.astype(BF16)
    outcome = dot(back_pick, result)
    for h in range(2):
        ret_send[h] = outcome[:, HDIM * h : HDIM * (h + 1)].reshape(groups, SEND, HDIM).astype(BF16)
    landing = c * groups + g
    pl.semaphore_wait(rounds.at[8], 1)
    for k in group_order:
        at = other_group(k)
        remote(ret_send.at[c, at], ret_recv.at[landing], 12, grp=at).start()
        remote(ret_send.at[1 - c, at], ret_recv.at[landing], 12, grp=at, exp=sibling).start()
    remote(ret_send.at[1 - c, g], ret_recv.at[landing], 12, exp=sibling).start()
    track(2 * groups - 1, ret_recv, 12)
    ret_recv[pl.ds(landing, 1)] = ret_send[c, pl.ds(g, 1)]
    own = jnp.where(c == 0, residual[:, 0:HDIM], residual[:, HDIM:chip])
    done("recv", 12)
    returned = ret_recv[...].astype(F32).reshape(2 * groups * SEND, HDIM).astype(BF16)
    both = dot(combine, returned)
    out_ref[0] = (
        (own + both[0:ROWS] + both[ROWS : 2 * ROWS]).reshape(STEPS, HALF, HDIM).astype(BF16)
    )

    finish()


def in_hbm(value):
    return pltpu.with_memory_space_constraint(value, pltpu.HBM)


def on_device(
    step_inputs,
    parents,
    routes,
    w_qkv,
    w_out,
    prompt_keys,
    prompt_values,
    prompt_parts,
    tail_keys,
    tail_values,
    w_router,
    norm_gain,
    w_gate_up,
    w_down,
):
    groups = lax.axis_size("grp")
    columns = lax.axis_size("exp")
    chips = columns // 2
    depth = step_inputs.shape[3]
    cap = prompt_keys.shape[1]
    ffe = w_down.shape[2]
    experts = w_router.shape[1]
    topk = routes.shape[3]
    chip = 2 * HDIM
    spans = column_spans(ffe)
    keys = cap + HALF * PREV + 2 * ROWS
    vmem = pl.BlockSpec(memory_space=pltpu.VMEM)
    out = pl.pallas_call(
        functools.partial(kernel, groups, columns, topk),
        out_shape=jax.ShapeDtypeStruct((1, STEPS, HALF, HDIM), BF16),
        in_specs=[
            pl.BlockSpec(memory_space=pltpu.HBM)
        ]
        * 14,
        out_specs=vmem,
        scratch_shapes=[
            pltpu.VMEM((STEPS, HALF, depth), BF16),
            pltpu.SMEM((1, STEPS, HALF), jnp.int32),
            pltpu.VMEM((STEPS, HALF, topk), jnp.int32),
            pltpu.SMEM((1,), jnp.int32),
            pltpu.VMEM((PREV, HALF, HDIM), BF16),
            pltpu.VMEM((PREV, HALF, HDIM), BF16),
            pltpu.VMEM((ROWS, depth), F32),
            pltpu.VMEM((ROWS, HDIM), jnp.int32),
            pltpu.VMEM((2, 1, HDIM), F32),
            pltpu.VMEM((2, experts, HDIM), BF16),
            pltpu.VMEM((depth, 3 * HDIM), BF16),
            pltpu.VMEM((chip, depth), BF16),
            pltpu.VMEM((keys, HDIM), BF16),
            pltpu.VMEM((keys, HDIM), BF16),
            pltpu.VMEM((chip, 2 * ffe), BF16),
            pltpu.VMEM((chip, ffe), BF16),
            pltpu.VMEM((2, ROWS, 4 * HDIM), BF16),
            pltpu.VMEM((2, ROWS, chip), F32),
            pltpu.VMEM((3, ROWS, chip), F32),
            pltpu.VMEM((chips, ROWS, chip), BF16),
            pltpu.VMEM((chips, ROWS, chip), BF16),
            pltpu.VMEM((ROWS, HDIM), F32),
            pltpu.VMEM((chips, ROWS, HDIM), F32),
            pltpu.VMEM((groups, SEND, chip), BF16),
            pltpu.VMEM((groups, SEND, chip), BF16),
            pltpu.VMEM((8, chips * PADB), F32),
            pltpu.VMEM((chips, 8, chips * PADB), F32),
            [pltpu.VMEM((chips, 2 * BLOCK, size), BF16) for _, size in spans],
            [pltpu.VMEM((3, 2 * BLOCK, size), BF16) for _, size in spans],
            [pltpu.VMEM((2, 2 * BLOCK, size), BF16) for _, size in spans],
            [pltpu.VMEM((4, 2 * BLOCK, size), BF16) for _, size in spans],
            pltpu.VMEM((2 * BLOCK, max(size for _, size in spans)), F32),
            [pltpu.VMEM((chips, BLOCK // HALF, HALF, size), BF16) for _, size in spans],
            pltpu.VMEM((2, groups, SEND, HDIM), BF16),
            pltpu.VMEM((2 * groups, SEND, HDIM), BF16),
            pltpu.SemaphoreType.DMA((16,)),
            pltpu.SemaphoreType.DMA((17 + 14 * len(spans),)),
            pltpu.SemaphoreType.DMA((17 + 14 * len(spans),)),
            pltpu.SemaphoreType.REGULAR((9,)),
        ],
        compiler_params=pltpu.CompilerParams(
            collective_id=0, has_side_effects=True, vmem_limit_bytes=48 * 1024 * 1024
        ),
        name="layer",
    )(
        in_hbm(step_inputs),
        in_hbm(parents),
        in_hbm(routes),
        prompt_parts,
        in_hbm(norm_gain.reshape(1, HDIM)),
        in_hbm(w_router.T),
        in_hbm(jnp.transpose(w_qkv, (1, 0, 2))),
        in_hbm(w_out),
        in_hbm(prompt_keys),
        in_hbm(prompt_values),
        in_hbm(jnp.transpose(tail_keys, (0, 2, 1, 3))),
        in_hbm(jnp.transpose(tail_values, (0, 2, 1, 3))),
        in_hbm(w_gate_up),
        in_hbm(w_down),
    )
    return out


def solution(mesh):
    placed = (
        P("grp", None, None, None),
        P("grp", None, None),
        P("grp", None, None, None),
        P(None, None, "exp"),
        P("exp", None),
        P("grp", None, "exp"),
        P("grp", None, "exp"),
        P("grp"),
        P("grp", None, None, "exp"),
        P("grp", None, None, "exp"),
        P("exp", None),
        P("exp"),
        P("grp", "exp", None),
        P("grp", "exp", None),
    )
    return jax.shard_map(
        on_device,
        mesh=mesh,
        in_specs=placed,
        out_specs=P("grp", None, None, "exp"),
        check_vma=False,
    )
```

```python
import functools

import jax
import jax.numpy as jnp
from jax import lax
from jax.experimental import pallas as pl
from jax.experimental.pallas import tpu as pltpu
from jax.sharding import PartitionSpec as P

HDIM = 128
TOPK = 6
STEPS = 4
HALF = 4
ROWS = STEPS * HALF
CAP_E = 3
PREV = 60
SEND = 4
BLOCK = 12
PADB = 16

NEGATIVE = -1e30
EPSILON = 1e-06
F32 = jnp.float32
BF16 = jnp.bfloat16


def iota(shape, axis):
    return lax.broadcasted_iota(jnp.int32, shape, axis)


def dot(a, b, precision=None):
    return jnp.dot(a, b, preferred_element_type=F32, precision=precision)


def dot_t(a, b, precision=None):
    return lax.dot_general(
        a, b, (((1,), (1,)), ((), ())), preferred_element_type=F32, precision=precision
    )


def one_hot(cond):
    return jnp.where(cond, 1.0, 0.0).astype(BF16)


def split_high(value):
    high = value.astype(BF16)
    return high, (value - high.astype(F32)).astype(BF16)


def column_spans(ffe, chunks=3):
    tiles = ffe // HDIM
    sizes = [HDIM * (tiles // chunks + (h < tiles % chunks)) for h in range(chunks)]
    return [(sum(sizes[:h]), sizes[h]) for h in range(chunks)]


def kernel(
    groups,
    columns,
    topk,
    x_hbm,
    par_hbm,
    routes_hbm,
    parts_hbm,
    gain_hbm,
    wr_hbm,
    wqkv_hbm,
    wout_hbm,
    pk_hbm,
    pv_hbm,
    tk_hbm,
    tv_hbm,
    wgu_hbm,
    wd_hbm,
    out_ref,
    x_ref,
    par_ref,
    routes_ref,
    parts_ref,
    tk_ref,
    tv_ref,
    xs,
    rts,
    gain,
    wr,
    wqkv,
    wout,
    kall,
    vall,
    wgu,
    wd,
    qkv,
    hot,
    part_send,
    part_recv,
    proj_send,
    proj_recv,
    stat_send,
    stat_recv,
    disp_send,
    disp_recv,
    sq_send,
    sq_recv,
    gu_send,
    gu_mid,
    gu_pass,
    gu_recv,
    gsum,
    hid,
    ret_send,
    ret_recv,
    local_sem,
    send_sem,
    recv_sem,
    rounds,
):
    chips = columns // 2
    ffe = wd.shape[1]
    spans = column_spans(ffe)
    cap = pk_hbm.shape[1]
    experts = wr.shape[1]
    depth = x_ref.shape[2]
    g = lax.axis_index("grp")
    e = lax.axis_index("exp")
    y = e // 2
    c = e % 2
    half = g % 2
    partner = g + 1 - 2 * half
    sibling = e + 1 - 2 * c
    own_rows = pl.ds(pl.multiple_of(c * HDIM, HDIM), HDIM)

    waits = {}

    def done(kind, index):
        waits.pop((kind, index))()

    def finish():
        for key in list(waits):
            done(*key)

    def local(src, dst, index):
        copy = pltpu.make_async_copy(src, dst, local_sem.at[index])
        copy.start()
        waits["load", index] = copy.wait

    def remote(src, dst, index, **where):
        return pltpu.make_async_remote_copy(
            src_ref=src,
            dst_ref=dst,
            send_sem=send_sem.at[index],
            recv_sem=recv_sem.at[index],
            device_id=where,
            device_id_type=pl.DeviceIdType.MESH,
        )

    def send(src, dst, index, **where):
        copy = remote(src, dst, index, **where)
        copy.start()
        waits["recv", index] = copy.wait_recv
        waits["send", index] = copy.wait_send

    def track(count, landing, index):
        whole = landing.at[pl.ds(0, count)]
        waits["recv", index] = pltpu.make_async_copy(whole, whole, recv_sem.at[index]).wait
        waits["send", index] = pltpu.make_async_copy(whole, whole, send_sem.at[index]).wait

    def send_each(order, one, landing, index):
        for k in order:
            one(k).start()
        track(len(order), landing, index)

    deep = 8
    wide_groups = groups // deep
    group_order = [(i, j) for i in range(wide_groups) for j in range(deep) if i or j]
    group_order.sort(key=lambda k: -min(k[0], wide_groups - k[0]) - min(k[1], deep - k[1]))
    chip_order = sorted(range(1, chips), key=lambda k: -min(k, chips - k))

    def other_group(k):
        return lax.rem(g // deep + k[0], wide_groups) * deep + lax.rem(g % deep + k[1], deep)

    def other_chip(k):
        return lax.rem(y + k, chips)

    def to_chip(src, dst, index, offset):
        send(src, dst, index, exp=2 * other_chip(offset + chips) + c)

    local(x_hbm.at[0], x_ref, 6)
    local(par_hbm, par_ref, 7)
    local(routes_hbm.at[0], routes_ref, 8)
    local(parts_hbm, parts_ref, 9)
    for i in range(3):
        local(wqkv_hbm.at[i], wqkv.at[:, pl.ds(HDIM * i, HDIM)], (0, 14, 15)[i])
    local(tk_hbm.at[0], tk_ref, 10)
    local(tv_hbm.at[0], tv_ref, 11)
    local(gain_hbm, gain.at[c], 12)
    local(wr_hbm, wr.at[c], 13)
    local(pk_hbm.at[0], kall.at[pl.ds(0, cap)], 1)
    local(pv_hbm.at[0], vall.at[pl.ds(0, cap)], 2)
    local(wout_hbm, wout.at[pl.ds(0, HDIM)], 3)
    local(wgu_hbm.at[c], wgu.at[own_rows], 4)
    local(wd_hbm.at[c], wd.at[own_rows], 5)

    barrier = pltpu.get_barrier_semaphore()

    def greet(semaphore, **where):
        pl.semaphore_signal(
            semaphore, inc=1, device_id=where, device_id_type=pl.DeviceIdType.MESH
        )

    def along_y(semaphore):
        for k in (1, chips - 1):
            greet(semaphore, exp=2 * other_chip(k) + c)

    def along_z(semaphore):
        for k in (1, deep - 1):
            greet(semaphore, grp=other_group((0, k)))

    def along_x(semaphore):
        for k in (1, wide_groups - 1):
            greet(semaphore, grp=other_group((k, 0)))

    along_x(barrier)
    along_y(barrier)
    along_z(barrier)
    greet(barrier, exp=sibling)
    greet(barrier, grp=partner, exp=sibling)

    def pass_word(index):
        along_y(rounds.at[index])
        along_z(rounds.at[3 + index])

    def hear_word(index):
        pl.semaphore_wait(rounds.at[index], 2)
        pl.semaphore_wait(rounds.at[3 + index], 2)

    done("load", 6)
    done("load", 8)
    done("load", 7)
    for s in range(STEPS):
        xs[HALF * s : HALF * (s + 1), :] = x_ref[s].astype(F32)
        rts[HALF * s : HALF * (s + 1), :topk] = routes_ref[s]
    x16 = xs[...].astype(BF16)
    row_sub = iota((ROWS, HDIM), 0)
    row_lane = iota((ROWS, HDIM), 1)
    parent_hot = jnp.zeros((ROWS, HDIM), F32)
    for s in range(STEPS):
        for b in range(HALF):
            parent_hot = jnp.where(
                (row_sub == HALF * s + b) & (row_lane == par_ref[0, s, b]), 1.0, parent_hot
            )
    hot[0] = parent_hot.astype(BF16)
    pl.semaphore_wait(barrier, 8)
    pass_word(0)
    send(hot.at[0], hot.at[1], 10, grp=partner)
    done("load", 0)
    done("load", 14)
    done("load", 15)
    qkv[0, :, 0 : 3 * HDIM] = dot(x16, wqkv[...]).astype(BF16)

    send(qkv.at[0], qkv.at[1], 0, grp=partner)
    send(wout_hbm, wout.at[pl.ds(HDIM, HDIM)], 6, exp=sibling)
    send(gain_hbm, gain.at[c], 1, exp=sibling)
    send(wr_hbm, wr.at[c], 2, exp=sibling)
    send(wgu_hbm.at[1 - c], wgu.at[own_rows], 3, exp=sibling)
    send(wd_hbm.at[1 - c], wd.at[own_rows], 4, exp=sibling)

    tail_at = cap
    new_at = cap + HALF * PREV
    total = new_at + 2 * ROWS
    done("load", 10)
    done("load", 11)
    kall[tail_at:new_at, :] = tk_ref[...].astype(F32).reshape(HALF * PREV, HDIM).astype(BF16)
    vall[tail_at:new_at, :] = tv_ref[...].astype(F32).reshape(HALF * PREV, HDIM).astype(BF16)

    done("load", 1)
    done("load", 2)
    hear_word(0)
    pass_word(1)
    done("recv", 10)
    parents = jnp.concatenate([hot[0], hot[1]], axis=0)
    tokens = 2 * ROWS
    beam_row = iota((HDIM, tokens), 0)
    token_lane = iota((HDIM, tokens), 1)
    beam_of = HALF * ((token_lane // ROWS + half) % 2) + token_lane % HALF
    before = dot(parents, one_hot(beam_row == beam_of))
    step_row = (iota((tokens, tokens), 0) % ROWS) // HALF
    step_lane = (iota((tokens, tokens), 1) % ROWS) // HALF
    same = jnp.where(iota((tokens, tokens), 0) == iota((tokens, tokens), 1), 1.0, 0.0)
    back = jnp.where(step_lane + 1 == step_row, before, 0.0)
    back_bf = back.astype(BF16)
    near = (same + back).astype(BF16)
    back_two = dot(back_bf, back_bf)
    path = dot(near, (same + back_two).astype(BF16)).astype(BF16)
    first_row = iota((tokens, HDIM), 0) % ROWS
    first = jnp.where(first_row < HALF, parents.astype(F32), 0.0).astype(BF16)
    origin = dot(path, first).astype(BF16)
    tails = HALF * PREV
    tail_row = iota((HDIM, tails), 0)
    tail_lane = iota((HDIM, tails), 1)
    tail_on = dot(origin, one_hot(tail_row == HALF * half + tail_lane % HALF))
    new_on = jnp.where(iota((tokens, tokens), 0) < ROWS, path.astype(F32), 0.0)

    done("recv", 0)
    for h in range(2):
        at = new_at + ROWS * h
        kall[at : at + ROWS, :] = qkv[h, :, HDIM : 2 * HDIM]
        vall[at : at + ROWS, :] = qkv[h, :, 2 * HDIM : 3 * HDIM]
    query = jnp.concatenate([qkv[0, :, 0:HDIM], qkv[1, :, 0:HDIM]], axis=0)
    done("load", 9)
    score_scale = HDIM ** (-0.5)
    scores = dot_t(query, kall[...]) * score_scale
    prompt_live = iota((tokens, cap), 1) < parts_ref[0]
    prompt_s = jnp.where(prompt_live, scores[:, 0:cap], NEGATIVE)
    tail_s = jnp.where(tail_on > 0.5, scores[:, tail_at:new_at], NEGATIVE)
    new_s = jnp.where(new_on > 0.5, scores[:, new_at:total], NEGATIVE)
    top = jnp.maximum(
        jnp.maximum(
            jnp.max(prompt_s, axis=1, keepdims=True), jnp.max(tail_s, axis=1, keepdims=True)
        ),
        jnp.max(new_s, axis=1, keepdims=True),
    )
    prompt_w = jnp.exp(prompt_s - top)
    tail_w = jnp.exp(tail_s - top)
    new_w = jnp.exp(new_s - top)
    weight_sum = (
        jnp.sum(prompt_w, axis=1, keepdims=True)
        + jnp.sum(tail_w, axis=1, keepdims=True)
        + jnp.sum(new_w, axis=1, keepdims=True)
    )

    def weighted(weights, values):
        high, low = split_high(weights)
        both = dot(jnp.concatenate([high, low], axis=0), values)
        return both[0:tokens] + both[tokens : 2 * tokens]

    mix = (
        weighted(prompt_w, vall[0:cap, :])
        + weighted(tail_w, vall[tail_at:new_at, :])
        + weighted(new_w, vall[new_at:total, :])
    )
    lane = iota((ROWS, HDIM), 1)
    for h in (1, 0):
        rows = slice(ROWS * h, ROWS * (h + 1))
        part_send[h, :, 0:HDIM] = mix[rows]
        part_send[h, :, HDIM : 2 * HDIM] = jnp.where(
            lane < HDIM // 2, top[rows], weight_sum[rows]
        )
        if h == 1:
            send(part_send.at[1], part_recv.at[2], 5, grp=partner, exp=sibling)
            send(part_send.at[1], part_recv.at[0], 14, grp=partner)
    send(part_send.at[0], part_recv.at[1], 15, exp=sibling)
    hear_word(1)
    pass_word(2)

    width = groups * SEND
    routes = rts[...]
    hit = jnp.zeros((ROWS, experts), jnp.bool_)
    expert_lane = iota((ROWS, experts), 1)
    for k in range(topk):
        hit = hit | (routes[:, k : k + 1] == expert_lane)
    hits = one_hot(hit)
    rank = dot(one_hot(iota((ROWS, ROWS), 1) < iota((ROWS, ROWS), 0)), hits)
    spread_row = iota((experts, 2 * width), 0)
    spread_lane = iota((experts, 2 * width), 1)
    spread = one_hot(
        spread_row == 2 * (spread_lane % width // SEND) + spread_lane // width
    )
    hit_wide = dot(hits, spread)
    rank_wide = dot(rank.astype(BF16), spread)
    slot_lane = (iota((ROWS, 2 * width), 1) % SEND).astype(F32)
    place = jnp.where((rank_wide == slot_lane) & (hit_wide > 0.5), 1.0, 0.0)
    own_place = jnp.where(c == 0, place[:, 0:width], place[:, width : 2 * width])

    def joined(near_mix, near_tail, far_mix, far_tail):
        near_top, near_sum = near_tail[:, 0:1], near_tail[:, HDIM // 2 : HDIM // 2 + 1]
        far_top, far_sum = far_tail[:, 0:1], far_tail[:, HDIM // 2 : HDIM // 2 + 1]
        best = jnp.maximum(near_top, far_top)
        near_factor = jnp.exp(near_top - best)
        far_factor = jnp.exp(far_top - best)
        return (
            (near_mix * near_factor + far_mix * far_factor)
            / (near_sum * near_factor + far_sum * far_factor)
        ).astype(BF16)

    def halves(ref, index):
        return ref[index, :, 0:HDIM], ref[index, :, HDIM : 2 * HDIM]

    done("recv", 15)
    done("recv", 14)
    own_head = joined(*halves(part_send, 0), *halves(part_recv, 0))
    done("recv", 5)
    other_head = joined(*halves(part_recv, 1), *halves(part_recv, 2))
    attention = jnp.concatenate([own_head, other_head], axis=1)
    done("load", 3)
    done("recv", 6)
    hear_word(2)
    along_x(rounds.at[6])

    chip = 2 * HDIM

    def features(at):
        return pl.ds(pl.multiple_of(at * chip, chip), chip)

    for k in chip_order:
        at = other_chip(k)
        proj_send[pl.ds(at, 1)] = (
            dot(attention, wout[:, features(at)]).astype(BF16).reshape(1, ROWS, chip)
        )
        remote(proj_send.at[at], proj_recv.at[y], 16, exp=2 * at + c).start()
    track(chips - 1, proj_recv, 16)
    pl.semaphore_wait(rounds.at[6], 2)
    along_x(rounds.at[7])
    residual = xs[:, features(y)] + dot(attention, wout[:, features(y)])
    proj_recv[pl.ds(y, 1)] = jnp.zeros((1, ROWS, chip), BF16)
    done("recv", 16)
    pl.semaphore_wait(rounds.at[7], 2)
    residual = residual + jnp.sum(proj_recv[...].astype(F32), axis=0)

    rows_bf = residual.astype(BF16)
    outgoing = lax.dot_general(
        own_place.astype(BF16), rows_bf, (((0,), (0,)), ((), ())), preferred_element_type=F32
    )
    disp_send[...] = outgoing.reshape(groups, SEND, chip).astype(BF16)

    send_each(
        group_order,
        lambda k: remote(
            disp_send.at[other_group(k)], disp_recv.at[g], 7, grp=other_group(k)
        ),
        disp_recv,
        7,
    )
    disp_recv[pl.ds(g, 1)] = disp_send[pl.ds(g, 1)]
    greet(rounds.at[8], exp=sibling)

    done("load", 12)
    done("load", 13)
    done("recv", 1)
    done("recv", 2)
    gains = jnp.concatenate([gain[0], gain[1]], axis=1)
    scaled = (residual * gains).astype(BF16)
    logit_part = dot_t(scaled[:, 0:HDIM], wr[0]) + dot_t(scaled[:, HDIM:chip], wr[1])
    stat_send[:, 0:experts] = logit_part
    stat_send[:, experts:HDIM] = jnp.broadcast_to(
        jnp.sum(residual * residual, axis=1, keepdims=True), (ROWS, HDIM - experts)
    )

    send_each(
        chip_order,
        lambda k: remote(stat_send, stat_recv.at[y], 8, exp=2 * other_chip(k) + c),
        stat_recv,
        8,
    )
    stat_recv[pl.ds(y, 1)] = stat_send[...].reshape(1, ROWS, stat_send.shape[1])

    packed = chips * PADB
    pick_row = iota((packed, groups * SEND), 0)
    pick_lane = iota((packed, groups * SEND), 1)
    per = BLOCK // CAP_E
    own_dest = pick_row // PADB

    def picks(shift):
        index = pick_row % PADB - shift
        safe = jnp.maximum(index, 0)
        source = (own_dest * per + safe // CAP_E) * SEND + safe % CAP_E
        return one_hot((index >= 0) & (index < BLOCK) & (pick_lane == source))

    gate_pick = picks(0)
    up_pick = picks(PADB - BLOCK)
    done("recv", 7)
    arrived = disp_recv[...].astype(F32).reshape(groups * SEND, chip).astype(BF16)
    gate_rows = dot(gate_pick, arrived)
    up_rows = dot(up_pick, arrived)
    gate_in = (gate_rows * gains).astype(BF16)
    up_in = (up_rows * gains).astype(BF16)
    done("load", 4)
    done("recv", 3)
    def rows_of(offset):
        return other_chip(offset + chips)

    chunks = len(spans)
    for h in range(chunks):
        first, size = spans[h]
        gate = dot(gate_in, wgu[:, first : first + size]).reshape(chips, 2, 8, size)
        up = dot(up_in, wgu[:, ffe + first : ffe + first + size]).reshape(chips, 2, 8, size)
        gu_send[h][:, 0:8] = gate[:, 0].astype(BF16)
        gu_send[h][:, 8:16] = (gate[:, 1] + up[:, 0]).astype(BF16)
        gu_send[h][:, 16:24] = up[:, 1].astype(BF16)
        base = 17 + 14 * h
        to_chip(gu_send[h].at[rows_of(4)], gu_mid[h].at[2], base + 2, 2 - 4 * (h % 2))
        to_chip(gu_send[h].at[rows_of(3)], gu_mid[h].at[0], base, 1)
        to_chip(gu_send[h].at[rows_of(-3)], gu_mid[h].at[1], base + 1, -1)
    squares = dot_t(
        jnp.ones((8, chip), F32), gate_rows * gate_rows, precision=lax.Precision.HIGHEST
    )
    sq_send[...] = squares

    send_each(
        chip_order,
        lambda k: remote(sq_send, sq_recv.at[y], 9, exp=2 * other_chip(k) + c),
        sq_recv,
        9,
    )
    sq_recv[pl.ds(y, 1)] = squares.reshape(1, 8, packed)

    for h in range(chunks):
        base = 17 + 14 * h
        for i in range(3):
            done("recv", base + i)
        for i in range(2):
            direction = 1 - 2 * i
            passing = gu_send[h][pl.ds(rows_of(2 * direction), 1)][0].astype(F32)
            passing = passing + gu_mid[h][i].astype(F32)
            if i == h % 2:
                passing = passing + gu_mid[h][2].astype(F32)
            gu_pass[h][i] = passing.astype(BF16)
            to_chip(gu_pass[h].at[i], gu_recv[h].at[2 + i], base + 5 + i, 2 * direction)
        to_chip(gu_send[h].at[rows_of(1)], gu_recv[h].at[0], base + 3, 1)
        to_chip(gu_send[h].at[rows_of(-1)], gu_recv[h].at[1], base + 4, -1)

    done("recv", 8)
    stats = jnp.sum(stat_recv[...], axis=0)
    mean_square = stats[:, experts : experts + 1] / depth
    logits = stats[:, 0:experts] * lax.rsqrt(mean_square + EPSILON)
    picked_top = jnp.max(jnp.where(hit, logits, NEGATIVE), axis=1, keepdims=True)
    picked = jnp.where(hit, jnp.exp(jnp.minimum(logits - picked_top, 0.0)), 0.0)
    share = picked / jnp.sum(picked, axis=1, keepdims=True)
    share_high, share_low = split_high(share)
    shares = jnp.concatenate([share_high, share_low], axis=0)
    share_wide = dot(shares, spread)
    combine = jnp.concatenate(
        [
            (share_wide[0:ROWS] * place).astype(BF16),
            (share_wide[ROWS : 2 * ROWS] * place).astype(BF16),
        ],
        axis=0,
    )
    done("recv", 9)
    square_sums = jnp.sum(sq_recv[...], axis=0)[0:1, :]
    scale_row = iota((2 * BLOCK, packed), 0) % BLOCK
    scale_lane = iota((2 * BLOCK, packed), 1)
    own_square = jnp.sum(
        jnp.where(scale_lane == y * PADB + scale_row, square_sums, 0.0), axis=1, keepdims=True
    )
    scale = lax.rsqrt(own_square / depth + EPSILON)

    back_row = iota((groups * SEND, chips * BLOCK), 0)
    back_lane = iota((groups * SEND, chips * BLOCK), 1)
    back_rank = back_row % SEND
    back_source = (back_row // SEND) * CAP_E + back_rank
    back_pick = one_hot((back_rank < CAP_E) & (back_lane == back_source))

    for h in range(chunks):
        first, size = spans[h]
        base = 17 + 14 * h
        for i in range(3, 7):
            done("recv", base + i)
        sums = gu_send[h][pl.ds(y, 1)][0].astype(F32)
        for i in range(4):
            sums = sums + gu_recv[h][i].astype(F32)
        gsum[:, 0:size] = sums * scale
        gates = gsum[0:BLOCK, 0:size]
        ups = gsum[BLOCK : 2 * BLOCK, 0:size]
        hidden = gates / (1.0 + jnp.exp(-gates)) * ups
        hid[h][pl.ds(y, 1)] = hidden.reshape(1, BLOCK // HALF, HALF, size).astype(BF16)
        for i, offset in enumerate((4, 3, -3, 2, -2, 1, -1)):
            to_chip(hid[h].at[y], hid[h].at[y], base + 7 + i, offset)
    done("load", 5)
    done("recv", 4)
    result = jnp.zeros((chips * BLOCK, chip), F32)
    for h in range(chunks):
        first, size = spans[h]
        for i in range(7, 14):
            done("recv", 17 + 14 * h + i)
        rows = hid[h][...].astype(F32).reshape(chips * BLOCK, size).astype(BF16)
        result = result + dot_t(rows, wd[:, first : first + size])
    result = result.astype(BF16)
    landing = c * groups + g
    pl.semaphore_wait(rounds.at[8], 1)
    for h in range(2):
        outcome = dot(back_pick, result[:, HDIM * h : HDIM * (h + 1)])
        ret_send[h] = outcome.reshape(groups, SEND, HDIM).astype(BF16)
        for k in group_order:
            at = other_group(k)
            remote(ret_send.at[h, at], ret_recv.at[landing], 12, grp=at, exp=2 * y + h).start()
    remote(ret_send.at[1 - c, g], ret_recv.at[landing], 12, exp=sibling).start()
    track(2 * groups - 1, ret_recv, 12)
    ret_recv[pl.ds(landing, 1)] = ret_send[c, pl.ds(g, 1)]
    own = jnp.where(c == 0, residual[:, 0:HDIM], residual[:, HDIM:chip])
    done("recv", 12)
    returned = ret_recv[...].astype(F32).reshape(2 * groups * SEND, HDIM).astype(BF16)
    both = dot(combine, returned)
    out_ref[0] = (
        (own + both[0:ROWS] + both[ROWS : 2 * ROWS]).reshape(STEPS, HALF, HDIM).astype(BF16)
    )

    finish()


def in_hbm(value):
    return pltpu.with_memory_space_constraint(value, pltpu.HBM)


def on_device(
    step_inputs,
    parents,
    routes,
    w_qkv,
    w_out,
    prompt_keys,
    prompt_values,
    prompt_parts,
    tail_keys,
    tail_values,
    w_router,
    norm_gain,
    w_gate_up,
    w_down,
):
    groups = lax.axis_size("grp")
    columns = lax.axis_size("exp")
    chips = columns // 2
    depth = step_inputs.shape[3]
    cap = prompt_keys.shape[1]
    ffe = w_down.shape[2]
    experts = w_router.shape[1]
    topk = routes.shape[3]
    chip = 2 * HDIM
    spans = column_spans(ffe)
    keys = cap + HALF * PREV + 2 * ROWS
    vmem = pl.BlockSpec(memory_space=pltpu.VMEM)
    out = pl.pallas_call(
        functools.partial(kernel, groups, columns, topk),
        out_shape=jax.ShapeDtypeStruct((1, STEPS, HALF, HDIM), BF16),
        in_specs=[
            pl.BlockSpec(memory_space=pltpu.HBM)
        ]
        * 14,
        out_specs=vmem,
        scratch_shapes=[
            pltpu.VMEM((STEPS, HALF, depth), BF16),
            pltpu.SMEM((1, STEPS, HALF), jnp.int32),
            pltpu.VMEM((STEPS, HALF, topk), jnp.int32),
            pltpu.SMEM((1,), jnp.int32),
            pltpu.VMEM((PREV, HALF, HDIM), BF16),
            pltpu.VMEM((PREV, HALF, HDIM), BF16),
            pltpu.VMEM((ROWS, depth), F32),
            pltpu.VMEM((ROWS, HDIM), jnp.int32),
            pltpu.VMEM((2, 1, HDIM), F32),
            pltpu.VMEM((2, experts, HDIM), BF16),
            pltpu.VMEM((depth, 3 * HDIM), BF16),
            pltpu.VMEM((chip, depth), BF16),
            pltpu.VMEM((keys, HDIM), BF16),
            pltpu.VMEM((keys, HDIM), BF16),
            pltpu.VMEM((chip, 2 * ffe), BF16),
            pltpu.VMEM((chip, ffe), BF16),
            pltpu.VMEM((2, ROWS, 3 * HDIM), BF16),
            pltpu.VMEM((2, ROWS, HDIM), BF16),
            pltpu.VMEM((2, ROWS, chip), F32),
            pltpu.VMEM((3, ROWS, chip), F32),
            pltpu.VMEM((chips, ROWS, chip), BF16),
            pltpu.VMEM((chips, ROWS, chip), BF16),
            pltpu.VMEM((ROWS, HDIM), F32),
            pltpu.VMEM((chips, ROWS, HDIM), F32),
            pltpu.VMEM((groups, SEND, chip), BF16),
            pltpu.VMEM((groups, SEND, chip), BF16),
            pltpu.VMEM((8, chips * PADB), F32),
            pltpu.VMEM((chips, 8, chips * PADB), F32),
            [pltpu.VMEM((chips, 2 * BLOCK, size), BF16) for _, size in spans],
            [pltpu.VMEM((3, 2 * BLOCK, size), BF16) for _, size in spans],
            [pltpu.VMEM((2, 2 * BLOCK, size), BF16) for _, size in spans],
            [pltpu.VMEM((4, 2 * BLOCK, size), BF16) for _, size in spans],
            pltpu.VMEM((2 * BLOCK, max(size for _, size in spans)), F32),
            [pltpu.VMEM((chips, BLOCK // HALF, HALF, size), BF16) for _, size in spans],
            pltpu.VMEM((2, groups, SEND, HDIM), BF16),
            pltpu.VMEM((2 * groups, SEND, HDIM), BF16),
            pltpu.SemaphoreType.DMA((16,)),
            pltpu.SemaphoreType.DMA((17 + 14 * len(spans),)),
            pltpu.SemaphoreType.DMA((17 + 14 * len(spans),)),
            pltpu.SemaphoreType.REGULAR((9,)),
        ],
        compiler_params=pltpu.CompilerParams(
            collective_id=0, has_side_effects=True, vmem_limit_bytes=48 * 1024 * 1024
        ),
        name="layer",
    )(
        in_hbm(step_inputs),
        in_hbm(parents),
        in_hbm(routes),
        prompt_parts,
        in_hbm(norm_gain.reshape(1, HDIM)),
        in_hbm(w_router.T),
        in_hbm(jnp.transpose(w_qkv, (1, 0, 2))),
        in_hbm(w_out),
        in_hbm(prompt_keys),
        in_hbm(prompt_values),
        in_hbm(jnp.transpose(tail_keys, (0, 2, 1, 3))),
        in_hbm(jnp.transpose(tail_values, (0, 2, 1, 3))),
        in_hbm(w_gate_up),
        in_hbm(w_down),
    )
    return out


def solution(mesh):
    placed = (
        P("grp", None, None, None),
        P("grp", None, None),
        P("grp", None, None, None),
        P(None, None, "exp"),
        P("exp", None),
        P("grp", None, "exp"),
        P("grp", None, "exp"),
        P("grp"),
        P("grp", None, None, "exp"),
        P("grp", None, None, "exp"),
        P("exp", None),
        P("exp"),
        P("grp", "exp", None),
        P("grp", "exp", None),
    )
    return jax.shard_map(
        on_device,
        mesh=mesh,
        in_specs=placed,
        out_specs=P("grp", None, None, "exp"),
        check_vma=False,
    )
```
